256 devices in a mesh: grp: 2 (over z_hi), dev: 128 (over y, z_lo, x, core).
Axes of the slice: x: 4, y: 4, z: 8 (z_hi: 2, z_lo: 4; z = z_hi * 4 + z_lo), core: 2. Of those that a mesh axis runs over, the one named last changes fastest.
Arguments:
- state: float32 [2, 3, 16777216], P('grp', None, 'dev'), may hold values from -6 to 6
- courant: float32 [16777216], P('dev'), may hold values from 0.25 to 1
- remesh: float32 [128, 128], replicated, may hold values from -0.5 to 0.5
- shell_dest: int32 [32768, 1], P('dev'), may hold values from 0 to 127; in each aligned block of 256 rows (0 to 255, 256 to 511, ...) at most 4 rows name the same one
- shell_row: int32 [32768], P('dev'), may hold values from 0 to 1023
- return_dest: int32 [32768, 1], P('dev'), may hold values from 0 to 127; in each aligned block of 256 rows (0 to 255, 256 to 511, ...) at most 4 rows name the same one
- return_row: int32 [32768], P('dev'), may hold values from 0 to 1023
- return_block: int32 [32768], P('dev'), may hold values from 0 to 15
Outputs:
- fields: float32 [2, 3, 16777216], P('grp', None, 'dev')
The draws below stay inside these ranges and needn't reach their ends.
Inputs may be any that keep to these rules, and one draw needn't show every extreme that they name: `shell_dest`: among the rows of one device (256 aligned rows) no brick is named more than 4 times, a bound that some block reaches. `return_dest`: among the rows of one brick (256 aligned rows) no owner is named more than 4 times, a bound that some block reaches.
All inputs are finite; a program needn't handle non-finite values.
Results may differ from the reference program's by a relative error of at most 0.00027.
Values sent between devices are 32-bit elements; how exact they have to be, the bound alone decides.
No kernel may reach another device: no remote copies, remote signals or barrier semaphores. Data moves between devices by JAX's collectives and lax.ppermute only.
A program may use at most 64 MiB of HBM per device.

```python
import math
import jax
import jax.numpy as jnp
import numpy as np
from jax import lax

NX = 512
NY = 256
NZ = 128
NI = 64
NK = 128
BRICKS = 128
CELLS = 16777216
NJ_DEV = 16
NJ = 2048
SHELL = 16
SB = 256
CAP = 4
RPB = 1024


def with_ends(drawn, stream_key, smallest, largest):
    extent = drawn.shape
    place = [jax.random.randint(jax.random.fold_in(stream_key, axis), (), 0, extent[axis]) for axis in range(len(extent))]
    drawn = drawn.at[tuple(place)].set(smallest)
    longest = extent.index(max(extent))
    place[longest] = (place[longest] + 1) % extent[longest]
    return drawn.at[tuple(place)].set(largest)


def steps_of(rng, shape, pieces, least, largest):
    loudness = 1.0
    for axis_at, shards_of in pieces:
        heights = jax.random.uniform(jax.random.fold_in(jax.random.fold_in(rng, 6), axis_at), (shards_of,), jnp.float32, least / len(pieces), largest / len(pieces))
        loudness = loudness * jnp.repeat(jnp.exp(heights), shape[axis_at] // shards_of).reshape((-1,) + (1,) * (len(shape) - 1 - axis_at))
    return loudness


def assign_block(stream_key, own, number, rows, number_of, top, most, lean):
    order = jax.random.permutation(stream_key, number_of)
    packed, ordinary = shares(number_of, rows * top, most, lean, True), shares(number_of, rows * top, most, lean, False)
    places = jnp.arange(number_of)

    def named(sizes, turn):
        used = int((sizes > 0).sum())
        fixed = max(1, used // 4)
        moved = fixed + (places - fixed + turn * (used - fixed)) % max(1, number_of - fixed)
        return jnp.zeros((number_of,), jnp.int32).at[order[jnp.where(places < fixed, places, moved)]].set(jnp.asarray(sizes, jnp.int32))

    sizes = jnp.where(number % 4 == 0, named(packed, number // 4), named(ordinary, number - number // 4 - 1))
    mixed = jax.random.permutation(jax.random.fold_in(own, 3), number_of)
    donor, taker = mixed[0:number_of // 2 * 2:2], mixed[1:number_of // 2 * 2:2]
    margin = jnp.minimum(sizes[donor] - 1, most - sizes[taker]) // 2
    margin = jnp.where((donor == order[0]) | (taker == order[0]) | (sizes[taker] == 0), 0, jnp.maximum(margin, 0))
    moved = jax.random.randint(jax.random.fold_in(own, 4), (number_of // 2,), 0, 1 << 20) % (margin + 1)
    sizes = sizes.at[donor].add(-moved).at[taker].add(moved)
    items = jnp.searchsorted(jnp.cumsum(sizes), jnp.arange(rows * top), side="right").astype(jnp.int32)
    listing = items.reshape(top, rows).T
    listing = listing[jax.random.permutation(jax.random.fold_in(own, 1), rows)]
    turn = jax.random.randint(jax.random.fold_in(own, 2), (rows, 1), 0, top)
    return jnp.take_along_axis(listing, (jnp.arange(top)[None, :] + turn) % top, axis=1)


def shares(amount, total, most, skew, full):
    portions = [(1 << 20) // math.isqrt(rank ** skew) + 1 for rank in range(1, amount + 1)]
    largest = most if full else min(most, max(-(-total // amount), total * portions[0] // sum(portions)))
    least = 1 if total - largest >= amount - 1 else 0
    given, rest = [largest] + [least] * (amount - 1), total - largest - least * (amount - 1)
    while rest > 0:
        movable = [i for i in range(1, amount) if given[i] < largest] or [i for i in range(1, amount) if given[i] < most]
        mass, remaining = sum([portions[i] for i in movable]), rest
        for i in movable:
            more = min(most - given[i], max(1, remaining * portions[i] // mass), rest)
            given[i] = given[i] + more
            rest = rest - more
    return np.array(given)


def scatter_about(stream_key, shape, width, most, shards=(), kind=jnp.bfloat16):
    values = width * jax.random.normal(stream_key, shape, jnp.float32)
    if shards:
        values = values * steps_of(stream_key, shape, shards, -0.22, 0.18)
    return jnp.clip(values, -most, most).astype(kind)


def setup_inputs(seed: int = 0) -> dict:
    arg_keys = jax.random.split(jax.random.key(seed), 9)
    state = scatter_about(arg_keys[0], (2, 3, CELLS), 1.0, 6.0, ((0, 2), (2, 128)), jnp.float32)
    courant = jnp.clip(jnp.exp(math.log(1.0) - 1.3862944 * jax.random.uniform(arg_keys[1], (CELLS,), jnp.float32) ** steps_of(arg_keys[1], (CELLS,), ((0, 128),), -0.2, 0.2)), 0.25, 1.0)
    remesh = scatter_about(arg_keys[2], (NK, NZ), NK ** -0.5, 0.5, (), jnp.float32)
    shell_dest_keys = jax.random.split(jax.random.fold_in(arg_keys[3], 1), (BRICKS * SB) // SB)
    shell_dest_turns = jax.random.permutation(jax.random.fold_in(arg_keys[3], 3), (BRICKS * SB) // SB)
    shell_dest = jax.vmap(lambda own, number: assign_block(jax.random.fold_in(arg_keys[3], 2), own, number, SB, BRICKS, 1, CAP, 2))(shell_dest_keys, shell_dest_turns).reshape((BRICKS * SB, 1))
    shell_row = with_ends(jax.random.randint(arg_keys[4], (BRICKS * SB,), 0, RPB), jax.random.fold_in(arg_keys[4], 1), 0, RPB - 1).astype(jnp.int32)
    return_dest_keys = jax.random.split(jax.random.fold_in(arg_keys[5], 1), (BRICKS * SB) // SB)
    return_dest_turns = jax.random.permutation(jax.random.fold_in(arg_keys[5], 3), (BRICKS * SB) // SB)
    return_dest = jax.vmap(lambda own, number: assign_block(jax.random.fold_in(arg_keys[5], 2), own, number, SB, BRICKS, 1, CAP, 2))(return_dest_keys, return_dest_turns).reshape((BRICKS * SB, 1))
    return_row = with_ends(jax.random.randint(arg_keys[6], (BRICKS * SB,), 0, RPB), jax.random.fold_in(arg_keys[6], 1), 0, RPB - 1).astype(jnp.int32)
    return_block = with_ends(jax.random.randint(arg_keys[7], (BRICKS * SB,), 0, NJ_DEV), jax.random.fold_in(arg_keys[7], 1), 0, NJ_DEV - 1).astype(jnp.int32)
    return dict(state=state, courant=courant, remesh=remesh, shell_dest=shell_dest, shell_row=shell_row, return_dest=return_dest, return_row=return_row, return_block=return_block)


viscosity = 0.2
coupling = 1.0
highest = lax.Precision.HIGHEST


def sine_table(length):
    counts = jnp.arange(length, dtype=jnp.int32) + 1
    phase = (counts[:, None] * counts[None, :]) % (2 * (length + 1))
    return jnp.sin(jnp.pi * phase.astype(jnp.float32) / (length + 1))


def laplace_eigen(length):
    counts = jnp.arange(length, dtype=jnp.float32) + 1.0
    return 2.0 - 2.0 * jnp.cos(jnp.pi * counts / (length + 1))


def advance(field, courant_part):
    transport = (8.0 * (field[:, 3:-1] - field[:, 1:-3]) - (field[:, 4:] - field[:, :-4])) / 12.0
    centre_part = field[:, 2:-2]
    padded = jnp.pad(centre_part, ((0, 0), (0, 0), (1, 1), (0, 0)))
    diffusion = padded[:, :, 2:] - 2.0 * centre_part + padded[:, :, :-2]
    return centre_part - courant_part * transport + viscosity * diffusion


def difference(field, axis):
    widths = [(0, 0)] * field.ndim
    widths[axis] = (1, 1)
    padded = jnp.pad(field, widths)
    upper = lax.slice_in_dim(padded, 2, padded.shape[axis], axis=axis)
    lower = lax.slice_in_dim(padded, 0, padded.shape[axis] - 2, axis=axis)
    return (upper - lower) / 2.0


def cross_product(first, second):
    return jnp.stack([first[1] * second[2] - first[2] * second[1],
                      first[2] * second[0] - first[0] * second[2],
                      first[0] * second[1] - first[1] * second[0]])


def reference(state, courant, remesh, shell_dest, shell_row, return_dest, return_row, return_block):
    near_field = state[0].reshape(3, NJ, NI, NK)
    courant_field = courant.reshape(NJ, NI, NK)
    updated = near_field
    for substep in range(2):
        extended = jnp.concatenate([updated[:, -2:], updated, updated[:, :2]], axis=1)
        updated = advance(extended, courant_field)
    blocks = near_field[:, :, NI - SHELL:, :].reshape(3, NJ * SHELL, NK)
    remeshed = jnp.einsum('cqk,kz->cqz', blocks, remesh, precision=highest)
    lattice_rows = shell_dest[:, 0] * RPB + shell_row
    deposit = jnp.zeros((3, NX * NY, NZ), jnp.float32).at[:, lattice_rows, :].add(remeshed)
    wake_field = state[1].reshape(3, NX, NY, NZ) + deposit.reshape(3, NX, NY, NZ)
    spectral = jnp.einsum('cxyz,zb->cxyb', wake_field, sine_table(NZ), precision=highest)
    spectral = jnp.einsum('cxyb,ya->cxab', spectral, sine_table(NY), precision=highest)
    spectral = jnp.einsum('cxab,xe->ceab', spectral, sine_table(NX), precision=highest)
    eigen_sum = (laplace_eigen(NX)[:, None, None] + laplace_eigen(NY)[None, :, None]) + laplace_eigen(NZ)[None, None, :]
    scale = 8.0 / ((NX + 1) * (NY + 1) * (NZ + 1))
    spectral = spectral * (scale / eigen_sum)
    potential = jnp.einsum('ceab,ex->cxab', spectral, sine_table(NX), precision=highest)
    potential = jnp.einsum('cxab,ay->cxyb', potential, sine_table(NY), precision=highest)
    potential = jnp.einsum('cxyb,bz->cxyz', potential, sine_table(NZ), precision=highest)
    velocity = jnp.stack([difference(potential[2], 1) - difference(potential[1], 2),
                          difference(potential[0], 2) - difference(potential[2], 0),
                          difference(potential[1], 0) - difference(potential[0], 1)])
    flat_rows = velocity.reshape(3, NX * NY, NZ)
    brick_of = jnp.arange(BRICKS * SB, dtype=jnp.int32) // SB
    picked = jnp.take(flat_rows, brick_of * RPB + return_row, axis=1)
    interp = jnp.einsum('cqz,kz->cqk', picked, remesh, precision=highest)
    targets = return_dest[:, 0] * NJ_DEV + return_block
    boundary = jnp.zeros((3, NJ, NK), jnp.float32).at[:, targets, :].add(interp)
    updated = updated.at[:, :, NI - 1, :].add(coupling * cross_product(boundary, near_field[:, :, NI - 1, :]))
    return jnp.stack([updated.reshape(3, CELLS), velocity.reshape(3, CELLS)])
```

```python
import jax
import jax.numpy as jnp
import ml_dtypes
import numpy as np
from jax import lax
from jax.experimental import pallas as pl
from jax.experimental.pallas import tpu as pltpu
from jax.sharding import Mesh
from jax.sharding import PartitionSpec as P

NX, NY, NZ = 512, 256, 128
NI, NK = 64, 128
NJ = 16
CY, CZ, CX, CC = 4, 4, 4, 2
BRICKS = 128
CAP = 4
SB = 256
RPB = 1024
TARGETS = CY * CX * CC
GROUP = CZ * CAP
SLOTS = BRICKS * CAP
DEV = ("y", "z", "x", "core")
ALL = ("grp",) + DEV

viscosity = 0.2
coupling = 1.0
f32 = jnp.float32
bf16 = jnp.bfloat16
i32 = jnp.int32
highest = lax.Precision.HIGHEST
NT = (((1,), (1,)), ((), ()))


def sines(length):
    counts = np.arange(length) + 1
    phase = counts[:, None] * counts[None, :] % (2 * (length + 1))
    return np.sin(np.pi * phase / (length + 1))


def eigen(length):
    counts = np.arange(length) + 1.0
    return 4.0 * np.sin(0.5 * np.pi * counts / (length + 1)) ** 2


def halves(table):
    table = table.astype(np.float32)
    high = table.astype(ml_dtypes.bfloat16)
    low = (table - high.astype(np.float32)).astype(ml_dtypes.bfloat16)
    return high, low


def paired(table):
    high, low = halves(table)
    return np.block([[high, low], [high, np.zeros_like(low)]]).astype(ml_dtypes.bfloat16)


def line_table():
    dev = np.arange(BRICKS)
    plane = np.where(dev % 2 == 1, 4 * dev + 3, 4 * dev - 1) + 1
    phase = (np.arange(NX) + 1)[:, None] * plane[None, :] % (2 * (NX + 1))
    return np.sin(np.pi * phase / (NX + 1))


def iota(shape, axis):
    return lax.broadcasted_iota(i32, shape, axis)


def split(value):
    high = value.astype(bf16)
    return high, (value - high.astype(f32)).astype(bf16)


def mm(a, b):
    return jnp.dot(a, b, preferred_element_type=f32)


def lanes_paired(value):
    return jnp.concatenate(split(value), axis=1)


def fold(value):
    half = value.shape[1] // 2
    return value[:, :half] + value[:, half:]


def pick(onehot, value):
    return fold(mm(onehot, lanes_paired(value)))


def times_paired(value, table):
    return fold(mm(lanes_paired(value), table))


def table_times(high, low, value):
    vh, vl = split(value)
    return mm(high, vh) + mm(high, vl) + mm(low, vh)


def exact(a, b, dims=(((1,), (0,)), ((), ()))):
    return lax.dot_general(a, b, dims, precision=highest, preferred_element_type=f32)


def onehot(condition):
    return jnp.where(condition, 1.0, 0.0).astype(bf16)


def ranks(matches):
    size = matches.shape[1]
    before = onehot(iota((size, size), 0) < iota((size, size), 1))
    counts = mm(matches.astype(bf16), before)
    return jnp.sum(matches * counts, axis=0, keepdims=True).astype(i32)


def route_kernel(flags, sd, sr, rd, rr, rb, remesh, sz, place, gather, codes, merged):
    zme = flags[3]
    bricks = iota((BRICKS, SB), 0)
    matches = jnp.where(bricks == sd[...], 1.0, 0.0)
    rank = ranks(matches)
    slot = rank * BRICKS + sd[...]
    place[...] = onehot(iota((SLOTS, SB), 0) == slot)
    tagged = jnp.where(bricks == rank, (sr[...] + 1).astype(f32), 0.0)
    sent = exact(matches, tagged, NT)
    owner = rd[...]
    oc = owner & (CC - 1)
    ox = (owner >> 1) & (CX - 1)
    oz = (owner >> 3) & (CZ - 1)
    oy = owner >> 5
    rank = ranks(jnp.where(bricks == owner, 1.0, 0.0))
    lane = oz * CAP + rank
    slot = ((oy * CX + ox) * CC + oc) * GROUP + lane
    gather[...] = lax.dot_general(
        onehot(iota((SLOTS, SB), 0) == slot),
        onehot(iota((RPB, SB), 0) == rr[...]),
        NT,
        preferred_element_type=f32,
    ).astype(bf16)
    via = ((oy * CZ + zme) * CX + ox) * CC + oc
    code = ((oz - zme) & (CZ - 1)) * NJ + rb[...] + 1
    tagged = jnp.where(bricks == lane + CAP, code.astype(f32), 0.0)
    codes[...] = sent + exact(jnp.where(bricks == via, 1.0, 0.0), tagged, NT)
    both = exact(remesh[...], sz[...])
    high, low = split(both)
    merged[...] = jnp.concatenate(
        [
            jnp.concatenate([high, low], axis=1),
            jnp.concatenate([high, jnp.zeros_like(low)], axis=1),
        ],
        axis=0,
    )


def decode_kernel(flags, codes, spread, cells):
    zme = flags[3]
    turned = codes[...].T
    rows = jnp.concatenate([turned[i : i + 1, :] for i in range(CAP)], axis=1).astype(i32)
    spread[...] = onehot(iota((RPB, SLOTS), 0) == rows - 1)
    target = iota((TARGETS, BRICKS), 0)
    source = ((target >> 3) * CZ + zme) * (CX * CC) + (target & (CX * CC - 1))
    chosen = exact(jnp.where(iota((TARGETS, BRICKS), 1) == source, 1.0, 0.0), codes[...])
    wide = jnp.where(
        iota((BRICKS, SLOTS), 0) == (iota((BRICKS, SLOTS), 1) & (GROUP - 1)) + CAP, 1.0, 0.0
    )
    chosen = exact(chosen, wide)
    own = iota((TARGETS, SLOTS), 0) == (iota((TARGETS, SLOTS), 1) >> 4)
    code = jnp.sum(jnp.where(own, chosen, 0.0), axis=0, keepdims=True).astype(i32)
    cells[...] = onehot(iota((CZ * NJ, SLOTS), 0) == code - 1)


def near_kernel(flags, state, courant, up, down, out, layer):
    @pl.when(flags[0] == 0)
    def _():
        cr = jnp.concatenate([up[768:896, :], courant[...], down[768:896, :]], axis=0)

        def step(field, speed):
            rows = speed.shape[0]
            centre = field[128 : 128 + rows]
            transport = (
                8.0 * (field[192 : 192 + rows] - field[64 : 64 + rows])
                - (field[256 : 256 + rows] - field[:rows])
            ) / 12.0
            place = iota((rows, NK), 0) & (NI - 1)
            above = jnp.where(place == NI - 1, 0.0, pltpu.roll(centre, rows - 1, 0))
            below = jnp.where(place == 0, 0.0, pltpu.roll(centre, 1, 0))
            return centre - speed * transport + viscosity * (above - 2.0 * centre + below)

        for c in range(3):
            field = jnp.concatenate(
                [up[c * 256 : (c + 1) * 256, :], state[c], down[c * 256 : (c + 1) * 256, :]], axis=0
            )
            field = step(field, cr)
            out[c] = step(field, courant[...])
            layer[c] = state[c, pl.ds(NI - 1, NJ, stride=NI), :]


def bucket_kernel(blocks, place, merged, out):
    for c in range(3):
        moved = times_paired(blocks[c], merged[...])
        slots = pick(place[...], moved)
        for rank in range(CAP):
            out[pl.ds(c * CAP + rank, BRICKS, stride=3 * CAP), :] = slots[
                rank * BRICKS : (rank + 1) * BRICKS
            ]


def weights(beta):
    outer = beta * beta - 2.0
    g12 = 1.0 / outer
    g13 = g12 / beta
    g11 = (beta * beta - 1.0) * g13
    return g11, g12, g13


def forward_kernel(flags, received, spread, state, sz, syh, syl, mu, planes, outgoing, kept):
    beta = mu[...] + 2.0
    g11, g12, g13 = weights(beta)
    first = flags[1] == 0
    for c in range(3):
        rows = jnp.concatenate(
            [received[pl.ds(c * CAP + r, BRICKS, stride=3 * CAP), :] for r in range(CAP)], axis=0
        )
        field = pick(spread[...], rows) + times_paired(state[c], sz[...])
        field = jnp.concatenate([field[p * NY : (p + 1) * NY] for p in range(4)], axis=1)
        field = table_times(syh[...], syl[...], field)
        f0, f1, f2, f3 = (field[:, p * NZ : (p + 1) * NZ] for p in range(4))
        for p, plane in enumerate((f0, f1, f2, f3)):
            planes[c, p] = plane
        low = g11 * f0 + g12 * f1 + g13 * f2
        high = f3 + g13 * f0 + g12 * f1 + g11 * f2
        outgoing[c * NY : (c + 1) * NY, :] = jnp.where(first, high, low)
        kept[c * NY : (c + 1) * NY, :] = jnp.where(first, low, high)


def reduce_kernel(outgoing, incoming, kept, mu, out):
    g11, g12, g13 = weights(mu[...] + 2.0)
    ratio = g13 / (mu[...] + 2.0 - 2.0 * g11)
    for c in range(3):
        block = slice(c * NY, (c + 1) * NY)
        share = kept[block, :] + ratio * (outgoing[block, :] + incoming[block, :])
        for i in range(2):
            out[pl.ds(c * 2 + i, BRICKS, stride=6), :] = share[i * BRICKS : (i + 1) * BRICKS]


def line_kernel(flags, received, kh, kl, th, tl, lamx, mu, out):
    shares = jnp.concatenate([received[pl.ds(j, BRICKS, stride=6), :] for j in range(6)], axis=1)
    modes = table_times(kh[...], kl[...], shares)
    factors = []
    for i in range(2):
        row = mu[pl.ds(flags[2] + i * BRICKS, 1), :]
        factors.append((2.0 / (NX + 1)) / (lamx[...] + row))
    modes = modes * jnp.concatenate(factors * 3, axis=1)
    solved = table_times(th[...], tl[...], modes)
    for j in range(6):
        out[pl.ds(j, BRICKS, stride=6), :] = solved[:, j * NZ : (j + 1) * NZ]


def inverse_kernel(
    flags, planes, outgoing, incoming, own, other, advanced, gather, sz, syh, syl, mu, out, send
):
    @pl.when(flags[0] == 0)
    def _():
        out[...] = advanced[...]

    @pl.when(flags[0] != 0)
    def _():
        beta = mu[...] + 2.0
        g11, g12, g13 = weights(beta)
        inv = 1.0 / (beta - 2.0 * g11)
        first = flags[1] == 0
        inside = jnp.where(flags[2] == BRICKS - 1, 0.0, 1.0)
        potentials = []
        for c in range(3):

            def unpacked(ref):
                return jnp.concatenate(
                    [ref[pl.ds(c * 2 + i, BRICKS, stride=6), :] for i in range(2)], axis=0
                )

            block = slice(c * NY, (c + 1) * NY)
            a, b = unpacked(own), unpacked(other)
            before, after = jnp.where(first, a, b), jnp.where(first, b, a)
            middle = (outgoing[block, :] + incoming[block, :] + g13 * (before + after)) * inv
            left = jnp.where(first, before, middle)
            right = jnp.where(first, middle, after)
            f0, f1, f2, f3 = (planes[c, p] for p in range(4))
            u0 = g11 * (f0 + left) + g12 * f1 + g13 * (f2 + right)
            u1 = g12 * (f0 + left + beta * f1 + f2 + right)
            u2 = g13 * (f0 + left) + g12 * f1 + g11 * (f2 + right)
            stack = [u0, u1, u2, right]
            if c:
                stack = [left] + stack + [(beta * right - u2 - f3) * inside]
            field = table_times(syh[...], syl[...], jnp.concatenate(stack, axis=1))
            field = jnp.concatenate(
                [field[:, p * NZ : (p + 1) * NZ] for p in range(len(stack))], axis=0
            )
            potentials.append(times_paired(field, sz[...]))
        rows = iota((RPB, NZ), 0) & (NY - 1)
        lanes = iota((RPB, NZ), 1)

        def dy(field):
            upper = jnp.where(rows == NY - 1, 0.0, pltpu.roll(field, RPB - 1, 0))
            lower = jnp.where(rows == 0, 0.0, pltpu.roll(field, 1, 0))
            return (upper - lower) * 0.5

        def dz(field):
            upper = jnp.where(lanes == NZ - 1, 0.0, pltpu.roll(field, NZ - 1, 1))
            lower = jnp.where(lanes == 0, 0.0, pltpu.roll(field, 1, 1))
            return (upper - lower) * 0.5

        def dx(field):
            return (field[2 * NY : 2 * NY + RPB] - field[:RPB]) * 0.5

        px, py, pz = potentials[0], potentials[1][NY : NY + RPB], potentials[2][NY : NY + RPB]
        velocity = (
            dy(pz) - dz(py),
            dz(px) - dx(potentials[2]),
            dx(potentials[1]) - dy(px),
        )
        for c in range(3):
            out[c] = velocity[c]
            rows_out = pick(gather[...], velocity[c])
            send[:, c * GROUP : (c + 1) * GROUP, :] = rows_out.reshape(TARGETS, GROUP, NZ)


def cell_kernel(received, cells, out):
    for c in range(3):
        rows = received[:, c * GROUP : (c + 1) * GROUP, :].reshape(SLOTS, NZ)
        out[:, c * NJ : (c + 1) * NJ, :] = pick(cells[...], rows).reshape(CZ, NJ, NZ)


def close_kernel(flags, field, layer, remesh, b0, b1, b2, b3, out):
    out[...] = field[...]

    @pl.when(flags[0] == 0)
    def _():
        total = exact((b0[...] + b1[...]) + (b2[...] + b3[...]), remesh[...], NT)
        first = [total[c * NJ : (c + 1) * NJ] for c in range(3)]
        second = [layer[c] for c in range(3)]
        for c in range(3):
            d, e = (c + 1) % 3, (c + 2) % 3
            cross = first[d] * second[e] - first[e] * second[d]
            edge = pl.ds(NI - 1, NJ, stride=NI)
            out[c, edge, :] = field[c, edge, :] + coupling * cross


def call(kernel, outs, flags, *args):
    scalars = [] if flags is None else [flags]
    return pl.pallas_call(
        kernel,
        out_shape=[jax.ShapeDtypeStruct(s, d) for s, d in outs],
        in_specs=[pl.BlockSpec(memory_space=pltpu.SMEM)] * len(scalars)
        + [pl.BlockSpec(memory_space=pltpu.VMEM)] * len(args),
        out_specs=[pl.BlockSpec(memory_space=pltpu.VMEM)] * len(outs),
        name=kernel.__name__,
    )(*scalars, *args)


def place_of(g, y, z, x, c):
    return (((g * CY + y) * CZ + z) * CX + x) * CC + c


def chips():
    return [
        (y, z, x, c) for y in range(CY) for z in range(CZ) for x in range(CX) for c in range(CC)
    ]


def on_device(state, courant, remesh, shell_dest, shell_row, return_dest, return_row, return_block):
    dev = lax.axis_index(DEV)
    flags = jnp.stack(
        [lax.axis_index("grp"), lax.axis_index("core"), dev, lax.axis_index("z")]
    ).astype(i32)
    field = state.reshape(3, RPB, NZ)
    speed = courant.reshape(RPB, NK)
    sy, sz, line = sines(NY), sines(NZ), line_table()
    syh, syl = halves(sy)
    iyh, iyl = halves(sy * (2.0 / (NY + 1)))
    szp, izp = paired(sz), paired(sz * (2.0 / (NZ + 1)))
    kh, kl = halves(line)
    th, tl = np.ascontiguousarray(kh.T), np.ascontiguousarray(kl.T)
    lamx = eigen(NX).astype(np.float32)[:, None]
    mu = (eigen(NY)[:, None] + eigen(NZ)[None, :]).astype(np.float32)

    blocks = field.reshape(3, NJ, NI, NK)[:, :, NI - NI // 4 :, :].reshape(3, SB, NK)
    across = [(place_of(0, *q), place_of(1, *q)) for q in chips()]
    blocks = lax.ppermute(blocks, ALL, across)

    ahead = [(d, (d + 1) % BRICKS) for d in range(BRICKS)]
    last = jnp.concatenate([field[:, 768:, :].reshape(768, NK), speed[896:, :]], axis=0)
    lead = jnp.concatenate([field[:, :256, :].reshape(768, NK), speed[:128, :]], axis=0)
    up = lax.ppermute(last, ALL, ahead)
    down = lax.ppermute(lead, ALL, [(b, a) for a, b in ahead])

    rows = [
        v.reshape(1, SB) for v in (shell_dest, shell_row, return_dest, return_row, return_block)
    ]
    place, gather, codes, merged = call(
        route_kernel,
        [
            ((SLOTS, SB), bf16),
            ((SLOTS, RPB), bf16),
            ((BRICKS, NZ), f32),
            ((2 * NK, 2 * NZ), bf16),
        ],
        flags,
        *rows,
        remesh,
        sz.astype(np.float32),
    )
    codes = lax.all_to_all(codes.reshape(BRICKS, 1, NZ), DEV, 0, 0, tiled=True)
    spread, cells = call(
        decode_kernel,
        [((RPB, SLOTS), bf16), ((CZ * NJ, SLOTS), bf16)],
        flags,
        codes.reshape(BRICKS, NZ),
    )
    advanced, layer = call(
        near_kernel, [((3, RPB, NK), f32), ((3, NJ, NK), f32)], flags, field, speed, up, down
    )

    (bundle,) = call(bucket_kernel, [((3 * SLOTS, NZ), f32)], None, blocks, place, merged)
    bundle = lax.all_to_all(bundle.reshape(BRICKS, 3, CAP, NZ), DEV, 0, 0, tiled=True)
    planes, outgoing, kept = call(
        forward_kernel,
        [((3, 4, NY, NZ), f32), ((3 * NY, NZ), f32), ((3 * NY, NZ), f32)],
        flags,
        bundle.reshape(3 * SLOTS, NZ),
        spread,
        field,
        szp,
        syh,
        syl,
        mu,
    )
    swap = [(0, 1), (1, 0)]
    incoming = lax.ppermute(outgoing, "core", swap)
    (share,) = call(reduce_kernel, [((3 * NY, NZ), f32)], None, outgoing, incoming, kept, mu)
    share = lax.all_to_all(share.reshape(BRICKS, 3, 2, NZ), DEV, 0, 0, tiled=True)
    (solved,) = call(
        line_kernel,
        [((3 * NY, NZ), f32)],
        flags,
        share.reshape(3 * NY, NZ),
        kh,
        kl,
        th,
        tl,
        lamx,
        mu,
    )
    own = lax.all_to_all(solved.reshape(BRICKS, 3, 2, NZ), DEV, 0, 0, tiled=True)
    own = own.reshape(3 * NY, NZ)
    other = lax.ppermute(own, "core", swap)
    result, send = call(
        inverse_kernel,
        [((3, RPB, NZ), f32), ((TARGETS, 3 * GROUP, NZ), f32)],
        flags,
        planes,
        outgoing,
        incoming,
        own,
        other,
        advanced,
        gather,
        izp,
        iyh,
        iyl,
        mu,
    )
    returned = lax.all_to_all(send, ("y", "x", "core"), 0, 0, tiled=True)
    (sums,) = call(cell_kernel, [((CZ, 3 * NJ, NZ), f32)], None, returned, cells)
    parts = []
    for k in range(CZ):
        pairs = [
            (place_of(1, y, z, x, c), place_of(0, y, (z + k) % CZ, x, c)) for y, z, x, c in chips()
        ]
        parts.append(lax.ppermute(sums[k], ALL, pairs))
    (result,) = call(close_kernel, [((3, RPB, NZ), f32)], flags, result, layer, remesh, *parts)
    return result.reshape(1, 3, RPB * NZ)


def solution(mesh):
    fine = Mesh(mesh.devices.reshape(2, CY, CZ, CX, CC), ALL)
    placed = (
        P("grp", None, DEV),
        P(DEV),
        P(),
        P(DEV, None),
        P(DEV),
        P(DEV, None),
        P(DEV),
        P(DEV),
    )
    return jax.shard_map(
        on_device, mesh=fine, in_specs=placed, out_specs=P("grp", None, DEV), check_vma=False
    )
```

```python
import jax
import jax.numpy as jnp
import ml_dtypes
import numpy as np
from jax import lax
from jax.experimental import pallas as pl
from jax.experimental.pallas import tpu as pltpu
from jax.sharding import Mesh
from jax.sharding import PartitionSpec as P

NX, NY, NZ = 512, 256, 128
NI, NK = 64, 128
NJ = 16
CY, CZ, CX, CC = 4, 4, 4, 2
BRICKS = 128
CAP = 4
SB = 256
RPB = 1024
TARGETS = CY * CX * CC
GROUP = CZ * CAP
SLOTS = BRICKS * CAP
DEV = ("y", "z", "x", "core")
ALL = ("grp",) + DEV

viscosity = 0.2
coupling = 1.0
f32 = jnp.float32
bf16 = jnp.bfloat16
i32 = jnp.int32
highest = lax.Precision.HIGHEST
NT = (((1,), (1,)), ((), ()))


def sines(length):
    counts = np.arange(length) + 1
    phase = counts[:, None] * counts[None, :] % (2 * (length + 1))
    return np.sin(np.pi * phase / (length + 1))


def eigen(length):
    counts = np.arange(length) + 1.0
    return 4.0 * np.sin(0.5 * np.pi * counts / (length + 1)) ** 2


def halves(table):
    table = table.astype(np.float32)
    high = table.astype(ml_dtypes.bfloat16)
    low = (table - high.astype(np.float32)).astype(ml_dtypes.bfloat16)
    return high, low


def paired(table):
    high, low = halves(table)
    return np.block([[high, low], [high, np.zeros_like(low)]]).astype(ml_dtypes.bfloat16)


def line_table():
    dev = np.arange(BRICKS)
    plane = np.where(dev % 2 == 1, 4 * dev + 3, 4 * dev - 1) + 1
    phase = (np.arange(NX) + 1)[:, None] * plane[None, :] % (2 * (NX + 1))
    return np.sin(np.pi * phase / (NX + 1))


def iota(shape, axis):
    return lax.broadcasted_iota(i32, shape, axis)


def split(value):
    high = value.astype(bf16)
    return high, (value - high.astype(f32)).astype(bf16)


def mm(a, b):
    return jnp.dot(a, b, preferred_element_type=f32)


def lanes_paired(value):
    return jnp.concatenate(split(value), axis=1)


def fold(value):
    half = value.shape[1] // 2
    return value[:, :half] + value[:, half:]


def pick(onehot, value):
    return fold(mm(onehot, lanes_paired(value)))


def times_paired(value, table):
    return fold(mm(lanes_paired(value), table))


def table_times(high, low, value):
    vh, vl = split(value)
    return mm(high, vh) + mm(high, vl) + mm(low, vh)


def exact(a, b, dims=(((1,), (0,)), ((), ()))):
    return lax.dot_general(a, b, dims, precision=highest, preferred_element_type=f32)


def onehot(condition):
    return jnp.where(condition, 1.0, 0.0).astype(bf16)


def ranks(matches):
    size = matches.shape[1]
    before = onehot(iota((size, size), 0) < iota((size, size), 1))
    counts = mm(matches.astype(bf16), before)
    return jnp.sum(matches * counts, axis=0, keepdims=True).astype(i32)


def route_kernel(flags, sd, sr, rd, rr, rb, remesh, sz, place, gather, codes, merged):
    zme = flags[3]
    bricks = iota((BRICKS, SB), 0)
    matches = jnp.where(bricks == sd[...], 1.0, 0.0)
    rank = ranks(matches)
    slot = rank * BRICKS + sd[...]
    place[...] = onehot(iota((SLOTS, SB), 0) == slot)
    tagged = jnp.where(bricks == rank, (sr[...] + 1).astype(f32), 0.0)
    sent = exact(matches, tagged, NT)
    owner = rd[...]
    oc = owner & (CC - 1)
    ox = (owner >> 1) & (CX - 1)
    oz = (owner >> 3) & (CZ - 1)
    oy = owner >> 5
    rank = ranks(jnp.where(bricks == owner, 1.0, 0.0))
    lane = oz * CAP + rank
    slot = ((oy * CX + ox) * CC + oc) * GROUP + lane
    gather[...] = lax.dot_general(
        onehot(iota((SLOTS, SB), 0) == slot),
        onehot(iota((RPB, SB), 0) == rr[...]),
        NT,
        preferred_element_type=f32,
    ).astype(bf16)
    via = ((oy * CZ + zme) * CX + ox) * CC + oc
    code = ((oz - zme) & (CZ - 1)) * NJ + rb[...] + 1
    tagged = jnp.where(bricks == lane + CAP, code.astype(f32), 0.0)
    codes[...] = sent + exact(jnp.where(bricks == via, 1.0, 0.0), tagged, NT)
    both = exact(remesh[...], sz[...])
    high, low = split(both)
    merged[...] = jnp.concatenate(
        [
            jnp.concatenate([high, low], axis=1),
            jnp.concatenate([high, jnp.zeros_like(low)], axis=1),
        ],
        axis=0,
    )


def decode_kernel(flags, codes, landing, cells):
    zme = flags[3]
    turned = codes[...].T
    landing[...] = jnp.concatenate([turned[i : i + 1, :] for i in range(CAP)], axis=1).astype(i32)
    target = iota((TARGETS, BRICKS), 0)
    source = ((target >> 3) * CZ + zme) * (CX * CC) + (target & (CX * CC - 1))
    chosen = exact(jnp.where(iota((TARGETS, BRICKS), 1) == source, 1.0, 0.0), codes[...])
    wide = jnp.where(
        iota((BRICKS, SLOTS), 0) == (iota((BRICKS, SLOTS), 1) & (GROUP - 1)) + CAP, 1.0, 0.0
    )
    chosen = exact(chosen, wide)
    own = iota((TARGETS, SLOTS), 0) == (iota((TARGETS, SLOTS), 1) >> 4)
    code = jnp.sum(jnp.where(own, chosen, 0.0), axis=0, keepdims=True).astype(i32)
    cells[...] = onehot(iota((CZ * NJ, SLOTS), 0) == code - 1)


def local_kernel(flags, state, courant, up, down, sz, out, layer):
    @pl.when(flags[0] == 0)
    def _():
        cr = jnp.concatenate([up[768:896, :], courant[...], down[768:896, :]], axis=0)

        def step(field, speed):
            rows = speed.shape[0]
            centre = field[128 : 128 + rows]
            transport = (
                8.0 * (field[192 : 192 + rows] - field[64 : 64 + rows])
                - (field[256 : 256 + rows] - field[:rows])
            ) / 12.0
            place = iota((rows, NK), 0) & (NI - 1)
            above = jnp.where(place == NI - 1, 0.0, pltpu.roll(centre, rows - 1, 0))
            below = jnp.where(place == 0, 0.0, pltpu.roll(centre, 1, 0))
            return centre - speed * transport + viscosity * (above - 2.0 * centre + below)

        for c in range(3):
            field = jnp.concatenate(
                [up[c * 256 : (c + 1) * 256, :], state[c], down[c * 256 : (c + 1) * 256, :]], axis=0
            )
            field = step(field, cr)
            out[c] = step(field, courant[...])
            layer[c] = state[c, pl.ds(NI - 1, NJ, stride=NI), :]

    @pl.when(flags[0] != 0)
    def _():
        for c in range(3):
            out[c] = times_paired(state[c], sz[...])


def bucket_kernel(blocks, place, merged, out):
    for c in range(3):
        moved = times_paired(blocks[c], merged[...])
        slots = pick(place[...], moved)
        for rank in range(CAP):
            out[pl.ds(c * CAP + rank, BRICKS, stride=3 * CAP), :] = slots[
                rank * BRICKS : (rank + 1) * BRICKS
            ]


def weights(beta):
    outer = beta * beta - 2.0
    g12 = 1.0 / outer
    g13 = g12 / beta
    g11 = (beta * beta - 1.0) * g13
    return g11, g12, g13


def forward_kernel(flags, received, landing, work, syh, syl, mu, planes, outgoing, kept):
    beta = mu[...] + 2.0
    g11, g12, g13 = weights(beta)
    first = flags[1] == 0
    spread = onehot(iota((RPB, SLOTS), 0) == landing[...] - 1)
    for c in range(3):
        rows = jnp.concatenate(
            [received[pl.ds(c * CAP + r, BRICKS, stride=3 * CAP), :] for r in range(CAP)], axis=0
        )
        field = pick(spread, rows) + work[c]
        field = jnp.concatenate([field[p * NY : (p + 1) * NY] for p in range(4)], axis=1)
        field = table_times(syh[...], syl[...], field)
        f0, f1, f2, f3 = (field[:, p * NZ : (p + 1) * NZ] for p in range(4))
        for p, plane in enumerate((f0, f1, f2, f3)):
            planes[c, p] = plane
        low = g11 * f0 + g12 * f1 + g13 * f2
        high = f3 + g13 * f0 + g12 * f1 + g11 * f2
        outgoing[c * NY : (c + 1) * NY, :] = jnp.where(first, high, low)
        kept[c * NY : (c + 1) * NY, :] = jnp.where(first, low, high)


def reduce_kernel(outgoing, incoming, kept, mu, out):
    g11, g12, g13 = weights(mu[...] + 2.0)
    ratio = g13 / (mu[...] + 2.0 - 2.0 * g11)
    for c in range(3):
        block = slice(c * NY, (c + 1) * NY)
        share = kept[block, :] + ratio * (outgoing[block, :] + incoming[block, :])
        for i in range(2):
            out[pl.ds(c * 2 + i, BRICKS, stride=6), :] = share[i * BRICKS : (i + 1) * BRICKS]


def line_kernel(flags, received, kh, kl, th, tl, lamx, mu, out):
    shares = jnp.concatenate([received[pl.ds(j, BRICKS, stride=6), :] for j in range(6)], axis=1)
    modes = table_times(kh[...], kl[...], shares)
    factors = []
    for i in range(2):
        row = mu[pl.ds(flags[2] + i * BRICKS, 1), :]
        factors.append((2.0 / (NX + 1)) / (lamx[...] + row))
    modes = modes * jnp.concatenate(factors * 3, axis=1)
    solved = table_times(th[...], tl[...], modes)
    for j in range(6):
        out[pl.ds(j, BRICKS, stride=6), :] = solved[:, j * NZ : (j + 1) * NZ]


def inverse_kernel(
    flags,
    planes,
    outgoing,
    incoming,
    own,
    other,
    work,
    gather,
    sz,
    syh,
    syl,
    mu,
    out,
    send,
    held,
    rows_held,
    out_sems,
    send_sems,
):
    @pl.when(flags[0] == 0)
    def _():
        copy = pltpu.make_async_copy(work, out, out_sems.at[0])
        copy.start()
        copy.wait()

    @pl.when(flags[0] != 0)
    def _():
        beta = mu[...] + 2.0
        g11, g12, g13 = weights(beta)
        inv = 1.0 / (beta - 2.0 * g11)
        first = flags[1] == 0
        inside = jnp.where(flags[2] == BRICKS - 1, 0.0, 1.0)
        potentials = []
        for c in range(3):

            def unpacked(ref):
                return jnp.concatenate(
                    [ref[pl.ds(c * 2 + i, BRICKS, stride=6), :] for i in range(2)], axis=0
                )

            block = slice(c * NY, (c + 1) * NY)
            a, b = unpacked(own), unpacked(other)
            before, after = jnp.where(first, a, b), jnp.where(first, b, a)
            middle = (outgoing[block, :] + incoming[block, :] + g13 * (before + after)) * inv
            left = jnp.where(first, before, middle)
            right = jnp.where(first, middle, after)
            f0, f1, f2, f3 = (planes[c, p] for p in range(4))
            u0 = g11 * (f0 + left) + g12 * f1 + g13 * (f2 + right)
            u1 = g12 * (f0 + left + beta * f1 + f2 + right)
            u2 = g13 * (f0 + left) + g12 * f1 + g11 * (f2 + right)
            stack = [u0, u1, u2, right]
            if c:
                stack = [left] + stack + [(beta * right - u2 - f3) * inside]
            field = table_times(syh[...], syl[...], jnp.concatenate(stack, axis=1))
            field = jnp.concatenate(
                [field[:, p * NZ : (p + 1) * NZ] for p in range(len(stack))], axis=0
            )
            potentials.append(times_paired(field, sz[...]))
        rows = iota((RPB, NZ), 0) & (NY - 1)
        lanes = iota((RPB, NZ), 1)

        def dy(field):
            upper = jnp.where(rows == NY - 1, 0.0, pltpu.roll(field, RPB - 1, 0))
            lower = jnp.where(rows == 0, 0.0, pltpu.roll(field, 1, 0))
            return (upper - lower) * 0.5

        def dz(field):
            upper = jnp.where(lanes == NZ - 1, 0.0, pltpu.roll(field, NZ - 1, 1))
            lower = jnp.where(lanes == 0, 0.0, pltpu.roll(field, 1, 1))
            return (upper - lower) * 0.5

        def dx(field):
            return (field[2 * NY : 2 * NY + RPB] - field[:RPB]) * 0.5

        px, py, pz = potentials[0], potentials[1][NY : NY + RPB], potentials[2][NY : NY + RPB]
        velocity = (
            dy(pz) - dz(py),
            dz(px) - dx(potentials[2]),
            dx(potentials[1]) - dy(px),
        )
        copies = []
        for c in range(3):
            held[c] = velocity[c]
            copies.append(pltpu.make_async_copy(held.at[c], out.at[c], out_sems.at[c]))
            copies[-1].start()
        for c in range(3):
            rows_out = pick(gather[...], velocity[c])
            rows_held[c] = rows_out.reshape(TARGETS, GROUP, NZ)
            target = send.at[:, pl.ds(c * GROUP, GROUP), :]
            copies.append(pltpu.make_async_copy(rows_held.at[c], target, send_sems.at[c]))
            copies[-1].start()
        for copy in copies:
            copy.wait()


def cell_kernel(received, cells, *outs):
    for c in range(3):
        rows = received[:, c * GROUP : (c + 1) * GROUP, :].reshape(SLOTS, NZ)
        sums = pick(cells[...], rows)
        for k in range(CZ):
            outs[k][c * NJ : (c + 1) * NJ, :] = sums[k * NJ : (k + 1) * NJ]


def close_kernel(flags, field, work, layer, remesh, b0, b1, b2, b3, out, slab, sem):
    @pl.when(flags[0] == 0)
    def _():
        total = exact((b0[...] + b1[...]) + (b2[...] + b3[...]), remesh[...], NT)
        first = [total[c * NJ : (c + 1) * NJ] for c in range(3)]
        second = [layer[c] for c in range(3)]
        for c in range(3):
            d, e = (c + 1) % 3, (c + 2) % 3
            cross = first[d] * second[e] - first[e] * second[d]
            for j in range(NJ):
                row = c * RPB + (j + 1) * NI
                slab[c, j, :7, :] = work[c, row - c * RPB - 8 : row - c * RPB - 1, :]
            slab[c, :, 7, :] = work[c, pl.ds(NI - 1, NJ, stride=NI), :] + coupling * cross
        copy = pltpu.make_async_copy(slab, out.at[:, :, pl.ds(NI - 8, 8), :], sem)
        copy.start()
        copy.wait()


def call(kernel, outs, flags, *args, home=pltpu.VMEM, alias=False, scratch=(), free=False):
    scalars = [] if flags is None else [flags]
    args = [jnp.asarray(a) for a in args]
    kept = [args.pop(0)] if alias else []
    return pl.pallas_call(
        kernel,
        out_shape=[(jax.ShapeDtypeStruct if free else home)(s, d) for s, d in outs],
        in_specs=[pl.BlockSpec(memory_space=pltpu.SMEM)] * len(scalars)
        + [pl.BlockSpec(memory_space=pltpu.HBM)] * len(kept)
        + [pl.BlockSpec(memory_space=pltpu.VMEM)] * len(args),
        out_specs=[pl.BlockSpec(memory_space=home)] * len(outs),
        scratch_shapes=list(scratch),
        input_output_aliases={len(scalars): 0} if alias else {},
        compiler_params=pltpu.CompilerParams(vmem_limit_bytes=24 << 20),
        name=kernel.__name__,
    )(
        *scalars,
        *kept,
        *[a if free else pltpu.with_memory_space_constraint(a, pltpu.VMEM) for a in args],
    )


def place_of(g, y, z, x, c):
    return (((g * CY + y) * CZ + z) * CX + x) * CC + c


def chips():
    return [
        (y, z, x, c) for y in range(CY) for z in range(CZ) for x in range(CX) for c in range(CC)
    ]


def on_device(state, courant, remesh, shell_dest, shell_row, return_dest, return_row, return_block):
    dev = lax.axis_index(DEV)
    flags = jnp.stack(
        [lax.axis_index("grp"), lax.axis_index("core"), dev, lax.axis_index("z")]
    ).astype(i32)
    field = state.reshape(3, RPB, NZ)
    speed = courant.reshape(RPB, NK)
    sy, sz, line = sines(NY), sines(NZ), line_table()
    syh, syl = halves(sy)
    iyh, iyl = halves(sy * (2.0 / (NY + 1)))
    szp, izp = paired(sz), paired(sz * (2.0 / (NZ + 1)))
    kh, kl = halves(line)
    th, tl = np.ascontiguousarray(kh.T), np.ascontiguousarray(kl.T)
    lamx = eigen(NX).astype(np.float32)[:, None]
    mu = (eigen(NY)[:, None] + eigen(NZ)[None, :]).astype(np.float32)

    blocks = field.reshape(3, NJ, NI, NK)[:, :, NI - NI // 4 :, :].reshape(3, SB, NK)
    across = [(place_of(0, *q), place_of(1, *q)) for q in chips()]
    blocks = lax.ppermute(blocks, ALL, across)

    ahead = [(d, (d + 1) % BRICKS) for d in range(BRICKS)]
    last = jnp.concatenate([field[:, 768:, :].reshape(768, NK), speed[896:, :]], axis=0)
    lead = jnp.concatenate([field[:, :256, :].reshape(768, NK), speed[:128, :]], axis=0)
    up = lax.ppermute(last, ALL, ahead)
    down = lax.ppermute(lead, ALL, [(b, a) for a, b in ahead])

    rows = [
        v.reshape(1, SB) for v in (shell_dest, shell_row, return_dest, return_row, return_block)
    ]
    place, gather, codes, merged = call(
        route_kernel,
        [
            ((SLOTS, SB), bf16),
            ((SLOTS, RPB), bf16),
            ((BRICKS, NZ), f32),
            ((2 * NK, 2 * NZ), bf16),
        ],
        flags,
        *rows,
        remesh,
        sz.astype(np.float32),
        free=True,
    )
    codes = lax.all_to_all(codes.reshape(BRICKS, 1, NZ), DEV, 0, 0, tiled=True)
    landing, cells = call(
        decode_kernel,
        [((1, SLOTS), i32), ((CZ * NJ, SLOTS), bf16)],
        flags,
        codes.reshape(BRICKS, NZ),
        free=True,
    )
    work, layer = call(
        local_kernel,
        [((3, RPB, NK), f32), ((3, NJ, NK), f32)],
        flags,
        field,
        speed,
        up,
        down,
        szp,
    )

    (bundle,) = call(bucket_kernel, [((3 * SLOTS, NZ), f32)], None, blocks, place, merged)
    bundle = lax.all_to_all(bundle.reshape(BRICKS, 3, CAP, NZ), DEV, 0, 0, tiled=True)
    planes, outgoing, kept = call(
        forward_kernel,
        [((3, 4, NY, NZ), f32), ((3 * NY, NZ), f32), ((3 * NY, NZ), f32)],
        flags,
        bundle.reshape(3 * SLOTS, NZ),
        landing,
        work,
        syh,
        syl,
        mu,
    )
    swap = [(0, 1), (1, 0)]
    incoming = lax.ppermute(outgoing, "core", swap)
    (share,) = call(reduce_kernel, [((3 * NY, NZ), f32)], None, outgoing, incoming, kept, mu)
    share = lax.all_to_all(share.reshape(BRICKS, 3, 2, NZ), DEV, 0, 0, tiled=True)
    (solved,) = call(
        line_kernel,
        [((3 * NY, NZ), f32)],
        flags,
        share.reshape(3 * NY, NZ),
        kh,
        kl,
        th,
        tl,
        lamx,
        mu,
    )
    own = lax.all_to_all(solved.reshape(BRICKS, 3, 2, NZ), DEV, 0, 0, tiled=True)
    own = own.reshape(3 * NY, NZ)
    other = lax.ppermute(own, "core", swap)
    result, send = call(
        inverse_kernel,
        [((3, RPB, NZ), f32), ((TARGETS, 3 * GROUP, NZ), f32)],
        flags,
        planes,
        outgoing,
        incoming,
        own,
        other,
        work,
        gather,
        izp,
        iyh,
        iyl,
        mu,
        home=pltpu.HBM,
        scratch=[
            pltpu.VMEM((3, RPB, NZ), f32),
            pltpu.VMEM((3, TARGETS, GROUP, NZ), f32),
            pltpu.SemaphoreType.DMA((3,)),
            pltpu.SemaphoreType.DMA((3,)),
        ],
    )
    returned = lax.all_to_all(send, ("y", "x", "core"), 0, 0, tiled=True)
    sums = call(cell_kernel, [((3 * NJ, NZ), f32)] * CZ, None, returned, cells)
    parts = []
    for k in range(CZ):
        pairs = [
            (place_of(1, y, z, x, c), place_of(0, y, (z + k) % CZ, x, c)) for y, z, x, c in chips()
        ]
        parts.append(lax.ppermute(sums[k], ALL, pairs))
    (result,) = call(
        close_kernel,
        [((3, NJ, NI, NZ), f32)],
        flags,
        result.reshape(3, NJ, NI, NZ),
        work,
        layer,
        remesh,
        *parts,
        home=pltpu.HBM,
        alias=True,
        scratch=[pltpu.VMEM((3, NJ, 8, NZ), f32), pltpu.SemaphoreType.DMA],
    )
    return result.reshape(1, 3, RPB * NZ)


def solution(mesh):
    fine = Mesh(mesh.devices.reshape(2, CY, CZ, CX, CC), ALL)
    placed = (
        P("grp", None, DEV),
        P(DEV),
        P(),
        P(DEV, None),
        P(DEV),
        P(DEV, None),
        P(DEV),
        P(DEV),
    )
    return jax.shard_map(
        on_device, mesh=fine, in_specs=placed, out_specs=P("grp", None, DEV), check_vma=False
    )
```

```python
import jax
import jax.numpy as jnp
import ml_dtypes
import numpy as np
from jax import lax
from jax.experimental import pallas as pl
from jax.experimental.pallas import tpu as pltpu
from jax.sharding import Mesh
from jax.sharding import PartitionSpec as P

NX, NY, NZ = 512, 256, 128
NI, NK = 64, 128
NJ = 16
CY, CZ, CX, CC = 4, 4, 4, 2
BRICKS = 128
CAP = 4
SB = 256
RPB = 1024
TARGETS = CY * CX * CC
GROUP = CZ * CAP
SLOTS = BRICKS * CAP
DEV = ("y", "z", "x", "core")
ALL = ("grp",) + DEV

viscosity = 0.2
coupling = 1.0
f32 = jnp.float32
bf16 = jnp.bfloat16
i32 = jnp.int32
highest = lax.Precision.HIGHEST
NT = (((1,), (1,)), ((), ()))


def sines(length):
    counts = np.arange(length) + 1
    phase = counts[:, None] * counts[None, :] % (2 * (length + 1))
    return np.sin(np.pi * phase / (length + 1))


def eigen(length):
    counts = np.arange(length) + 1.0
    return 4.0 * np.sin(0.5 * np.pi * counts / (length + 1)) ** 2


def halves(table):
    table = table.astype(np.float32)
    high = table.astype(ml_dtypes.bfloat16)
    low = (table - high.astype(np.float32)).astype(ml_dtypes.bfloat16)
    return high, low


def paired(table):
    high, low = halves(table)
    return np.block([[high, low], [high, np.zeros_like(low)]]).astype(ml_dtypes.bfloat16)


def line_table():
    dev = np.arange(BRICKS)
    plane = np.where(dev % 2 == 1, 4 * dev + 3, 4 * dev - 1) + 1
    phase = (np.arange(NX) + 1)[:, None] * plane[None, :] % (2 * (NX + 1))
    return np.sin(np.pi * phase / (NX + 1))


def iota(shape, axis):
    return lax.broadcasted_iota(i32, shape, axis)


def split(value):
    high = value.astype(bf16)
    return high, (value - high.astype(f32)).astype(bf16)


def mm(a, b):
    return jnp.dot(a, b, preferred_element_type=f32)


def lanes_paired(value):
    return jnp.concatenate(split(value), axis=1)


def fold(value):
    half = value.shape[1] // 2
    return value[:, :half] + value[:, half:]


def pick(onehot, value):
    return fold(mm(onehot, lanes_paired(value)))


def times_paired(value, table):
    return fold(mm(lanes_paired(value), table))


def table_times(high, low, value):
    vh, vl = split(value)
    return mm(high, vh) + mm(high, vl) + mm(low, vh)


def exact(a, b, dims=(((1,), (0,)), ((), ()))):
    return lax.dot_general(a, b, dims, precision=highest, preferred_element_type=f32)


def onehot(condition):
    return jnp.where(condition, 1.0, 0.0).astype(bf16)


def ranks(matches):
    size = matches.shape[1]
    before = onehot(iota((size, size), 0) < iota((size, size), 1))
    counts = mm(matches.astype(bf16), before)
    return jnp.sum(matches * counts, axis=0, keepdims=True).astype(i32)


def owners(owner):
    core = owner & (CC - 1)
    x = (owner >> 1) & (CX - 1)
    z = (owner >> 3) & (CZ - 1)
    lane = z * CAP + ranks(jnp.where(iota((BRICKS, SB), 0) == owner, 1.0, 0.0))
    return owner >> 5, z, x, core, lane


def route_kernel(flags, sd, sr, rd, rb, remesh, sz, place, codes, merged):
    bricks = iota((BRICKS, SB), 0)
    matches = jnp.where(bricks == sd[...], 1.0, 0.0)
    rank = ranks(matches)
    slot = rank * BRICKS + sd[...]
    place[...] = onehot(iota((SLOTS, SB), 0) == slot)
    tagged = jnp.where(bricks == rank, (sr[...] + 1).astype(f32), 0.0)
    sent = exact(matches, tagged, NT)
    zme = flags[3]
    y, z, x, core, lane = owners(rd[...])
    via = ((y * CZ + zme) * CX + x) * CC + core
    code = ((z - zme) & (CZ - 1)) * NJ + rb[...] + 1
    tagged = jnp.where(bricks == lane + CAP, code.astype(f32), 0.0)
    codes[...] = sent + exact(jnp.where(bricks == via, 1.0, 0.0), tagged, NT)
    high, low = split(exact(remesh[...], sz[...]))
    merged[...] = jnp.concatenate(
        [
            jnp.concatenate([high, low], axis=1),
            jnp.concatenate([high, jnp.zeros_like(low)], axis=1),
        ],
        axis=0,
    )


def decode_kernel(flags, codes, rd, rr, landing, cells, gather):
    @pl.when(flags[0] != 0)
    def _():
        zme = flags[3]
        turned = codes[...].T
        landing[...] = jnp.concatenate(
            [turned[i : i + 1, :] for i in range(CAP)], axis=1
        ).astype(i32)
        target = iota((TARGETS, BRICKS), 0)
        source = ((target >> 3) * CZ + zme) * (CX * CC) + (target & (CX * CC - 1))
        chosen = exact(jnp.where(iota((TARGETS, BRICKS), 1) == source, 1.0, 0.0), codes[...])
        wide = jnp.where(
            iota((BRICKS, SLOTS), 0) == (iota((BRICKS, SLOTS), 1) & (GROUP - 1)) + CAP, 1.0, 0.0
        )
        chosen = exact(chosen, wide)
        own = iota((TARGETS, SLOTS), 0) == (iota((TARGETS, SLOTS), 1) >> 4)
        code = jnp.sum(jnp.where(own, chosen, 0.0), axis=0, keepdims=True).astype(i32)
        cells[...] = onehot(iota((CZ * NJ, SLOTS), 0) == code - 1)
        y, _, x, core, lane = owners(rd[...])
        slot = ((y * CX + x) * CC + core) * GROUP + lane
        gather[...] = lax.dot_general(
            onehot(iota((SLOTS, SB), 0) == slot),
            onehot(iota((RPB, SB), 0) == rr[...]),
            NT,
            preferred_element_type=f32,
        ).astype(bf16)


def near_kernel(flags, state, courant, up, down, out, edge, layer):
    @pl.when(flags[0] == 0)
    def _():
        cr = jnp.concatenate([up[768:896, :], courant[...], down[768:896, :]], axis=0)

        def step(field, speed):
            rows = speed.shape[0]
            centre = field[128 : 128 + rows]
            transport = (
                8.0 * (field[192 : 192 + rows] - field[64 : 64 + rows])
                - (field[256 : 256 + rows] - field[:rows])
            ) / 12.0
            place = iota((rows, NK), 0) & (NI - 1)
            above = jnp.where(place == NI - 1, 0.0, pltpu.roll(centre, rows - 1, 0))
            below = jnp.where(place == 0, 0.0, pltpu.roll(centre, 1, 0))
            return centre - speed * transport + viscosity * (above - 2.0 * centre + below)

        for c in range(3):
            field = jnp.concatenate(
                [up[c * 256 : (c + 1) * 256, :], state[c], down[c * 256 : (c + 1) * 256, :]], axis=0
            )
            field = step(field, cr)
            field = step(field, courant[...])
            out[c] = field
            edge[c] = field.reshape(NJ, NI, NK)[:, NI - 8 :, :]
            layer[c] = state[c, pl.ds(NI - 1, NJ, stride=NI), :]


def ready_kernel(flags, state, speed, sz, kh, kl, out, th, tl, last, lead):
    @pl.when(flags[0] == 0)
    def _():
        for c in range(3):
            last[c * 256 : (c + 1) * 256, :] = state[c, 768:, :]
            lead[c * 256 : (c + 1) * 256, :] = state[c, :256, :]
        last[768:, :] = speed[896:, :]
        lead[768:, :] = speed[:128, :]

    @pl.when(flags[0] != 0)
    def _():
        for c in range(3):
            out[c] = times_paired(state[c], sz[...])
        th[...] = kh[...].T
        tl[...] = kl[...].T


def bucket_kernel(flags, blocks, place, merged, out):
    @pl.when(flags[0] != 0)
    def _():
        for c in range(3):
            moved = times_paired(blocks[c], merged[...])
            slots = pick(place[...], moved)
            for rank in range(CAP):
                out[pl.ds(c * CAP + rank, BRICKS, stride=3 * CAP), :] = slots[
                    rank * BRICKS : (rank + 1) * BRICKS
                ]


def weights(beta):
    outer = beta * beta - 2.0
    g12 = 1.0 / outer
    g13 = g12 / beta
    g11 = (beta * beta - 1.0) * g13
    return g11, g12, g13


def forward_kernel(flags, received, landing, work, syh, syl, mu, planes, outgoing, kept):
    @pl.when(flags[0] != 0)
    def _():
        beta = mu[...] + 2.0
        g11, g12, g13 = weights(beta)
        first = flags[1] == 0
        spread = onehot(iota((RPB, SLOTS), 0) == landing[...] - 1)
        for c in range(3):
            rows = jnp.concatenate(
                [received[pl.ds(c * CAP + r, BRICKS, stride=3 * CAP), :] for r in range(CAP)], axis=0
            )
            field = (pick(spread, rows) + work[c]) * (4.0 / ((NY + 1) * (NZ + 1)))
            field = jnp.concatenate([field[p * NY : (p + 1) * NY] for p in range(4)], axis=1)
            field = table_times(syh[...], syl[...], field)
            f0, f1, f2, f3 = (field[:, p * NZ : (p + 1) * NZ] for p in range(4))
            for p, plane in enumerate((f0, f1, f2, f3)):
                planes[c, p] = plane
            low = g11 * f0 + g12 * f1 + g13 * f2
            high = f3 + g13 * f0 + g12 * f1 + g11 * f2
            outgoing[c * NY : (c + 1) * NY, :] = jnp.where(first, high, low)
            kept[c * NY : (c + 1) * NY, :] = jnp.where(first, low, high)


def reduce_kernel(flags, outgoing, incoming, kept, mu, out):
    @pl.when(flags[0] != 0)
    def _():
        g11, g12, g13 = weights(mu[...] + 2.0)
        ratio = g13 / (mu[...] + 2.0 - 2.0 * g11)
        for c in range(3):
            block = slice(c * NY, (c + 1) * NY)
            share = kept[block, :] + ratio * (outgoing[block, :] + incoming[block, :])
            for i in range(2):
                out[pl.ds(c * 2 + i, BRICKS, stride=6), :] = share[i * BRICKS : (i + 1) * BRICKS]


def line_kernel(flags, received, kh, kl, th, tl, lamx, mu, out):
    @pl.when(flags[0] != 0)
    def _():
        shares = jnp.concatenate([received[pl.ds(j, BRICKS, stride=6), :] for j in range(6)], axis=1)
        modes = table_times(kh[...], kl[...], shares)
        factors = []
        for i in range(2):
            row = mu[pl.ds(flags[2] + i * BRICKS, 1), :]
            factors.append((2.0 / (NX + 1)) / (lamx[...] + row))
        modes = modes * jnp.concatenate(factors * 3, axis=1)
        solved = table_times(th[...], tl[...], modes)
        for j in range(6):
            out[pl.ds(j, BRICKS, stride=6), :] = solved[:, j * NZ : (j + 1) * NZ]


def inverse_kernel(
    flags,
    advanced,
    planes,
    outgoing,
    incoming,
    own,
    other,
    gather,
    sz,
    syh,
    syl,
    mu,
    out,
    send,
    held,
    rows_held,
    out_sems,
    send_sems,
):
    @pl.when(flags[0] != 0)
    def _():
        beta = mu[...] + 2.0
        g11, g12, g13 = weights(beta)
        inv = 1.0 / (beta - 2.0 * g11)
        first = flags[1] == 0
        inside = jnp.where(flags[2] == BRICKS - 1, 0.0, 1.0)
        potentials = []
        for c in range(3):

            def unpacked(ref):
                return jnp.concatenate(
                    [ref[pl.ds(c * 2 + i, BRICKS, stride=6), :] for i in range(2)], axis=0
                )

            block = slice(c * NY, (c + 1) * NY)
            a, b = unpacked(own), unpacked(other)
            before, after = jnp.where(first, a, b), jnp.where(first, b, a)
            middle = (outgoing[block, :] + incoming[block, :] + g13 * (before + after)) * inv
            left = jnp.where(first, before, middle)
            right = jnp.where(first, middle, after)
            f0, f1, f2, f3 = (planes[c, p] for p in range(4))
            u0 = g11 * (f0 + left) + g12 * f1 + g13 * (f2 + right)
            u1 = g12 * (f0 + left + beta * f1 + f2 + right)
            u2 = g13 * (f0 + left) + g12 * f1 + g11 * (f2 + right)
            stack = [u0, u1, u2, right]
            if c:
                stack = [left] + stack + [(beta * right - u2 - f3) * inside]
            field = table_times(syh[...], syl[...], jnp.concatenate(stack, axis=1))
            field = jnp.concatenate(
                [field[:, p * NZ : (p + 1) * NZ] for p in range(len(stack))], axis=0
            )
            potentials.append(times_paired(field, sz[...]))
        rows = iota((RPB, NZ), 0) & (NY - 1)
        lanes = iota((RPB, NZ), 1)

        def dy(field):
            upper = jnp.where(rows == NY - 1, 0.0, pltpu.roll(field, RPB - 1, 0))
            lower = jnp.where(rows == 0, 0.0, pltpu.roll(field, 1, 0))
            return (upper - lower) * 0.5

        def dz(field):
            upper = jnp.where(lanes == NZ - 1, 0.0, pltpu.roll(field, NZ - 1, 1))
            lower = jnp.where(lanes == 0, 0.0, pltpu.roll(field, 1, 1))
            return (upper - lower) * 0.5

        def dx(field):
            return (field[2 * NY : 2 * NY + RPB] - field[:RPB]) * 0.5

        px, py, pz = potentials[0], potentials[1][NY : NY + RPB], potentials[2][NY : NY + RPB]
        velocity = (
            dy(pz) - dz(py),
            dz(px) - dx(potentials[2]),
            dx(potentials[1]) - dy(px),
        )
        copies = []
        for c in range(3):
            held[c] = velocity[c]
            copies.append(pltpu.make_async_copy(held.at[c], out.at[c], out_sems.at[c]))
            copies[-1].start()
        for c in range(3):
            rows_out = pick(gather[...], velocity[c])
            rows_held[c] = rows_out.reshape(TARGETS, GROUP, NZ)
            target = send.at[:, pl.ds(c * GROUP, GROUP), :]
            copies.append(pltpu.make_async_copy(rows_held.at[c], target, send_sems.at[c]))
            copies[-1].start()
        for copy in copies:
            copy.wait()


def cell_kernel(flags, received, cells, *outs):
    @pl.when(flags[0] != 0)
    def _():
        for c in range(3):
            rows = received[:, c * GROUP : (c + 1) * GROUP, :].reshape(SLOTS, NZ)
            sums = pick(cells[...], rows)
            for k in range(CZ):
                outs[k][c * NJ : (c + 1) * NJ, :] = sums[k * NJ : (k + 1) * NJ]


def close_kernel(flags, field, edge, layer, remesh, b0, b1, b2, b3, out, slab, sem):
    @pl.when(flags[0] == 0)
    def _():
        total = exact((b0[...] + b1[...]) + (b2[...] + b3[...]), remesh[...], NT)
        first = [total[c * NJ : (c + 1) * NJ] for c in range(3)]
        second = [layer[c] for c in range(3)]
        for c in range(3):
            d, e = (c + 1) % 3, (c + 2) % 3
            cross = first[d] * second[e] - first[e] * second[d]
            slab[c] = edge[c]
            slab[c, :, 7, :] = edge[c, :, 7, :] + coupling * cross
        copy = pltpu.make_async_copy(slab, out.at[:, :, pl.ds(NI - 8, 8), :], sem)
        copy.start()
        copy.wait()


def call(kernel, outs, flags, *args, fetch=False, raw=False, alias=False, scratch=()):
    args = [jnp.asarray(a) for a in args]
    spaces = [pltpu.HBM if fetch or (alias and i == 0) else pltpu.VMEM for i in range(len(args))]
    homes = [raw or len(o) > 2 for o in outs]
    staged = [] if raw else [i for i, home in enumerate(homes) if home]
    loads = [pltpu.VMEM(a.shape, a.dtype) for a in args] if fetch else []
    stores = [pltpu.VMEM(*outs[i][:2]) for i in staged]
    sems = [pltpu.SemaphoreType.DMA((len(loads) + len(stores),))] if loads or stores else []

    def body(flags, *refs):
        given, made = list(refs[: len(args)]), list(refs[len(args) : len(args) + len(outs)])
        rest = refs[len(args) + len(outs) :]
        held, kept = rest[: len(loads)], rest[len(loads) : len(loads) + len(stores)]
        own = rest[len(loads) + len(stores) + len(sems) :]
        if sems:
            sem = rest[len(loads) + len(stores)]
        copies = [
            pltpu.make_async_copy(a, b, sem.at[i]) for i, (a, b) in enumerate(zip(given, held))
        ]
        for copy in copies:
            copy.start()
        for copy in copies:
            copy.wait()
        homes_out = [made[i] for i in staged]
        for i, ref in zip(staged, kept):
            made[i] = ref
        kernel(flags, *(held if fetch else given), *made, *own)
        copies = [
            pltpu.make_async_copy(a, b, sem.at[len(loads) + i])
            for i, (a, b) in enumerate(zip(kept, homes_out))
        ]
        for copy in copies:
            copy.start()
        for copy in copies:
            copy.wait()

    return pl.pallas_call(
        body,
        out_shape=[(pltpu.HBM if home else pltpu.VMEM)(*o[:2]) for o, home in zip(outs, homes)],
        in_specs=[pl.BlockSpec(memory_space=pltpu.SMEM)]
        + [pl.BlockSpec(memory_space=space) for space in spaces],
        out_specs=[
            pl.BlockSpec(memory_space=pltpu.HBM if home else pltpu.VMEM) for home in homes
        ],
        scratch_shapes=loads + stores + sems + list(scratch),
        input_output_aliases={1: 0} if alias else {},
        compiler_params=pltpu.CompilerParams(vmem_limit_bytes=24 << 20),
        name=kernel.__name__,
    )(
        flags,
        *[
            a if alias and i == 0 else pltpu.with_memory_space_constraint(a, space)
            for i, (a, space) in enumerate(zip(args, spaces))
        ],
    )


def place_of(g, y, z, x, c):
    return (((g * CY + y) * CZ + z) * CX + x) * CC + c


def chips():
    return [
        (y, z, x, c) for y in range(CY) for z in range(CZ) for x in range(CX) for c in range(CC)
    ]


def on_device(state, courant, remesh, shell_dest, shell_row, return_dest, return_row, return_block):
    dev = lax.axis_index(DEV)
    flags = jnp.stack(
        [lax.axis_index("grp"), lax.axis_index("core"), dev, lax.axis_index("z")]
    ).astype(i32)
    field = state.reshape(3, RPB, NZ)
    speed = courant.reshape(RPB, NK)
    sy, sz, line = sines(NY), sines(NZ), line_table()
    syh, syl = halves(sy)
    szp = paired(sz)
    kh, kl = halves(line)
    lamx = eigen(NX).astype(np.float32)[:, None]
    mu = (eigen(NY)[:, None] + eigen(NZ)[None, :]).astype(np.float32)

    blocks = field.reshape(3, NJ, NI, NK)[:, :, NI - NI // 4 :, :].reshape(3, SB, NK)
    across = [(place_of(0, *q), place_of(1, *q)) for q in chips()]
    blocks = lax.ppermute(blocks, ALL, across)

    sd, sr, rd, rr, rb = (
        v.reshape(1, SB) for v in (shell_dest, shell_row, return_dest, return_row, return_block)
    )
    place, codes, merged = call(
        route_kernel,
        [((SLOTS, SB), bf16), ((BRICKS, NZ), f32, "home"), ((2 * NK, 2 * NZ), bf16)],
        flags,
        sd,
        sr,
        rd,
        rb,
        remesh,
        sz.astype(np.float32),
        fetch=True,
    )
    codes = lax.all_to_all(codes.reshape(BRICKS, 1, NZ), DEV, 0, 0, tiled=True)
    landing, cells, gather = call(
        decode_kernel,
        [((1, SLOTS), i32), ((CZ * NJ, SLOTS), bf16, "home"), ((SLOTS, RPB), bf16, "home")],
        flags,
        codes.reshape(BRICKS, NZ),
        rd,
        rr,
        fetch=True,
    )
    turned, th, tl, last, lead = call(
        ready_kernel,
        [
            ((3, RPB, NZ), f32),
            ((BRICKS, NX), bf16, "home"),
            ((BRICKS, NX), bf16, "home"),
            ((896, NK), f32, "home"),
            ((896, NK), f32, "home"),
        ],
        flags,
        field,
        speed,
        szp,
        kh,
        kl,
        fetch=True,
    )
    ahead = [(d, (d + 1) % BRICKS) for d in range(BRICKS)]
    up = lax.ppermute(last, ALL, ahead)
    down = lax.ppermute(lead, ALL, [(b, a) for a, b in ahead])
    advanced, edge, layer = call(
        near_kernel,
        [((3, RPB, NK), f32, "home"), ((3, NJ, 8, NK), f32, "home"), ((3, NJ, NK), f32, "home")],
        flags,
        field,
        speed,
        up,
        down,
        fetch=True,
    )

    (bundle,) = call(bucket_kernel, [((3 * SLOTS, NZ), f32)], flags, blocks, place, merged)
    bundle = lax.all_to_all(bundle.reshape(BRICKS, 3, CAP, NZ), DEV, 0, 0, tiled=True)
    bundle, advanced, gather = lax.optimization_barrier((bundle, advanced, gather))
    planes, outgoing, kept = call(
        forward_kernel,
        [((3, 4, NY, NZ), f32), ((3 * NY, NZ), f32), ((3 * NY, NZ), f32)],
        flags,
        bundle.reshape(3 * SLOTS, NZ),
        landing,
        turned,
        syh,
        syl,
        mu,
    )
    swap = [(0, 1), (1, 0)]
    incoming = lax.ppermute(outgoing, "core", swap)
    (share,) = call(reduce_kernel, [((3 * NY, NZ), f32)], flags, outgoing, incoming, kept, mu)
    share = lax.all_to_all(share.reshape(BRICKS, 3, 2, NZ), DEV, 0, 0, tiled=True)
    (solved,) = call(
        line_kernel,
        [((3 * NY, NZ), f32)],
        flags,
        share.reshape(3 * NY, NZ),
        kh,
        kl,
        th,
        tl,
        lamx,
        mu,
    )
    own = lax.all_to_all(solved.reshape(BRICKS, 3, 2, NZ), DEV, 0, 0, tiled=True)
    own = own.reshape(3 * NY, NZ)
    other = lax.ppermute(own, "core", swap)
    result, send = call(
        inverse_kernel,
        [((3, RPB, NZ), f32), ((TARGETS, 3 * GROUP, NZ), f32)],
        flags,
        advanced,
        planes,
        outgoing,
        incoming,
        own,
        other,
        gather,
        szp,
        syh,
        syl,
        mu,
        raw=True,
        alias=True,
        scratch=[
            pltpu.VMEM((3, RPB, NZ), f32),
            pltpu.VMEM((3, TARGETS, GROUP, NZ), f32),
            pltpu.SemaphoreType.DMA((3,)),
            pltpu.SemaphoreType.DMA((3,)),
        ],
    )
    returned = lax.all_to_all(send, ("y", "x", "core"), 0, 0, tiled=True)
    sums = call(cell_kernel, [((3 * NJ, NZ), f32)] * CZ, flags, returned, cells)
    parts = []
    for k in range(CZ):
        pairs = [
            (place_of(1, y, z, x, c), place_of(0, y, (z + k) % CZ, x, c)) for y, z, x, c in chips()
        ]
        parts.append(lax.ppermute(sums[k], ALL, pairs))
    (result,) = call(
        close_kernel,
        [((3, NJ, NI, NZ), f32)],
        flags,
        result.reshape(3, NJ, NI, NZ),
        edge,
        layer,
        remesh,
        *parts,
        raw=True,
        alias=True,
        scratch=[pltpu.VMEM((3, NJ, 8, NZ), f32), pltpu.SemaphoreType.DMA],
    )
    return result.reshape(1, 3, RPB * NZ)


def solution(mesh):
    fine = Mesh(mesh.devices.reshape(2, CY, CZ, CX, CC), ALL)
    placed = (
        P("grp", None, DEV),
        P(DEV),
        P(),
        P(DEV, None),
        P(DEV),
        P(DEV, None),
        P(DEV),
        P(DEV),
    )
    return jax.shard_map(
        on_device, mesh=fine, in_specs=placed, out_specs=P("grp", None, DEV), check_vma=False
    )
```

```python
import jax
import jax.numpy as jnp
import ml_dtypes
import numpy as np
from jax import lax
from jax.experimental import pallas as pl
from jax.experimental.pallas import tpu as pltpu
from jax.sharding import Mesh
from jax.sharding import PartitionSpec as P

NX, NY, NZ = 512, 256, 128
NI, NK = 64, 128
NJ = 16
CY, CZ, CX, CC = 4, 4, 4, 2
BRICKS = 128
CAP = 4
SB = 256
RPB = 1024
TARGETS = CY * CX * CC
GROUP = CZ * CAP
SLOTS = BRICKS * CAP
CHUNK = 3 * CAP + 1
BACK = 3 * GROUP + 1
DEV = ("y", "z", "x", "core")
ALL = ("grp",) + DEV

viscosity = 0.2
coupling = 1.0
f32 = jnp.float32
bf16 = jnp.bfloat16
i32 = jnp.int32
highest = lax.Precision.HIGHEST
NT = (((1,), (1,)), ((), ()))


def sines(length):
    counts = np.arange(length) + 1
    phase = counts[:, None] * counts[None, :] % (2 * (length + 1))
    return np.sin(np.pi * phase / (length + 1))


def eigen(length):
    counts = np.arange(length) + 1.0
    return 4.0 * np.sin(0.5 * np.pi * counts / (length + 1)) ** 2


def halves(table):
    table = table.astype(np.float32)
    high = table.astype(ml_dtypes.bfloat16)
    low = (table - high.astype(np.float32)).astype(ml_dtypes.bfloat16)
    return high, low


def paired(table):
    high, low = halves(table)
    return np.block([[high, low], [high, np.zeros_like(low)]]).astype(ml_dtypes.bfloat16)


def line_table():
    dev = np.arange(BRICKS)
    plane = np.where(dev % 2 == 1, 4 * dev + 3, 4 * dev - 1) + 1
    phase = (np.arange(NX) + 1)[:, None] * plane[None, :] % (2 * (NX + 1))
    return np.sin(np.pi * phase / (NX + 1))


def iota(shape, axis):
    return lax.broadcasted_iota(i32, shape, axis)


def split(value):
    high = value.astype(bf16)
    return high, (value - high.astype(f32)).astype(bf16)


def mm(a, b):
    return jnp.dot(a, b, preferred_element_type=f32)


def lanes_paired(value):
    return jnp.concatenate(split(value), axis=1)


def fold(value):
    half = value.shape[1] // 2
    return value[:, :half] + value[:, half:]


def pick(onehot, value):
    return fold(mm(onehot, lanes_paired(value)))


def times_paired(value, table):
    return fold(mm(lanes_paired(value), table))


def table_times(high, low, value):
    vh, vl = split(value)
    return mm(high, vh) + mm(high, vl) + mm(low, vh)


def exact(a, b, dims=(((1,), (0,)), ((), ()))):
    return lax.dot_general(a, b, dims, precision=highest, preferred_element_type=f32)


def onehot(condition):
    return jnp.where(condition, 1.0, 0.0).astype(bf16)


def ranks(matches):
    size = matches.shape[1]
    before = onehot(iota((size, size), 0) < iota((size, size), 1))
    counts = mm(matches.astype(bf16), before)
    return jnp.sum(matches * counts, axis=0, keepdims=True).astype(i32)


def owners(owner):
    core = owner & (CC - 1)
    x = (owner >> 1) & (CX - 1)
    z = (owner >> 3) & (CZ - 1)
    lane = z * CAP + ranks(jnp.where(iota((BRICKS, SB), 0) == owner, 1.0, 0.0))
    return owner >> 5, z, x, core, lane


def route_kernel(flags, sd, sr, remesh, sz, place, codes, merged):
    bricks = iota((BRICKS, SB), 0)
    matches = jnp.where(bricks == sd[...], 1.0, 0.0)
    rank = ranks(matches)
    place[...] = onehot(iota((SLOTS, SB), 0) == rank * BRICKS + sd[...])
    tagged = jnp.where(bricks == rank, (sr[...] + 1).astype(f32), 0.0)
    codes[...] = exact(matches, tagged, NT)
    high, low = split(exact(remesh[...], sz[...]))
    merged[...] = jnp.concatenate(
        [
            jnp.concatenate([high, low], axis=1),
            jnp.concatenate([high, jnp.zeros_like(low)], axis=1),
        ],
        axis=0,
    )


def ready_kernel(
    flags, state, speed, sz, kh, kl, rd, rr, rb, out, th, tl, gather, codes, last, lead
):
    @pl.when(flags[0] == 0)
    def _():
        for c in range(3):
            last[c * 256 : (c + 1) * 256, :] = state[c, 768:, :]
            lead[c * 256 : (c + 1) * 256, :] = state[c, :256, :]
        last[768:, :] = speed[896:, :]
        lead[768:, :] = speed[:128, :]

    @pl.when(flags[0] != 0)
    def _():
        for c in range(3):
            out[c] = times_paired(state[c], sz[...])
        th[...] = kh[...].T
        tl[...] = kl[...].T
        y, z, x, core, lane = owners(rd[...])
        target = (y * CX + x) * CC + core
        gather[...] = lax.dot_general(
            onehot(iota((SLOTS, SB), 0) == lane * TARGETS + target),
            onehot(iota((RPB, SB), 0) == rr[...]),
            NT,
            preferred_element_type=f32,
        ).astype(bf16)
        code = ((z - flags[3]) & (CZ - 1)) * NJ + rb[...] + 1
        tagged = jnp.where(iota((NZ, SB), 0) == lane, code.astype(f32), 0.0)
        sent = onehot(iota((TARGETS, SB), 0) == target)
        codes[...] = lax.dot_general(sent, tagged.astype(bf16), NT, preferred_element_type=f32)


def near_step(field, speed):
    rows = speed.shape[0]
    centre = field[128 : 128 + rows]
    transport = (
        8.0 * (field[192 : 192 + rows] - field[64 : 64 + rows])
        - (field[256 : 256 + rows] - field[:rows])
    ) / 12.0
    place = iota((rows, NK), 0) & (NI - 1)
    above = jnp.where(place == NI - 1, 0.0, pltpu.roll(centre, rows - 1, 0))
    below = jnp.where(place == 0, 0.0, pltpu.roll(centre, 1, 0))
    return centre - speed * transport + viscosity * (above - 2.0 * centre + below)


def bucket_kernel(flags, blocks, codes, place, merged, out):
    @pl.when(flags[0] != 0)
    def _():
        out[pl.ds(3 * CAP, BRICKS, stride=CHUNK), :] = codes[...]
        for c in range(3):
            moved = times_paired(blocks[c], merged[...])
            slots = pick(place[...], moved)
            for rank in range(CAP):
                out[pl.ds(c * CAP + rank, BRICKS, stride=CHUNK), :] = slots[
                    rank * BRICKS : (rank + 1) * BRICKS
                ]


def weights(beta):
    outer = beta * beta - 2.0
    g12 = 1.0 / outer
    g13 = g12 / beta
    g11 = (beta * beta - 1.0) * g13
    return g11, g12, g13


def forward_kernel(flags, received, work, syh, syl, mu, planes, outgoing, kept):
    @pl.when(flags[0] != 0)
    def _():
        beta = mu[...] + 2.0
        g11, g12, g13 = weights(beta)
        first = flags[1] == 0
        codes = received[pl.ds(3 * CAP, BRICKS, stride=CHUNK), :].T
        landing = jnp.concatenate([codes[r : r + 1, :] for r in range(CAP)], axis=1).astype(i32)
        spread = onehot(iota((RPB, SLOTS), 0) == landing - 1)
        for c in range(3):
            rows = jnp.concatenate(
                [received[pl.ds(c * CAP + r, BRICKS, stride=CHUNK), :] for r in range(CAP)], axis=0
            )
            field = (pick(spread, rows) + work[c]) * (4.0 / ((NY + 1) * (NZ + 1)))
            field = jnp.concatenate([field[p * NY : (p + 1) * NY] for p in range(4)], axis=1)
            field = table_times(syh[...], syl[...], field)
            f0, f1, f2, f3 = (field[:, p * NZ : (p + 1) * NZ] for p in range(4))
            for p, plane in enumerate((f0, f1, f2, f3)):
                planes[c, p] = plane
            low = g11 * f0 + g12 * f1 + g13 * f2
            high = f3 + g13 * f0 + g12 * f1 + g11 * f2
            outgoing[c * NY : (c + 1) * NY, :] = jnp.where(first, high, low)
            kept[c * NY : (c + 1) * NY, :] = jnp.where(first, low, high)


def reduce_kernel(flags, outgoing, incoming, kept, mu, out):
    @pl.when(flags[0] != 0)
    def _():
        g11, g12, g13 = weights(mu[...] + 2.0)
        ratio = g13 / (mu[...] + 2.0 - 2.0 * g11)
        for c in range(3):
            block = slice(c * NY, (c + 1) * NY)
            share = kept[block, :] + ratio * (outgoing[block, :] + incoming[block, :])
            for i in range(2):
                out[pl.ds(c * 2 + i, BRICKS, stride=6), :] = share[i * BRICKS : (i + 1) * BRICKS]


def line_kernel(flags, received, kh, kl, th, tl, lamx, mu, out):
    @pl.when(flags[0] != 0)
    def _():
        shares = jnp.concatenate([received[pl.ds(j, BRICKS, stride=6), :] for j in range(6)], axis=1)
        modes = table_times(kh[...], kl[...], shares)
        factors = []
        for i in range(2):
            row = mu[pl.ds(flags[2] + i * BRICKS, 1), :]
            factors.append((2.0 / (NX + 1)) / (lamx[...] + row))
        modes = modes * jnp.concatenate(factors * 3, axis=1)
        solved = table_times(th[...], tl[...], modes)
        for j in range(6):
            out[pl.ds(j, BRICKS, stride=6), :] = solved[:, j * NZ : (j + 1) * NZ]


def inverse_kernel(
    flags,
    planes,
    outgoing,
    incoming,
    own,
    other,
    gather,
    codes,
    sz,
    syh,
    syl,
    mu,
    state_home,
    speed_home,
    up_home,
    down_home,
    send,
    out,
    edge_home,
    layer_home,
    held,
    edge,
    layer,
    state,
    speed,
    up,
    down,
    sems,
):
    @pl.when(flags[0] == 0)
    def _():
        pairs = [(state_home, state), (speed_home, speed), (up_home, up), (down_home, down)]
        copies = [pltpu.make_async_copy(a, b, sems.at[i]) for i, (a, b) in enumerate(pairs)]
        for copy in copies:
            copy.start()
        for copy in copies:
            copy.wait()
        wide = jnp.concatenate([up[768:896, :], speed[...], down[768:896, :]], axis=0)
        copies = []
        for c in range(3):
            block = slice(c * 256, (c + 1) * 256)
            field = jnp.concatenate([up[block, :], state[c], down[block, :]], axis=0)
            field = near_step(near_step(field, wide), speed[...])
            held[c] = field
            copies.append(pltpu.make_async_copy(held.at[c], out.at[c], sems.at[c]))
            copies[-1].start()
            edge[c] = field.reshape(NJ, NI, NK)[:, NI - 8 :, :]
            layer[c] = state[c, pl.ds(NI - 1, NJ, stride=NI), :]
        for a, b, i in ((edge, edge_home, 3), (layer, layer_home, 4)):
            copies.append(pltpu.make_async_copy(a, b, sems.at[i]))
            copies[-1].start()
        for copy in copies:
            copy.wait()

    @pl.when(flags[0] != 0)
    def _():
        beta = mu[...] + 2.0
        g11, g12, g13 = weights(beta)
        inv = 1.0 / (beta - 2.0 * g11)
        first = flags[1] == 0
        inside = jnp.where(flags[2] == BRICKS - 1, 0.0, 1.0)
        potentials = []
        for c in range(3):

            def unpacked(ref):
                return jnp.concatenate(
                    [ref[pl.ds(c * 2 + i, BRICKS, stride=6), :] for i in range(2)], axis=0
                )

            block = slice(c * NY, (c + 1) * NY)
            a, b = unpacked(own), unpacked(other)
            before, after = jnp.where(first, a, b), jnp.where(first, b, a)
            middle = (outgoing[block, :] + incoming[block, :] + g13 * (before + after)) * inv
            left = jnp.where(first, before, middle)
            right = jnp.where(first, middle, after)
            f0, f1, f2, f3 = (planes[c, p] for p in range(4))
            u0 = g11 * (f0 + left) + g12 * f1 + g13 * (f2 + right)
            u1 = g12 * (f0 + left + beta * f1 + f2 + right)
            u2 = g13 * (f0 + left) + g12 * f1 + g11 * (f2 + right)
            stack = [u0, u1, u2, right]
            if c:
                stack = [left] + stack + [(beta * right - u2 - f3) * inside]
            field = table_times(syh[...], syl[...], jnp.concatenate(stack, axis=1))
            field = jnp.concatenate(
                [field[:, p * NZ : (p + 1) * NZ] for p in range(len(stack))], axis=0
            )
            potentials.append(times_paired(field, sz[...]))
        rows = iota((RPB, NZ), 0) & (NY - 1)
        lanes = iota((RPB, NZ), 1)

        def dy(field):
            upper = jnp.where(rows == NY - 1, 0.0, pltpu.roll(field, RPB - 1, 0))
            lower = jnp.where(rows == 0, 0.0, pltpu.roll(field, 1, 0))
            return (upper - lower) * 0.5

        def dz(field):
            upper = jnp.where(lanes == NZ - 1, 0.0, pltpu.roll(field, NZ - 1, 1))
            lower = jnp.where(lanes == 0, 0.0, pltpu.roll(field, 1, 1))
            return (upper - lower) * 0.5

        def dx(field):
            return (field[2 * NY : 2 * NY + RPB] - field[:RPB]) * 0.5

        px, py, pz = potentials[0], potentials[1][NY : NY + RPB], potentials[2][NY : NY + RPB]
        velocity = (
            dy(pz) - dz(py),
            dz(px) - dx(potentials[2]),
            dx(potentials[1]) - dy(px),
        )
        copies = []
        for c in range(3):
            held[c] = velocity[c]
            copies.append(pltpu.make_async_copy(held.at[c], out.at[c], sems.at[c]))
            copies[-1].start()
        send[pl.ds(3 * GROUP, TARGETS, stride=BACK), :] = codes[...]
        for c in range(3):
            rows_out = pick(gather[...], velocity[c])
            for lane in range(GROUP):
                send[pl.ds(c * GROUP + lane, TARGETS, stride=BACK), :] = rows_out[
                    lane * TARGETS : (lane + 1) * TARGETS
                ]
        for copy in copies:
            copy.wait()


def cell_kernel(flags, received, *outs):
    @pl.when(flags[0] != 0)
    def _():
        codes = received[pl.ds(3 * GROUP, TARGETS, stride=BACK), :].astype(bf16)
        codes = mm(codes, onehot(iota((NZ, SLOTS), 0) == (iota((NZ, SLOTS), 1) >> 5)))
        mine = iota((TARGETS, SLOTS), 0) == (iota((TARGETS, SLOTS), 1) & (TARGETS - 1))
        code = jnp.sum(jnp.where(mine, codes, 0.0), axis=0, keepdims=True).astype(i32)
        cells = onehot(iota((CZ * NJ, SLOTS), 0) == code - 1)
        for c in range(3):
            rows = jnp.concatenate(
                [
                    received[pl.ds(c * GROUP + lane, TARGETS, stride=BACK), :]
                    for lane in range(GROUP)
                ],
                axis=0,
            )
            sums = pick(cells, rows)
            for k in range(CZ):
                outs[k][c * NJ : (c + 1) * NJ, :] = sums[k * NJ : (k + 1) * NJ]


def close_kernel(flags, field, edge, layer, remesh, b0, b1, b2, b3, out, slab, sem):
    @pl.when(flags[0] == 0)
    def _():
        total = exact((b0[...] + b1[...]) + (b2[...] + b3[...]), remesh[...], NT)
        first = [total[c * NJ : (c + 1) * NJ] for c in range(3)]
        second = [layer[c] for c in range(3)]
        for c in range(3):
            d, e = (c + 1) % 3, (c + 2) % 3
            cross = first[d] * second[e] - first[e] * second[d]
            slab[c] = edge[c]
            slab[c, :, 7, :] = edge[c, :, 7, :] + coupling * cross
        copy = pltpu.make_async_copy(slab, out.at[:, :, pl.ds(NI - 8, 8), :], sem)
        copy.start()
        copy.wait()


def call(kernel, outs, flags, *args, fetch=False, alias=False, far=0, scratch=()):
    args = [jnp.asarray(a) for a in args]
    spaces = [
        pltpu.HBM if fetch or (alias and i == 0) or i >= len(args) - far else pltpu.VMEM
        for i in range(len(args))
    ]
    homes = [len(o) > 2 for o in outs]
    staged = [i for i, o in enumerate(outs) if o[2:] == ("home",)]
    loads = [pltpu.VMEM(a.shape, a.dtype) for a in args] if fetch else []
    stores = [pltpu.VMEM(*outs[i][:2]) for i in staged]
    sems = [pltpu.SemaphoreType.DMA((len(loads) + len(stores),))] if loads or stores else []

    def body(flags, *refs):
        given, made = list(refs[: len(args)]), list(refs[len(args) : len(args) + len(outs)])
        rest = refs[len(args) + len(outs) :]
        held, kept = rest[: len(loads)], rest[len(loads) : len(loads) + len(stores)]
        own = rest[len(loads) + len(stores) + len(sems) :]
        if sems:
            sem = rest[len(loads) + len(stores)]
        copies = [
            pltpu.make_async_copy(a, b, sem.at[i]) for i, (a, b) in enumerate(zip(given, held))
        ]
        for copy in copies:
            copy.start()
        for copy in copies:
            copy.wait()
        homes_out = [made[i] for i in staged]
        for i, ref in zip(staged, kept):
            made[i] = ref
        kernel(flags, *(held if fetch else given), *made, *own)
        copies = [
            pltpu.make_async_copy(a, b, sem.at[len(loads) + i])
            for i, (a, b) in enumerate(zip(kept, homes_out))
        ]
        for copy in copies:
            copy.start()
        for copy in copies:
            copy.wait()

    return pl.pallas_call(
        body,
        out_shape=[(pltpu.HBM if home else pltpu.VMEM)(*o[:2]) for o, home in zip(outs, homes)],
        in_specs=[pl.BlockSpec(memory_space=pltpu.SMEM)]
        + [pl.BlockSpec(memory_space=space) for space in spaces],
        out_specs=[
            pl.BlockSpec(memory_space=pltpu.HBM if home else pltpu.VMEM) for home in homes
        ],
        scratch_shapes=loads + stores + sems + list(scratch),
        input_output_aliases={1: 0} if alias else {},
        compiler_params=pltpu.CompilerParams(vmem_limit_bytes=24 << 20),
        name=kernel.__name__,
    )(
        flags,
        *[
            a if alias and i == 0 else pltpu.with_memory_space_constraint(a, space)
            for i, (a, space) in enumerate(zip(args, spaces))
        ],
    )


def place_of(g, y, z, x, c):
    return (((g * CY + y) * CZ + z) * CX + x) * CC + c


def chips():
    return [
        (y, z, x, c) for y in range(CY) for z in range(CZ) for x in range(CX) for c in range(CC)
    ]


def on_device(state, courant, remesh, shell_dest, shell_row, return_dest, return_row, return_block):
    dev = lax.axis_index(DEV)
    flags = jnp.stack(
        [lax.axis_index("grp"), lax.axis_index("core"), dev, lax.axis_index("z")]
    ).astype(i32)
    field = state.reshape(3, RPB, NZ)
    speed = courant.reshape(RPB, NK)
    sy, sz, line = sines(NY), sines(NZ), line_table()
    syh, syl = halves(sy)
    szp = paired(sz)
    kh, kl = halves(line)
    lamx = eigen(NX).astype(np.float32)[:, None]
    mu = (eigen(NY)[:, None] + eigen(NZ)[None, :]).astype(np.float32)

    blocks = field.reshape(3, NJ, NI, NK)[:, :, NI - NI // 4 :, :].reshape(3, SB, NK)
    across = [(place_of(0, *q), place_of(1, *q)) for q in chips()]
    blocks = lax.ppermute(blocks, ALL, across)

    sd, sr, rd, rr, rb = (
        v.reshape(1, SB) for v in (shell_dest, shell_row, return_dest, return_row, return_block)
    )
    place, codes, merged = call(
        route_kernel,
        [((SLOTS, SB), bf16), ((BRICKS, NZ), f32), ((2 * NK, 2 * NZ), bf16)],
        flags,
        sd,
        sr,
        remesh,
        sz.astype(np.float32),
        fetch=True,
    )
    (bundle,) = call(
        bucket_kernel, [((BRICKS * CHUNK, NZ), f32)], flags, blocks, codes, place, merged
    )
    bundle = lax.all_to_all(bundle.reshape(BRICKS, CHUNK, 1, NZ), DEV, 0, 0, tiled=True)
    turned, th, tl, gather, codes, last, lead = call(
        ready_kernel,
        [
            ((3, RPB, NZ), f32),
            ((BRICKS, NX), bf16, "home"),
            ((BRICKS, NX), bf16, "home"),
            ((SLOTS, RPB), bf16, "home"),
            ((TARGETS, NZ), f32, "home"),
            ((896, NK), f32, "home"),
            ((896, NK), f32, "home"),
        ],
        flags,
        field,
        speed,
        szp,
        kh,
        kl,
        rd,
        rr,
        rb,
        fetch=True,
    )
    ahead = [(d, (d + 1) % BRICKS) for d in range(BRICKS)]
    up = lax.ppermute(last, ALL, ahead)
    down = lax.ppermute(lead, ALL, [(b, a) for a, b in ahead])
    bundle, up, down = lax.optimization_barrier((bundle, up, down))
    planes, outgoing, kept = call(
        forward_kernel,
        [((3, 4, NY, NZ), f32), ((3 * NY, NZ), f32), ((3 * NY, NZ), f32)],
        flags,
        bundle.reshape(BRICKS * CHUNK, NZ),
        turned,
        syh,
        syl,
        mu,
    )
    swap = [(0, 1), (1, 0)]
    incoming = lax.ppermute(outgoing, "core", swap)
    (share,) = call(reduce_kernel, [((3 * NY, NZ), f32)], flags, outgoing, incoming, kept, mu)
    share = lax.all_to_all(share.reshape(BRICKS, 3, 2, NZ), DEV, 0, 0, tiled=True)
    (solved,) = call(
        line_kernel,
        [((3 * NY, NZ), f32)],
        flags,
        share.reshape(3 * NY, NZ),
        kh,
        kl,
        th,
        tl,
        lamx,
        mu,
    )
    own = lax.all_to_all(solved.reshape(BRICKS, 3, 2, NZ), DEV, 0, 0, tiled=True)
    own = own.reshape(3 * NY, NZ)
    other = lax.ppermute(own, "core", swap)
    halo = pltpu.VMEM((896, NK), f32)
    send, result, edge, layer = call(
        inverse_kernel,
        [
            ((TARGETS * BACK, NZ), f32),
            ((3, RPB, NZ), f32, "raw"),
            ((3, NJ, 8, NK), f32, "raw"),
            ((3, NJ, NK), f32, "raw"),
        ],
        flags,
        planes,
        outgoing,
        incoming,
        own,
        other,
        gather,
        codes,
        szp,
        syh,
        syl,
        mu,
        field,
        speed,
        up,
        down,
        far=4,
        scratch=[
            pltpu.VMEM((3, RPB, NZ), f32),
            pltpu.VMEM((3, NJ, 8, NK), f32),
            pltpu.VMEM((3, NJ, NK), f32),
            pltpu.VMEM((3, RPB, NK), f32),
            pltpu.VMEM((RPB, NK), f32),
            halo,
            halo,
            pltpu.SemaphoreType.DMA((5,)),
        ],
    )
    returned = lax.all_to_all(
        send.reshape(TARGETS, BACK, 1, NZ), ("y", "x", "core"), 0, 0, tiled=True
    )
    sums = call(
        cell_kernel, [((3 * NJ, NZ), f32)] * CZ, flags, returned.reshape(TARGETS * BACK, NZ)
    )
    parts = []
    for k in range(CZ):
        pairs = [
            (place_of(1, y, z, x, c), place_of(0, y, (z + k) % CZ, x, c)) for y, z, x, c in chips()
        ]
        parts.append(lax.ppermute(sums[k], ALL, pairs))
    (result,) = call(
        close_kernel,
        [((3, NJ, NI, NZ), f32, "raw")],
        flags,
        result.reshape(3, NJ, NI, NZ),
        edge,
        layer,
        remesh,
        *parts,
        alias=True,
        scratch=[pltpu.VMEM((3, NJ, 8, NZ), f32), pltpu.SemaphoreType.DMA],
    )
    return result.reshape(1, 3, RPB * NZ)


def solution(mesh):
    fine = Mesh(mesh.devices.reshape(2, CY, CZ, CX, CC), ALL)
    placed = (
        P("grp", None, DEV),
        P(DEV),
        P(),
        P(DEV, None),
        P(DEV),
        P(DEV, None),
        P(DEV),
        P(DEV),
    )
    return jax.shard_map(
        on_device, mesh=fine, in_specs=placed, out_specs=P("grp", None, DEV), check_vma=False
    )
```

```python
import jax
import jax.numpy as jnp
import ml_dtypes
import numpy as np
from jax import lax
from jax.experimental import pallas as pl
from jax.experimental.pallas import tpu as pltpu
from jax.sharding import Mesh
from jax.sharding import PartitionSpec as P

NX, NY, NZ = 512, 256, 128
NI, NK = 64, 128
NJ = 16
CY, CZ, CX, CC = 4, 4, 4, 2
BRICKS = 128
CHIPS = 64
HALF = 128
CAP = 4
SB = 256
RPB = 1024
TARGETS = CY * CX * CC
GROUP = CZ * CAP
SLOTS = BRICKS * CAP
CHUNK = 3 * CAP + 1
BACK = 3 * GROUP + 1
DEV = ("y", "z", "x", "core")
ALL = ("grp",) + DEV

viscosity = 0.2
coupling = 1.0
f32 = jnp.float32
bf16 = jnp.bfloat16
i32 = jnp.int32
highest = lax.Precision.HIGHEST
NT = (((1,), (1,)), ((), ()))


def sines(length):
    counts = np.arange(length) + 1
    phase = counts[:, None] * counts[None, :] % (2 * (length + 1))
    return np.sin(np.pi * phase / (length + 1))


def eigen(length):
    counts = np.arange(length) + 1.0
    return 4.0 * np.sin(0.5 * np.pi * counts / (length + 1)) ** 2


def halves(table):
    table = table.astype(np.float32)
    high = table.astype(ml_dtypes.bfloat16)
    low = (table - high.astype(np.float32)).astype(ml_dtypes.bfloat16)
    return high, low


def paired(table):
    high, low = halves(table)
    return np.block([[high, low], [high, np.zeros_like(low)]]).astype(ml_dtypes.bfloat16)


def line_table():
    plane = 8 * (np.arange(CHIPS) + 1)
    phase = (np.arange(NX) + 1)[:, None] * plane[None, :] % (2 * (NX + 1))
    return np.sin(np.pi * phase / (NX + 1))


def iota(shape, axis):
    return lax.broadcasted_iota(i32, shape, axis)


def split(value):
    high = value.astype(bf16)
    return high, (value - high.astype(f32)).astype(bf16)


def mm(a, b):
    return jnp.dot(a, b, preferred_element_type=f32)


def lanes_paired(value):
    return jnp.concatenate(split(value), axis=1)


def fold(value):
    half = value.shape[1] // 2
    return value[:, :half] + value[:, half:]


def pick(onehot, value):
    return fold(mm(onehot, lanes_paired(value)))


def times_paired(value, table):
    return fold(mm(lanes_paired(value), table))


def table_times(high, low, value):
    vh, vl = split(value)
    return mm(high, vh) + mm(high, vl) + mm(low, vh)


def exact(a, b, dims=(((1,), (0,)), ((), ()))):
    return lax.dot_general(a, b, dims, precision=highest, preferred_element_type=f32)


def onehot(condition):
    return jnp.where(condition, 1.0, 0.0).astype(bf16)


def ranks(matches):
    size = matches.shape[1]
    before = onehot(iota((size, size), 0) < iota((size, size), 1))
    counts = mm(matches.astype(bf16), before)
    return jnp.sum(matches * counts, axis=0, keepdims=True).astype(i32)


def owners(owner):
    core = owner & (CC - 1)
    x = (owner >> 1) & (CX - 1)
    z = (owner >> 3) & (CZ - 1)
    lane = z * CAP + ranks(jnp.where(iota((BRICKS, SB), 0) == owner, 1.0, 0.0))
    return owner >> 5, z, x, core, lane


def route_kernel(flags, sd, sr, remesh, sz, place, codes, merged):
    bricks = iota((BRICKS, SB), 0)
    matches = jnp.where(bricks == sd[...], 1.0, 0.0)
    rank = ranks(matches)
    place[...] = onehot(iota((SLOTS, SB), 0) == rank * BRICKS + sd[...])
    tagged = jnp.where(bricks == rank, (sr[...] + 1).astype(f32), 0.0)
    codes[...] = exact(matches, tagged, NT)
    high, low = split(exact(remesh[...], sz[...]))
    merged[...] = jnp.concatenate(
        [
            jnp.concatenate([high, low], axis=1),
            jnp.concatenate([high, jnp.zeros_like(low)], axis=1),
        ],
        axis=0,
    )


def ready_kernel(
    flags, state, speed, sz, rd, rr, rb, out, gather, codes, last, lead
):
    @pl.when(flags[0] == 0)
    def _():
        for c in range(3):
            last[c * 256 : (c + 1) * 256, :] = state[c, 768:, :]
            lead[c * 256 : (c + 1) * 256, :] = state[c, :256, :]
        last[768:, :] = speed[896:, :]
        lead[768:, :] = speed[:128, :]

    @pl.when(flags[0] != 0)
    def _():
        for c in range(3):
            out[c] = times_paired(state[c], sz[...])
        y, z, x, core, lane = owners(rd[...])
        target = (y * CX + x) * CC + core
        gather[...] = lax.dot_general(
            onehot(iota((SLOTS, SB), 0) == lane * TARGETS + target),
            onehot(iota((RPB, SB), 0) == rr[...]),
            NT,
            preferred_element_type=f32,
        ).astype(bf16)
        code = z * NJ + rb[...] + 1
        tagged = jnp.where(iota((NZ, SB), 0) == lane, code.astype(f32), 0.0)
        sent = onehot(iota((TARGETS, SB), 0) == target)
        codes[...] = lax.dot_general(sent, tagged.astype(bf16), NT, preferred_element_type=f32)


def near_step(field, speed):
    rows = speed.shape[0]
    centre = field[128 : 128 + rows]
    transport = (
        8.0 * (field[192 : 192 + rows] - field[64 : 64 + rows])
        - (field[256 : 256 + rows] - field[:rows])
    ) / 12.0
    place = iota((rows, NK), 0) & (NI - 1)
    above = jnp.where(place == NI - 1, 0.0, pltpu.roll(centre, rows - 1, 0))
    below = jnp.where(place == 0, 0.0, pltpu.roll(centre, 1, 0))
    return centre - speed * transport + viscosity * (above - 2.0 * centre + below)


def shell_kernel(group, state, out, sem):
    @pl.when(group[0] == 0)
    def _():
        copy = pltpu.make_async_copy(state.at[:, :, pl.ds(NI - NI // 4, NI // 4), :], out, sem)
        copy.start()
        copy.wait()


def bucket_kernel(flags, blocks, codes, place, merged, out):
    @pl.when(flags[0] != 0)
    def _():
        out[pl.ds(3 * CAP, BRICKS, stride=CHUNK), :] = codes[...]
        for c in range(3):
            moved = times_paired(blocks[c], merged[...])
            slots = pick(place[...], moved)
            for rank in range(CAP):
                out[pl.ds(c * CAP + rank, BRICKS, stride=CHUNK), :] = slots[
                    rank * BRICKS : (rank + 1) * BRICKS
                ]


def weights(beta):
    outer = beta * beta - 2.0
    g12 = 1.0 / outer
    g13 = g12 / beta
    g11 = (beta * beta - 1.0) * g13
    return g11, g12, g13


def forward_kernel(flags, received, work, syh, syl, mu, planes, outgoing, kept):
    @pl.when(flags[0] != 0)
    def _():
        beta = mu[...] + 2.0
        g11, g12, g13 = weights(beta)
        first = flags[1] == 0
        codes = received[pl.ds(3 * CAP, BRICKS, stride=CHUNK), :].T
        landing = jnp.concatenate([codes[r : r + 1, :] for r in range(CAP)], axis=1).astype(i32)
        spread = onehot(iota((RPB, SLOTS), 0) == landing - 1)
        for c in range(3):
            rows = jnp.concatenate(
                [received[pl.ds(c * CAP + r, BRICKS, stride=CHUNK), :] for r in range(CAP)], axis=0
            )
            field = (pick(spread, rows) + work[c]) * (4.0 / ((NY + 1) * (NZ + 1)))
            field = jnp.concatenate([field[p * NY : (p + 1) * NY] for p in range(4)], axis=1)
            field = table_times(syh[...], syl[...], field)
            f0, f1, f2, f3 = (field[:, p * NZ : (p + 1) * NZ] for p in range(4))
            for p, plane in enumerate((f0, f1, f2, f3)):
                planes[c, p] = plane
            low = g11 * f0 + g12 * f1 + g13 * f2
            high = f3 + g13 * f0 + g12 * f1 + g11 * f2
            for kind, value in enumerate((low, high)):
                block = slice((kind * 3 + c) * HALF, (kind * 3 + c + 1) * HALF)
                outgoing[block, :] = jnp.where(first, value[HALF:], value[:HALF])
                kept[block, :] = jnp.where(first, value[:HALF], value[HALF:])


def reduce_kernel(flags, incoming, kept, mu, out, joint):
    @pl.when(flags[0] != 0)
    def _():
        beta = mu[pl.ds(pl.multiple_of(flags[1] * HALF, HALF), HALF), :] + 2.0
        g11, g12, g13 = weights(beta)
        ratio = g13 / (beta - 2.0 * g11)
        first = flags[1] == 0
        for c in range(3):
            low, high = (slice((k * 3 + c) * HALF, (k * 3 + c + 1) * HALF) for k in range(2))
            low0, low1 = (
                jnp.where(first, kept[low, :], incoming[low, :]),
                jnp.where(first, incoming[low, :], kept[low, :]),
            )
            high0, high1 = (
                jnp.where(first, kept[high, :], incoming[high, :]),
                jnp.where(first, incoming[high, :], kept[high, :]),
            )
            middle = high0 + low1
            joint[c * HALF : (c + 1) * HALF, :] = middle
            for kind, value in enumerate((low0 + ratio * middle, high1 + ratio * middle)):
                for i in range(2):
                    out[pl.ds(c * 4 + kind * 2 + i, CHIPS, stride=12), :] = value[
                        i * CHIPS : (i + 1) * CHIPS
                    ]


def line_kernel(flags, received, spread, th, tl, lamx, mu, out):
    @pl.when(flags[0] != 0)
    def _():
        def part(c, kind, i):
            return received[pl.ds(c * 4 + kind * 2 + i, CHIPS, stride=12), :]

        place = iota((CHIPS, NZ), 0)
        rows = []
        for c in range(3):
            for i in range(2):
                ahead = jnp.where(
                    place == CHIPS - 1, 0.0, pltpu.roll(part(c, 0, i), CHIPS - 1, 0)
                )
                rows.append(part(c, 1, i) + ahead)
        high, low = split(jnp.concatenate(rows, axis=1))
        modes = mm(spread[...], jnp.concatenate([high, low, high], axis=0))
        factors = []
        for i in range(2):
            row = mu[pl.ds(flags[1] * HALF + i * CHIPS + (flags[2] >> 1), 1), :]
            factors.append((2.0 / (NX + 1)) / (lamx[...] + row))
        modes = modes * jnp.concatenate(factors * 3, axis=1)
        solved = table_times(th[...], tl[...], modes)
        for c in range(3):
            for i in range(2):
                j = c * 2 + i
                value = solved[:, j * NZ : (j + 1) * NZ]
                behind = jnp.where(place == 0, 0.0, pltpu.roll(value, 1, 0))
                out[pl.ds(c * 4 + i, CHIPS, stride=12), :] = behind
                out[pl.ds(c * 4 + 2 + i, CHIPS, stride=12), :] = value


def inverse_kernel(
    flags,
    planes,
    joint,
    joined,
    own,
    other,
    gather,
    codes,
    sz,
    syh,
    syl,
    mu,
    state_home,
    speed_home,
    up_home,
    down_home,
    send,
    out,
    edge_home,
    layer_home,
    held,
    edge,
    layer,
    state,
    speed,
    up,
    down,
    sems,
):
    @pl.when(flags[0] == 0)
    def _():
        pairs = [(state_home, state), (speed_home, speed), (up_home, up), (down_home, down)]
        copies = [pltpu.make_async_copy(a, b, sems.at[i]) for i, (a, b) in enumerate(pairs)]
        for copy in copies:
            copy.start()
        for copy in copies:
            copy.wait()
        wide = jnp.concatenate([up[768:896, :], speed[...], down[768:896, :]], axis=0)
        copies = []
        for c in range(3):
            block = slice(c * 256, (c + 1) * 256)
            field = jnp.concatenate([up[block, :], state[c], down[block, :]], axis=0)
            field = near_step(near_step(field, wide), speed[...])
            held[c] = field
            copies.append(pltpu.make_async_copy(held.at[c], out.at[c], sems.at[c]))
            copies[-1].start()
            edge[c] = field.reshape(NJ, NI, NK)[:, NI - 8 :, :]
            layer[c] = state[c, pl.ds(NI - 1, NJ, stride=NI), :]
        for a, b, i in ((edge, edge_home, 3), (layer, layer_home, 4)):
            copies.append(pltpu.make_async_copy(a, b, sems.at[i]))
            copies[-1].start()
        for copy in copies:
            copy.wait()

    @pl.when(flags[0] != 0)
    def _():
        beta = mu[...] + 2.0
        g11, g12, g13 = weights(beta)
        inv = 1.0 / (beta - 2.0 * g11)
        first = flags[1] == 0
        inside = jnp.where(flags[2] == BRICKS - 1, 0.0, 1.0)
        potentials = []
        for c in range(3):

            def full(pieces):
                a, b = pieces(own, joint), pieces(other, joined)
                return jnp.concatenate([jnp.where(first, a, b), jnp.where(first, b, a)], axis=0)

            def solved(kind):
                return full(
                    lambda ref, _: jnp.concatenate(
                        [
                            ref[pl.ds(c * 4 + kind * 2 + i, CHIPS, stride=12), :]
                            for i in range(2)
                        ],
                        axis=0,
                    )
                )

            before, after = solved(0), solved(1)
            middle = full(lambda _, ref: ref[c * HALF : (c + 1) * HALF, :])
            middle = (middle + g13 * (before + after)) * inv
            left = jnp.where(first, before, middle)
            right = jnp.where(first, middle, after)
            f0, f1, f2, f3 = (planes[c, p] for p in range(4))
            u0 = g11 * (f0 + left) + g12 * f1 + g13 * (f2 + right)
            u1 = g12 * (f0 + left + beta * f1 + f2 + right)
            u2 = g13 * (f0 + left) + g12 * f1 + g11 * (f2 + right)
            stack = [u0, u1, u2, right]
            if c:
                stack = [left] + stack + [(beta * right - u2 - f3) * inside]
            field = table_times(syh[...], syl[...], jnp.concatenate(stack, axis=1))
            field = jnp.concatenate(
                [field[:, p * NZ : (p + 1) * NZ] for p in range(len(stack))], axis=0
            )
            potentials.append(times_paired(field, sz[...]))
        rows = iota((RPB, NZ), 0) & (NY - 1)
        lanes = iota((RPB, NZ), 1)

        def dy(field):
            upper = jnp.where(rows == NY - 1, 0.0, pltpu.roll(field, RPB - 1, 0))
            lower = jnp.where(rows == 0, 0.0, pltpu.roll(field, 1, 0))
            return (upper - lower) * 0.5

        def dz(field):
            upper = jnp.where(lanes == NZ - 1, 0.0, pltpu.roll(field, NZ - 1, 1))
            lower = jnp.where(lanes == 0, 0.0, pltpu.roll(field, 1, 1))
            return (upper - lower) * 0.5

        def dx(field):
            return (field[2 * NY : 2 * NY + RPB] - field[:RPB]) * 0.5

        px, py, pz = potentials[0], potentials[1][NY : NY + RPB], potentials[2][NY : NY + RPB]
        velocity = (
            dy(pz) - dz(py),
            dz(px) - dx(potentials[2]),
            dx(potentials[1]) - dy(px),
        )
        copies = []
        for c in range(3):
            held[c] = velocity[c]
            copies.append(pltpu.make_async_copy(held.at[c], out.at[c], sems.at[c]))
            copies[-1].start()
        send[pl.ds(3 * GROUP, TARGETS, stride=BACK), :] = codes[...]
        for c in range(3):
            rows_out = pick(gather[...], velocity[c])
            for lane in range(GROUP):
                send[pl.ds(c * GROUP + lane, TARGETS, stride=BACK), :] = rows_out[
                    lane * TARGETS : (lane + 1) * TARGETS
                ]
        for copy in copies:
            copy.wait()


def cell_kernel(flags, received, out):
    @pl.when(flags[0] != 0)
    def _():
        codes = received[pl.ds(3 * GROUP, TARGETS, stride=BACK), :].astype(bf16)
        codes = mm(codes, onehot(iota((NZ, SLOTS), 0) == (iota((NZ, SLOTS), 1) >> 5)))
        mine = iota((TARGETS, SLOTS), 0) == (iota((TARGETS, SLOTS), 1) & (TARGETS - 1))
        code = jnp.sum(jnp.where(mine, codes, 0.0), axis=0, keepdims=True).astype(i32)
        cells = onehot(iota((CZ * NJ, SLOTS), 0) == code - 1)
        for c in range(3):
            rows = jnp.concatenate(
                [
                    received[pl.ds(c * GROUP + lane, TARGETS, stride=BACK), :]
                    for lane in range(GROUP)
                ],
                axis=0,
            )
            sums = pick(cells, rows)
            for k in range(CZ):
                out[k, c * NJ : (c + 1) * NJ, :] = sums[k * NJ : (k + 1) * NJ]


def close_kernel(flags, field, edge, layer, remesh, sums, out, slab, sem):
    @pl.when(flags[0] == 0)
    def _():
        total = exact((sums[4] + sums[5]) + (sums[6] + sums[7]), remesh[...], NT)
        first = [total[c * NJ : (c + 1) * NJ] for c in range(3)]
        second = [layer[c] for c in range(3)]
        for c in range(3):
            d, e = (c + 1) % 3, (c + 2) % 3
            cross = first[d] * second[e] - first[e] * second[d]
            slab[c] = edge[c]
            slab[c, :, 7, :] = edge[c, :, 7, :] + coupling * cross
        copy = pltpu.make_async_copy(slab, out.at[:, :, pl.ds(NI - 8, 8), :], sem)
        copy.start()
        copy.wait()


def call(kernel, outs, flags, *args, fetch=False, alias=False, far=0, scratch=()):
    args = [jnp.asarray(a) for a in args]
    spaces = [
        pltpu.HBM if fetch or (alias and i == 0) or i >= len(args) - far else pltpu.VMEM
        for i in range(len(args))
    ]
    homes = [len(o) > 2 for o in outs]
    staged = [i for i, o in enumerate(outs) if o[2:] == ("home",)]
    loads = [pltpu.VMEM(a.shape, a.dtype) for a in args] if fetch else []
    stores = [pltpu.VMEM(*outs[i][:2]) for i in staged]
    sems = [pltpu.SemaphoreType.DMA((len(loads) + len(stores),))] if loads or stores else []

    def body(flags, *refs):
        given, made = list(refs[: len(args)]), list(refs[len(args) : len(args) + len(outs)])
        rest = refs[len(args) + len(outs) :]
        held, kept = rest[: len(loads)], rest[len(loads) : len(loads) + len(stores)]
        own = rest[len(loads) + len(stores) + len(sems) :]
        if sems:
            sem = rest[len(loads) + len(stores)]
        copies = [
            pltpu.make_async_copy(a, b, sem.at[i]) for i, (a, b) in enumerate(zip(given, held))
        ]
        for copy in copies:
            copy.start()
        for copy in copies:
            copy.wait()
        homes_out = [made[i] for i in staged]
        for i, ref in zip(staged, kept):
            made[i] = ref
        kernel(flags, *(held if fetch else given), *made, *own)
        copies = [
            pltpu.make_async_copy(a, b, sem.at[len(loads) + i])
            for i, (a, b) in enumerate(zip(kept, homes_out))
        ]
        for copy in copies:
            copy.start()
        for copy in copies:
            copy.wait()

    return pl.pallas_call(
        body,
        out_shape=[(pltpu.HBM if home else pltpu.VMEM)(*o[:2]) for o, home in zip(outs, homes)],
        in_specs=[pl.BlockSpec(memory_space=pltpu.SMEM)]
        + [pl.BlockSpec(memory_space=space) for space in spaces],
        out_specs=[
            pl.BlockSpec(memory_space=pltpu.HBM if home else pltpu.VMEM) for home in homes
        ],
        scratch_shapes=loads + stores + sems + list(scratch),
        input_output_aliases={1: 0} if alias else {},
        compiler_params=pltpu.CompilerParams(vmem_limit_bytes=24 << 20),
        name=kernel.__name__,
    )(
        flags,
        *[
            a if alias and i == 0 else pltpu.with_memory_space_constraint(a, space)
            for i, (a, space) in enumerate(zip(args, spaces))
        ],
    )


def place_of(g, y, z, x, c):
    return (((g * CY + y) * CZ + z) * CX + x) * CC + c


def chips():
    return [
        (y, z, x, c) for y in range(CY) for z in range(CZ) for x in range(CX) for c in range(CC)
    ]


def on_device(state, courant, remesh, shell_dest, shell_row, return_dest, return_row, return_block):
    dev = lax.axis_index(DEV)
    flags = jnp.stack(
        [lax.axis_index("grp"), lax.axis_index("core"), dev, lax.axis_index("z")]
    ).astype(i32)
    field = state.reshape(3, RPB, NZ)
    speed = courant.reshape(RPB, NK)
    sy, sz, line = sines(NY), sines(NZ), line_table()
    syh, syl = halves(sy)
    szp = paired(sz)
    kh, kl = halves(line)
    triple = np.concatenate([kh, kh, kl], axis=1)
    th, tl = np.ascontiguousarray(kh.T), np.ascontiguousarray(kl.T)
    lamx = eigen(NX).astype(np.float32)[:, None]
    mu = (eigen(NY)[:, None] + eigen(NZ)[None, :]).astype(np.float32)

    group = lax.axis_index("grp").astype(i32).reshape(1)
    (blocks,) = call(
        shell_kernel,
        [((3, NJ, NI // 4, NK), f32)],
        group,
        field.reshape(3, NJ, NI, NK),
        far=1,
        scratch=[pltpu.SemaphoreType.DMA],
    )
    across = [(place_of(0, *q), place_of(1, *q)) for q in chips()]
    blocks = lax.ppermute(blocks.reshape(3, SB, NK), ALL, across)

    sd, sr, rd, rr, rb = (
        v.reshape(1, SB) for v in (shell_dest, shell_row, return_dest, return_row, return_block)
    )
    place, codes, merged = call(
        route_kernel,
        [((SLOTS, SB), bf16), ((BRICKS, NZ), f32), ((2 * NK, 2 * NZ), bf16)],
        flags,
        sd,
        sr,
        remesh,
        sz.astype(np.float32),
        fetch=True,
    )
    (bundle,) = call(
        bucket_kernel, [((BRICKS * CHUNK, NZ), f32)], flags, blocks, codes, place, merged
    )
    bundle = lax.all_to_all(bundle.reshape(BRICKS, CHUNK, 1, NZ), DEV, 0, 0, tiled=True)
    turned, gather, codes, last, lead = call(
        ready_kernel,
        [
            ((3, RPB, NZ), f32),
            ((SLOTS, RPB), bf16, "home"),
            ((TARGETS, NZ), f32, "home"),
            ((896, NK), f32, "home"),
            ((896, NK), f32, "home"),
        ],
        flags,
        field,
        speed,
        szp,
        rd,
        rr,
        rb,
        fetch=True,
    )
    ahead = [(d, (d + 1) % BRICKS) for d in range(BRICKS)]
    up = lax.ppermute(last, ALL, ahead)
    down = lax.ppermute(lead, ALL, [(b, a) for a, b in ahead])
    bundle, up, down = lax.optimization_barrier((bundle, up, down))
    planes, outgoing, kept = call(
        forward_kernel,
        [((3, 4, NY, NZ), f32), ((3 * NY, NZ), f32), ((3 * NY, NZ), f32)],
        flags,
        bundle.reshape(BRICKS * CHUNK, NZ),
        turned,
        syh,
        syl,
        mu,
    )
    swap = [(0, 1), (1, 0)]
    same = ("y", "z", "x")
    incoming = lax.ppermute(outgoing, "core", swap)
    share, joint = call(
        reduce_kernel,
        [((CHIPS * 12, NZ), f32), ((3 * HALF, NZ), f32)],
        flags,
        incoming,
        kept,
        mu,
    )
    joined = lax.ppermute(joint, "core", swap)
    share = lax.all_to_all(share.reshape(CHIPS, 3, 4, NZ), same, 0, 0, tiled=True)
    share, joined = lax.optimization_barrier((share, joined))
    (solved,) = call(
        line_kernel,
        [((CHIPS * 12, NZ), f32)],
        flags,
        share.reshape(CHIPS * 12, NZ),
        triple,
        th,
        tl,
        lamx,
        mu,
    )
    own = lax.all_to_all(solved.reshape(CHIPS, 3, 4, NZ), same, 0, 0, tiled=True)
    own = own.reshape(CHIPS * 12, NZ)
    other = lax.ppermute(own, "core", swap)
    halo = pltpu.VMEM((896, NK), f32)
    send, result, edge, layer = call(
        inverse_kernel,
        [
            ((TARGETS * BACK, NZ), f32),
            ((3, RPB, NZ), f32, "raw"),
            ((3, NJ, 8, NK), f32, "raw"),
            ((3, NJ, NK), f32, "raw"),
        ],
        flags,
        planes,
        joint,
        joined,
        own,
        other,
        gather,
        codes,
        szp,
        syh,
        syl,
        mu,
        field,
        speed,
        up,
        down,
        far=4,
        scratch=[
            pltpu.VMEM((3, RPB, NZ), f32),
            pltpu.VMEM((3, NJ, 8, NK), f32),
            pltpu.VMEM((3, NJ, NK), f32),
            pltpu.VMEM((3, RPB, NK), f32),
            pltpu.VMEM((RPB, NK), f32),
            halo,
            halo,
            pltpu.SemaphoreType.DMA((5,)),
        ],
    )
    returned = lax.all_to_all(
        send.reshape(TARGETS, BACK, 1, NZ), ("y", "x", "core"), 0, 0, tiled=True
    )
    (sums,) = call(
        cell_kernel, [((2 * CZ, 3 * NJ, NZ), f32)], flags, returned.reshape(TARGETS * BACK, NZ)
    )
    sums = lax.all_to_all(sums, ("grp", "z"), 0, 0, tiled=True)
    (result,) = call(
        close_kernel,
        [((3, NJ, NI, NZ), f32, "raw")],
        flags,
        result.reshape(3, NJ, NI, NZ),
        edge,
        layer,
        remesh,
        sums,
        alias=True,
        scratch=[pltpu.VMEM((3, NJ, 8, NZ), f32), pltpu.SemaphoreType.DMA],
    )
    return result.reshape(1, 3, RPB * NZ)


def solution(mesh):
    fine = Mesh(mesh.devices.reshape(2, CY, CZ, CX, CC), ALL)
    placed = (
        P("grp", None, DEV),
        P(DEV),
        P(),
        P(DEV, None),
        P(DEV),
        P(DEV, None),
        P(DEV),
        P(DEV),
    )
    return jax.shard_map(
        on_device, mesh=fine, in_specs=placed, out_specs=P("grp", None, DEV), check_vma=False
    )
```

```python
import jax
import jax.numpy as jnp
import ml_dtypes
import numpy as np
from jax import lax
from jax.experimental import pallas as pl
from jax.experimental.pallas import tpu as pltpu
from jax.sharding import Mesh
from jax.sharding import PartitionSpec as P

NX, NY, NZ = 512, 256, 128
NI, NK = 64, 128
NJ = 16
CY, CZ, CX, CC = 4, 4, 4, 2
BRICKS = 128
CHIPS = 64
HALF = 128
CAP = 4
SB = 256
RPB = 1024
TARGETS = CY * CX * CC
GROUP = CZ * CAP
SLOTS = BRICKS * CAP
CHUNK = 3 * CAP + 1
BACK = 3 * GROUP + 1
DEV = ("y", "z", "x", "core")
ALL = ("grp",) + DEV

viscosity = 0.2
coupling = 1.0
f32 = jnp.float32
bf16 = jnp.bfloat16
i32 = jnp.int32
highest = lax.Precision.HIGHEST
NT = (((1,), (1,)), ((), ()))


def sines(length):
    counts = np.arange(length) + 1
    phase = counts[:, None] * counts[None, :] % (2 * (length + 1))
    return np.sin(np.pi * phase / (length + 1))


def eigen(length):
    counts = np.arange(length) + 1.0
    return 4.0 * np.sin(0.5 * np.pi * counts / (length + 1)) ** 2


def halves(table):
    table = table.astype(np.float32)
    high = table.astype(ml_dtypes.bfloat16)
    low = (table - high.astype(np.float32)).astype(ml_dtypes.bfloat16)
    return high, low


def paired(table):
    high, low = halves(table)
    return np.block([[high, low], [high, np.zeros_like(low)]]).astype(ml_dtypes.bfloat16)


def line_table():
    plane = 8 * (np.arange(CHIPS) + 1)
    phase = (np.arange(NX) + 1)[:, None] * plane[None, :] % (2 * (NX + 1))
    return np.sin(np.pi * phase / (NX + 1))


def iota(shape, axis):
    return lax.broadcasted_iota(i32, shape, axis)


def split(value):
    high = value.astype(bf16)
    return high, (value - high.astype(f32)).astype(bf16)


def mm(a, b):
    return jnp.dot(a, b, preferred_element_type=f32)


def lanes_paired(value):
    return jnp.concatenate(split(value), axis=1)


def fold(value):
    half = value.shape[1] // 2
    return value[:, :half] + value[:, half:]


def pick(onehot, value):
    return fold(mm(onehot, lanes_paired(value)))


def times_paired(value, table):
    return fold(mm(lanes_paired(value), table))


def table_times(high, low, value):
    vh, vl = split(value)
    return mm(high, vh) + mm(high, vl) + mm(low, vh)


def exact(a, b, dims=(((1,), (0,)), ((), ()))):
    return lax.dot_general(a, b, dims, precision=highest, preferred_element_type=f32)


def onehot(condition):
    return jnp.where(condition, 1.0, 0.0).astype(bf16)


def ranks(matches):
    size = matches.shape[1]
    before = onehot(iota((size, size), 0) < iota((size, size), 1))
    counts = mm(matches.astype(bf16), before)
    return jnp.sum(matches * counts, axis=0, keepdims=True).astype(i32)


def owners(owner):
    core = owner & (CC - 1)
    x = (owner >> 1) & (CX - 1)
    z = (owner >> 3) & (CZ - 1)
    lane = z * CAP + ranks(jnp.where(iota((BRICKS, SB), 0) == owner, 1.0, 0.0))
    return owner >> 5, z, x, core, lane


def route_kernel(flags, sd, sr, remesh, sz, place, codes, merged):
    bricks = iota((BRICKS, SB), 0)
    matches = jnp.where(bricks == sd[...], 1.0, 0.0)
    rank = ranks(matches)
    place[...] = onehot(iota((SLOTS, SB), 0) == rank * BRICKS + sd[...])
    tagged = jnp.where(bricks == rank, (sr[...] + 1).astype(f32), 0.0)
    codes[...] = exact(matches, tagged, NT)
    high, low = split(exact(remesh[...], sz[...]))
    merged[...] = jnp.concatenate(
        [
            jnp.concatenate([high, low], axis=1),
            jnp.concatenate([high, jnp.zeros_like(low)], axis=1),
        ],
        axis=0,
    )


def ready_kernel(
    flags, state, speed, sz, rd, rr, rb, out, gather, codes, last, lead
):
    @pl.when(flags[0] == 0)
    def _():
        for c in range(3):
            last[c * 256 : (c + 1) * 256, :] = state[c, 768:, :]
            lead[c * 256 : (c + 1) * 256, :] = state[c, :256, :]
        last[768:, :] = speed[896:, :]
        lead[768:, :] = speed[:128, :]

    @pl.when(flags[0] != 0)
    def _():
        for c in range(3):
            out[c] = times_paired(state[c], sz[...])
        y, z, x, core, lane = owners(rd[...])
        target = (y * CX + x) * CC + core
        gather[...] = lax.dot_general(
            onehot(iota((SLOTS, SB), 0) == lane * TARGETS + target),
            onehot(iota((RPB, SB), 0) == rr[...]),
            NT,
            preferred_element_type=f32,
        ).astype(bf16)
        code = ((z - flags[3]) & (CZ - 1)) * NJ + rb[...] + 1
        tagged = jnp.where(iota((NZ, SB), 0) == lane, code.astype(f32), 0.0)
        sent = onehot(iota((TARGETS, SB), 0) == target)
        codes[...] = lax.dot_general(sent, tagged.astype(bf16), NT, preferred_element_type=f32)


def near_step(field, speed):
    rows = speed.shape[0]
    centre = field[128 : 128 + rows]
    transport = (
        8.0 * (field[192 : 192 + rows] - field[64 : 64 + rows])
        - (field[256 : 256 + rows] - field[:rows])
    ) / 12.0
    place = iota((rows, NK), 0) & (NI - 1)
    above = jnp.where(place == NI - 1, 0.0, pltpu.roll(centre, rows - 1, 0))
    below = jnp.where(place == 0, 0.0, pltpu.roll(centre, 1, 0))
    return centre - speed * transport + viscosity * (above - 2.0 * centre + below)


def shell_kernel(group, state, out, sem):
    @pl.when(group[0] == 0)
    def _():
        copy = pltpu.make_async_copy(state.at[:, :, pl.ds(NI - NI // 4, NI // 4), :], out, sem)
        copy.start()
        copy.wait()


def bucket_kernel(flags, blocks, codes, place, merged, out):
    @pl.when(flags[0] != 0)
    def _():
        out[pl.ds(3 * CAP, BRICKS, stride=CHUNK), :] = codes[...]
        for c in range(3):
            moved = times_paired(blocks[c], merged[...])
            slots = pick(place[...], moved)
            for rank in range(CAP):
                out[pl.ds(c * CAP + rank, BRICKS, stride=CHUNK), :] = slots[
                    rank * BRICKS : (rank + 1) * BRICKS
                ]


def weights(beta):
    outer = beta * beta - 2.0
    g12 = 1.0 / outer
    g13 = g12 / beta
    g11 = (beta * beta - 1.0) * g13
    return g11, g12, g13


def forward_kernel(flags, received, work, syh, syl, mu, planes, outgoing, kept):
    @pl.when(flags[0] != 0)
    def _():
        beta = mu[...] + 2.0
        g11, g12, g13 = weights(beta)
        first = flags[1] == 0
        codes = received[pl.ds(3 * CAP, BRICKS, stride=CHUNK), :].T
        landing = jnp.concatenate([codes[r : r + 1, :] for r in range(CAP)], axis=1).astype(i32)
        spread = onehot(iota((RPB, SLOTS), 0) == landing - 1)
        for c in range(3):
            rows = jnp.concatenate(
                [received[pl.ds(c * CAP + r, BRICKS, stride=CHUNK), :] for r in range(CAP)], axis=0
            )
            field = (pick(spread, rows) + work[c]) * (4.0 / ((NY + 1) * (NZ + 1)))
            field = jnp.concatenate([field[p * NY : (p + 1) * NY] for p in range(4)], axis=1)
            field = table_times(syh[...], syl[...], field)
            f0, f1, f2, f3 = (field[:, p * NZ : (p + 1) * NZ] for p in range(4))
            for p, plane in enumerate((f0, f1, f2, f3)):
                planes[c, p] = plane
            low = g11 * f0 + g12 * f1 + g13 * f2
            high = f3 + g13 * f0 + g12 * f1 + g11 * f2
            for kind, value in enumerate((low, high)):
                block = slice((kind * 3 + c) * HALF, (kind * 3 + c + 1) * HALF)
                outgoing[block, :] = jnp.where(first, value[HALF:], value[:HALF])
                kept[block, :] = jnp.where(first, value[:HALF], value[HALF:])


def reduce_kernel(flags, incoming, kept, mu, out, joint):
    @pl.when(flags[0] != 0)
    def _():
        beta = mu[pl.ds(pl.multiple_of(flags[1] * HALF, HALF), HALF), :] + 2.0
        g11, _, g13 = weights(beta)
        ratio = g13 / (beta - 2.0 * g11)
        first = flags[1] == 0
        for c in range(3):
            low, high = (slice((k * 3 + c) * HALF, (k * 3 + c + 1) * HALF) for k in range(2))
            low0, low1 = (
                jnp.where(first, kept[low, :], incoming[low, :]),
                jnp.where(first, incoming[low, :], kept[low, :]),
            )
            high0, high1 = (
                jnp.where(first, kept[high, :], incoming[high, :]),
                jnp.where(first, incoming[high, :], kept[high, :]),
            )
            middle = high0 + low1
            joint[c * HALF : (c + 1) * HALF, :] = middle
            for kind, value in enumerate((low0 + ratio * middle, high1 + ratio * middle)):
                for i in range(2):
                    out[pl.ds(c * 4 + kind * 2 + i, CHIPS, stride=12), :] = value[
                        i * CHIPS : (i + 1) * CHIPS
                    ]


def line_kernel(flags, received, spread, th, tl, lamx, mu, out):
    @pl.when(flags[0] != 0)
    def _():
        def part(c, kind, i):
            return received[pl.ds(c * 4 + kind * 2 + i, CHIPS, stride=12), :]

        place = iota((CHIPS, NZ), 0)
        rows = []
        for c in range(3):
            for i in range(2):
                ahead = jnp.where(
                    place == CHIPS - 1, 0.0, pltpu.roll(part(c, 0, i), CHIPS - 1, 0)
                )
                rows.append(part(c, 1, i) + ahead)
        high, low = split(jnp.concatenate(rows, axis=1))
        modes = mm(spread[...], jnp.concatenate([high, low, high], axis=0))
        factors = []
        for i in range(2):
            row = mu[pl.ds(flags[1] * HALF + i * CHIPS + (flags[2] >> 1), 1), :]
            factors.append((2.0 / (NX + 1)) / (lamx[...] + row))
        modes = modes * jnp.concatenate(factors * 3, axis=1)
        solved = table_times(th[...], tl[...], modes)
        for c in range(3):
            for i in range(2):
                j = c * 2 + i
                value = solved[:, j * NZ : (j + 1) * NZ]
                behind = jnp.where(place == 0, 0.0, pltpu.roll(value, 1, 0))
                out[pl.ds(c * 4 + i, CHIPS, stride=12), :] = behind
                out[pl.ds(c * 4 + 2 + i, CHIPS, stride=12), :] = value


def inverse_kernel(
    flags,
    planes,
    joint,
    joined,
    own,
    other,
    gather,
    codes,
    sz,
    syh,
    syl,
    mu,
    state_home,
    speed_home,
    up_home,
    down_home,
    send,
    out,
    edge_home,
    layer_home,
    held,
    edge,
    layer,
    state,
    speed,
    up,
    down,
    sems,
):
    @pl.when(flags[0] == 0)
    def _():
        pairs = [(state_home, state), (speed_home, speed), (up_home, up), (down_home, down)]
        copies = [pltpu.make_async_copy(a, b, sems.at[i]) for i, (a, b) in enumerate(pairs)]
        for copy in copies:
            copy.start()
        for copy in copies:
            copy.wait()
        wide = jnp.concatenate([up[768:896, :], speed[...], down[768:896, :]], axis=0)
        copies = []
        for c in range(3):
            block = slice(c * 256, (c + 1) * 256)
            field = jnp.concatenate([up[block, :], state[c], down[block, :]], axis=0)
            field = near_step(near_step(field, wide), speed[...])
            held[c] = field
            copies.append(pltpu.make_async_copy(held.at[c], out.at[c], sems.at[c]))
            copies[-1].start()
            edge[c] = field.reshape(NJ, NI, NK)[:, NI - 8 :, :]
            layer[c] = state[c, pl.ds(NI - 1, NJ, stride=NI), :]
        for a, b, i in ((edge, edge_home, 3), (layer, layer_home, 4)):
            copies.append(pltpu.make_async_copy(a, b, sems.at[i]))
            copies[-1].start()
        for copy in copies:
            copy.wait()

    @pl.when(flags[0] != 0)
    def _():
        beta = mu[...] + 2.0
        g11, g12, g13 = weights(beta)
        inv = 1.0 / (beta - 2.0 * g11)
        first = flags[1] == 0
        inside = jnp.where(flags[2] == BRICKS - 1, 0.0, 1.0)
        potentials = []
        for c in range(3):

            def full(pieces):
                a, b = pieces(own, joint), pieces(other, joined)
                return jnp.concatenate([jnp.where(first, a, b), jnp.where(first, b, a)], axis=0)

            def solved(kind):
                return full(
                    lambda ref, _: jnp.concatenate(
                        [
                            ref[pl.ds(c * 4 + kind * 2 + i, CHIPS, stride=12), :]
                            for i in range(2)
                        ],
                        axis=0,
                    )
                )

            before, after = solved(0), solved(1)
            middle = full(lambda _, ref: ref[c * HALF : (c + 1) * HALF, :])
            middle = (middle + g13 * (before + after)) * inv
            left = jnp.where(first, before, middle)
            right = jnp.where(first, middle, after)
            f0, f1, f2, f3 = (planes[c, p] for p in range(4))
            u0 = g11 * (f0 + left) + g12 * f1 + g13 * (f2 + right)
            u1 = g12 * (f0 + left + beta * f1 + f2 + right)
            u2 = g13 * (f0 + left) + g12 * f1 + g11 * (f2 + right)
            stack = [u0, u1, u2, right]
            if c:
                stack = [left] + stack + [(beta * right - u2 - f3) * inside]
            field = table_times(syh[...], syl[...], jnp.concatenate(stack, axis=1))
            field = jnp.concatenate(
                [field[:, p * NZ : (p + 1) * NZ] for p in range(len(stack))], axis=0
            )
            potentials.append(times_paired(field, sz[...]))
        rows = iota((RPB, NZ), 0) & (NY - 1)
        lanes = iota((RPB, NZ), 1)

        def dy(field):
            upper = jnp.where(rows == NY - 1, 0.0, pltpu.roll(field, RPB - 1, 0))
            lower = jnp.where(rows == 0, 0.0, pltpu.roll(field, 1, 0))
            return (upper - lower) * 0.5

        def dz(field):
            upper = jnp.where(lanes == NZ - 1, 0.0, pltpu.roll(field, NZ - 1, 1))
            lower = jnp.where(lanes == 0, 0.0, pltpu.roll(field, 1, 1))
            return (upper - lower) * 0.5

        def dx(field):
            return (field[2 * NY : 2 * NY + RPB] - field[:RPB]) * 0.5

        px, py, pz = potentials[0], potentials[1][NY : NY + RPB], potentials[2][NY : NY + RPB]
        velocity = (
            dy(pz) - dz(py),
            dz(px) - dx(potentials[2]),
            dx(potentials[1]) - dy(px),
        )
        copies = []
        for c in range(3):
            held[c] = velocity[c]
            copies.append(pltpu.make_async_copy(held.at[c], out.at[c], sems.at[c]))
            copies[-1].start()
        send[pl.ds(3 * GROUP, TARGETS, stride=BACK), :] = codes[...]
        for c in range(3):
            rows_out = pick(gather[...], velocity[c])
            for lane in range(GROUP):
                send[pl.ds(c * GROUP + lane, TARGETS, stride=BACK), :] = rows_out[
                    lane * TARGETS : (lane + 1) * TARGETS
                ]
        for copy in copies:
            copy.wait()


def cell_kernel(flags, received, *outs):
    @pl.when(flags[0] != 0)
    def _():
        codes = received[pl.ds(3 * GROUP, TARGETS, stride=BACK), :].astype(bf16)
        codes = mm(codes, onehot(iota((NZ, SLOTS), 0) == (iota((NZ, SLOTS), 1) >> 5)))
        mine = iota((TARGETS, SLOTS), 0) == (iota((TARGETS, SLOTS), 1) & (TARGETS - 1))
        code = jnp.sum(jnp.where(mine, codes, 0.0), axis=0, keepdims=True).astype(i32)
        cells = onehot(iota((CZ * NJ, SLOTS), 0) == code - 1)
        for c in range(3):
            rows = jnp.concatenate(
                [
                    received[pl.ds(c * GROUP + lane, TARGETS, stride=BACK), :]
                    for lane in range(GROUP)
                ],
                axis=0,
            )
            sums = pick(cells, rows)
            for k in range(CZ):
                outs[k][c * NJ : (c + 1) * NJ, :] = sums[k * NJ : (k + 1) * NJ]


def close_kernel(flags, field, edge, layer, remesh, b0, b1, b2, b3, out, slab, sem):
    @pl.when(flags[0] == 0)
    def _():
        total = exact((b0[...] + b1[...]) + (b2[...] + b3[...]), remesh[...], NT)
        first = [total[c * NJ : (c + 1) * NJ] for c in range(3)]
        second = [layer[c] for c in range(3)]
        for c in range(3):
            d, e = (c + 1) % 3, (c + 2) % 3
            cross = first[d] * second[e] - first[e] * second[d]
            slab[c] = edge[c]
            slab[c, :, 7, :] = edge[c, :, 7, :] + coupling * cross
        copy = pltpu.make_async_copy(slab, out.at[:, :, pl.ds(NI - 8, 8), :], sem)
        copy.start()
        copy.wait()


def call(kernel, outs, flags, *args, fetch=False, alias=False, far=0, scratch=()):
    args = [jnp.asarray(a) for a in args]
    spaces = [
        pltpu.HBM if fetch or (alias and i == 0) or i >= len(args) - far else pltpu.VMEM
        for i in range(len(args))
    ]
    homes = [len(o) > 2 for o in outs]
    staged = [i for i, o in enumerate(outs) if o[2:] == ("home",)]
    loads = [pltpu.VMEM(a.shape, a.dtype) for a in args] if fetch else []
    stores = [pltpu.VMEM(*outs[i][:2]) for i in staged]
    sems = [pltpu.SemaphoreType.DMA((len(loads) + len(stores),))] if loads or stores else []

    def body(flags, *refs):
        given, made = list(refs[: len(args)]), list(refs[len(args) : len(args) + len(outs)])
        rest = refs[len(args) + len(outs) :]
        held, kept = rest[: len(loads)], rest[len(loads) : len(loads) + len(stores)]
        own = rest[len(loads) + len(stores) + len(sems) :]
        if sems:
            sem = rest[len(loads) + len(stores)]
        copies = [
            pltpu.make_async_copy(a, b, sem.at[i]) for i, (a, b) in enumerate(zip(given, held))
        ]
        for copy in copies:
            copy.start()
        for copy in copies:
            copy.wait()
        homes_out = [made[i] for i in staged]
        for i, ref in zip(staged, kept):
            made[i] = ref
        kernel(flags, *(held if fetch else given), *made, *own)
        copies = [
            pltpu.make_async_copy(a, b, sem.at[len(loads) + i])
            for i, (a, b) in enumerate(zip(kept, homes_out))
        ]
        for copy in copies:
            copy.start()
        for copy in copies:
            copy.wait()

    return pl.pallas_call(
        body,
        out_shape=[(pltpu.HBM if home else pltpu.VMEM)(*o[:2]) for o, home in zip(outs, homes)],
        in_specs=[pl.BlockSpec(memory_space=pltpu.SMEM)]
        + [pl.BlockSpec(memory_space=space) for space in spaces],
        out_specs=[
            pl.BlockSpec(memory_space=pltpu.HBM if home else pltpu.VMEM) for home in homes
        ],
        scratch_shapes=loads + stores + sems + list(scratch),
        input_output_aliases={1: 0} if alias else {},
        compiler_params=pltpu.CompilerParams(vmem_limit_bytes=24 << 20),
    )(
        flags,
        *[
            a if alias and i == 0 else pltpu.with_memory_space_constraint(a, space)
            for i, (a, space) in enumerate(zip(args, spaces))
        ],
    )


def place_of(g, y, z, x, c):
    return (((g * CY + y) * CZ + z) * CX + x) * CC + c


def chips():
    return [
        (y, z, x, c) for y in range(CY) for z in range(CZ) for x in range(CX) for c in range(CC)
    ]


def on_device(state, courant, remesh, shell_dest, shell_row, return_dest, return_row, return_block):
    dev = lax.axis_index(DEV)
    flags = jnp.stack(
        [lax.axis_index("grp"), lax.axis_index("core"), dev, lax.axis_index("z")]
    ).astype(i32)
    field = state.reshape(3, RPB, NZ)
    speed = courant.reshape(RPB, NK)
    sy, sz, line = sines(NY), sines(NZ), line_table()
    syh, syl = halves(sy)
    szp = paired(sz)
    kh, kl = halves(line)
    triple = np.concatenate([kh, kh, kl], axis=1)
    th, tl = np.ascontiguousarray(kh.T), np.ascontiguousarray(kl.T)
    lamx = eigen(NX).astype(np.float32)[:, None]
    mu = (eigen(NY)[:, None] + eigen(NZ)[None, :]).astype(np.float32)

    group = lax.axis_index("grp").astype(i32).reshape(1)
    (blocks,) = call(
        shell_kernel,
        [((3, NJ, NI // 4, NK), f32)],
        group,
        field.reshape(3, NJ, NI, NK),
        far=1,
        scratch=[pltpu.SemaphoreType.DMA],
    )
    across = [(place_of(0, *q), place_of(1, *q)) for q in chips()]
    blocks = lax.ppermute(blocks.reshape(3, SB, NK), ALL, across)

    sd, sr, rd, rr, rb = (
        v.reshape(1, SB) for v in (shell_dest, shell_row, return_dest, return_row, return_block)
    )
    place, rows, merged = call(
        route_kernel,
        [((SLOTS, SB), bf16), ((BRICKS, NZ), f32), ((2 * NK, 2 * NZ), bf16)],
        flags,
        sd,
        sr,
        remesh,
        sz.astype(np.float32),
        fetch=True,
    )
    turned, gather, codes, last, lead = call(
        ready_kernel,
        [
            ((3, RPB, NZ), f32),
            ((SLOTS, RPB), bf16, "home"),
            ((TARGETS, NZ), f32, "home"),
            ((896, NK), f32, "home"),
            ((896, NK), f32, "home"),
        ],
        flags,
        field,
        speed,
        szp,
        rd,
        rr,
        rb,
        fetch=True,
    )
    blocks, turned = lax.optimization_barrier((blocks, turned))
    (bundle,) = call(
        bucket_kernel, [((BRICKS * CHUNK, NZ), f32)], flags, blocks, rows, place, merged
    )
    bundle, last, lead = lax.optimization_barrier((bundle, last, lead))
    bundle = lax.all_to_all(bundle.reshape(BRICKS, CHUNK, 1, NZ), DEV, 0, 0, tiled=True)
    ahead = [(d, (d + 1) % BRICKS) for d in range(BRICKS)]
    up = lax.ppermute(last, ALL, ahead)
    down = lax.ppermute(lead, ALL, [(b, a) for a, b in ahead])
    bundle, up, down = lax.optimization_barrier((bundle, up, down))
    planes, outgoing, kept = call(
        forward_kernel,
        [((3, 4, NY, NZ), f32), ((3 * NY, NZ), f32), ((3 * NY, NZ), f32)],
        flags,
        bundle.reshape(BRICKS * CHUNK, NZ),
        turned,
        syh,
        syl,
        mu,
    )
    swap = [(0, 1), (1, 0)]
    same = ("y", "z", "x")
    incoming = lax.ppermute(outgoing, "core", swap)
    share, joint = call(
        reduce_kernel,
        [((CHIPS * 12, NZ), f32), ((3 * HALF, NZ), f32)],
        flags,
        incoming,
        kept,
        mu,
    )
    joined = lax.ppermute(joint, "core", swap)
    share = lax.all_to_all(share.reshape(CHIPS, 3, 4, NZ), same, 0, 0, tiled=True)
    (solved,) = call(
        line_kernel,
        [((CHIPS * 12, NZ), f32)],
        flags,
        share.reshape(CHIPS * 12, NZ),
        triple,
        th,
        tl,
        lamx,
        mu,
    )
    own = lax.all_to_all(solved.reshape(CHIPS, 3, 4, NZ), same, 0, 0, tiled=True)
    own = own.reshape(CHIPS * 12, NZ)
    other = lax.ppermute(own, "core", swap)
    halo = pltpu.VMEM((896, NK), f32)
    send, result, edge, layer = call(
        inverse_kernel,
        [
            ((TARGETS * BACK, NZ), f32),
            ((3, RPB, NZ), f32, "raw"),
            ((3, NJ, 8, NK), f32, "raw"),
            ((3, NJ, NK), f32, "raw"),
        ],
        flags,
        planes,
        joint,
        joined,
        own,
        other,
        gather,
        codes,
        szp,
        syh,
        syl,
        mu,
        field,
        speed,
        up,
        down,
        far=4,
        scratch=[
            pltpu.VMEM((3, RPB, NZ), f32),
            pltpu.VMEM((3, NJ, 8, NK), f32),
            pltpu.VMEM((3, NJ, NK), f32),
            pltpu.VMEM((3, RPB, NK), f32),
            pltpu.VMEM((RPB, NK), f32),
            halo,
            halo,
            pltpu.SemaphoreType.DMA((5,)),
        ],
    )
    returned = lax.all_to_all(
        send.reshape(TARGETS, BACK, 1, NZ), ("y", "x", "core"), 0, 0, tiled=True
    )
    sums = call(
        cell_kernel, [((3 * NJ, NZ), f32)] * CZ, flags, returned.reshape(TARGETS * BACK, NZ)
    )
    parts = []
    for k in range(CZ):
        pairs = [
            (place_of(1, y, z, x, c), place_of(0, y, (z + k) % CZ, x, c)) for y, z, x, c in chips()
        ]
        parts.append(lax.ppermute(sums[k], ALL, pairs))
    (result,) = call(
        close_kernel,
        [((3, NJ, NI, NZ), f32, "raw")],
        flags,
        result.reshape(3, NJ, NI, NZ),
        edge,
        layer,
        remesh,
        *parts,
        alias=True,
        scratch=[pltpu.VMEM((3, NJ, 8, NZ), f32), pltpu.SemaphoreType.DMA],
    )
    return result.reshape(1, 3, RPB * NZ)


def solution(mesh):
    fine = Mesh(mesh.devices.reshape(2, CY, CZ, CX, CC), ALL)
    placed = (
        P("grp", None, DEV),
        P(DEV),
        P(),
        P(DEV, None),
        P(DEV),
        P(DEV, None),
        P(DEV),
        P(DEV),
    )
    return jax.shard_map(
        on_device, mesh=fine, in_specs=placed, out_specs=P("grp", None, DEV), check_vma=False
    )
```

```python
import jax
import jax.numpy as jnp
import ml_dtypes
import numpy as np
from jax import lax
from jax.experimental import pallas as pl
from jax.experimental.pallas import tpu as pltpu
from jax.sharding import Mesh
from jax.sharding import PartitionSpec as P

NX, NY, NZ = 512, 256, 128
NI, NK = 64, 128
NJ = 16
CY, CZ, CX, CC = 4, 4, 4, 2
BRICKS = 128
CHIPS = 64
HALF = 128
CAP = 4
SB = 256
RPB = 1024
TARGETS = CY * CX * CC
GROUP = CZ * CAP
SLOTS = BRICKS * CAP
CHUNK = 3 * CAP + 1
BACK = 3 * GROUP + 1
DEV = ("y", "z", "x", "core")
ALL = ("grp",) + DEV

viscosity = 0.2
coupling = 1.0
f32 = jnp.float32
bf16 = jnp.bfloat16
i32 = jnp.int32
highest = lax.Precision.HIGHEST
NT = (((1,), (1,)), ((), ()))


def sines(length):
    counts = np.arange(length) + 1
    phase = counts[:, None] * counts[None, :] % (2 * (length + 1))
    return np.sin(np.pi * phase / (length + 1))


def eigen(length):
    counts = np.arange(length) + 1.0
    return 4.0 * np.sin(0.5 * np.pi * counts / (length + 1)) ** 2


def halves(table):
    table = table.astype(np.float32)
    high = table.astype(ml_dtypes.bfloat16)
    low = (table - high.astype(np.float32)).astype(ml_dtypes.bfloat16)
    return high, low


def paired(table):
    high, low = halves(table)
    return np.block([[high, low], [high, np.zeros_like(low)]]).astype(ml_dtypes.bfloat16)


def line_table():
    plane = 8 * (np.arange(CHIPS) + 1)
    phase = (np.arange(NX) + 1)[:, None] * plane[None, :] % (2 * (NX + 1))
    return np.sin(np.pi * phase / (NX + 1))


def iota(shape, axis):
    return lax.broadcasted_iota(i32, shape, axis)


def split(value):
    high = value.astype(bf16)
    return high, (value - high.astype(f32)).astype(bf16)


def mm(a, b):
    return jnp.dot(a, b, preferred_element_type=f32)


def lanes_paired(value):
    return jnp.concatenate(split(value), axis=1)


def fold(value):
    half = value.shape[1] // 2
    return value[:, :half] + value[:, half:]


def pick(onehot, value):
    return fold(mm(onehot, lanes_paired(value)))


def times_paired(value, table):
    return fold(mm(lanes_paired(value), table))


def table_times(high, low, value):
    vh, vl = split(value)
    return mm(high, vh) + mm(high, vl) + mm(low, vh)


def exact(a, b, dims=(((1,), (0,)), ((), ()))):
    return lax.dot_general(a, b, dims, precision=highest, preferred_element_type=f32)


def onehot(condition):
    return jnp.where(condition, 1.0, 0.0).astype(bf16)


def ranks(matches):
    size = matches.shape[1]
    before = onehot(iota((size, size), 0) < iota((size, size), 1))
    counts = mm(matches.astype(bf16), before)
    return jnp.sum(matches * counts, axis=0, keepdims=True).astype(i32)


def owners(owner):
    core = owner & (CC - 1)
    x = (owner >> 1) & (CX - 1)
    z = (owner >> 3) & (CZ - 1)
    lane = z * CAP + ranks(jnp.where(iota((BRICKS, SB), 0) == owner, 1.0, 0.0))
    return owner >> 5, z, x, core, lane


def route_kernel(flags, sd, sr, remesh, sz, place, codes, merged):
    bricks = iota((BRICKS, SB), 0)
    matches = jnp.where(bricks == sd[...], 1.0, 0.0)
    rank = ranks(matches)
    place[...] = onehot(iota((SLOTS, SB), 0) == rank * BRICKS + sd[...])
    tagged = jnp.where(bricks == rank, (sr[...] + 1).astype(f32), 0.0)
    codes[...] = exact(matches, tagged, NT)
    high, low = split(exact(remesh[...], sz[...]))
    merged[...] = jnp.concatenate(
        [
            jnp.concatenate([high, low], axis=1),
            jnp.concatenate([high, jnp.zeros_like(low)], axis=1),
        ],
        axis=0,
    )


def ready_kernel(
    flags, state, speed, sz, rd, rr, rb, out, gather, codes, last, lead
):
    @pl.when(flags[0] == 0)
    def _():
        for c in range(3):
            last[c * 256 : (c + 1) * 256, :] = state[c, 768:, :]
            lead[c * 256 : (c + 1) * 256, :] = state[c, :256, :]
        last[768:, :] = speed[896:, :]
        lead[768:, :] = speed[:128, :]

    @pl.when(flags[0] != 0)
    def _():
        for c in range(3):
            out[c] = times_paired(state[c], sz[...])
        y, z, x, core, lane = owners(rd[...])
        target = (y * CX + x) * CC + core
        gather[...] = lax.dot_general(
            onehot(iota((SLOTS, SB), 0) == lane * TARGETS + target),
            onehot(iota((RPB, SB), 0) == rr[...]),
            NT,
            preferred_element_type=f32,
        ).astype(bf16)
        code = ((z - flags[3]) & (CZ - 1)) * NJ + rb[...] + 1
        tagged = jnp.where(iota((NZ, SB), 0) == lane, code.astype(f32), 0.0)
        sent = onehot(iota((TARGETS, SB), 0) == target)
        codes[...] = lax.dot_general(sent, tagged.astype(bf16), NT, preferred_element_type=f32)


def near_step(field, speed):
    rows = speed.shape[0]
    centre = field[128 : 128 + rows]
    transport = (
        8.0 * (field[192 : 192 + rows] - field[64 : 64 + rows])
        - (field[256 : 256 + rows] - field[:rows])
    ) / 12.0
    place = iota((rows, NK), 0) & (NI - 1)
    above = jnp.where(place == NI - 1, 0.0, pltpu.roll(centre, rows - 1, 0))
    below = jnp.where(place == 0, 0.0, pltpu.roll(centre, 1, 0))
    return centre - speed * transport + viscosity * (above - 2.0 * centre + below)


def shell_kernel(flags, state, out, sem):
    @pl.when(flags[0] == 0)
    def _():
        copy = pltpu.make_async_copy(state.at[:, :, pl.ds(NI - NI // 4, NI // 4), :], out, sem)
        copy.start()
        copy.wait()


def bucket_kernel(flags, blocks, codes, place, merged, out):
    @pl.when(flags[0] != 0)
    def _():
        out[pl.ds(3 * CAP, BRICKS, stride=CHUNK), :] = codes[...]
        for c in range(3):
            moved = times_paired(blocks[c], merged[...])
            slots = pick(place[...], moved)
            for rank in range(CAP):
                out[pl.ds(c * CAP + rank, BRICKS, stride=CHUNK), :] = slots[
                    rank * BRICKS : (rank + 1) * BRICKS
                ]


def weights(beta):
    outer = beta * beta - 2.0
    g12 = 1.0 / outer
    g13 = g12 / beta
    g11 = (beta * beta - 1.0) * g13
    return g11, g12, g13


def forward_kernel(flags, received, work, syh, syl, mu, planes, outgoing, kept):
    @pl.when(flags[0] != 0)
    def _():
        beta = mu[...] + 2.0
        g11, g12, g13 = weights(beta)
        first = flags[1] == 0
        codes = received[pl.ds(3 * CAP, BRICKS, stride=CHUNK), :].T
        landing = jnp.concatenate([codes[r : r + 1, :] for r in range(CAP)], axis=1).astype(i32)
        spread = onehot(iota((RPB, SLOTS), 0) == landing - 1)
        for c in range(3):
            rows = jnp.concatenate(
                [received[pl.ds(c * CAP + r, BRICKS, stride=CHUNK), :] for r in range(CAP)], axis=0
            )
            field = (pick(spread, rows) + work[c]) * (4.0 / ((NY + 1) * (NZ + 1)))
            field = jnp.concatenate([field[p * NY : (p + 1) * NY] for p in range(4)], axis=1)
            field = table_times(syh[...], syl[...], field)
            f0, f1, f2, f3 = (field[:, p * NZ : (p + 1) * NZ] for p in range(4))
            for p, plane in enumerate((f0, f1, f2, f3)):
                planes[c, p] = plane
            low = g11 * f0 + g12 * f1 + g13 * f2
            high = f3 + g13 * f0 + g12 * f1 + g11 * f2
            for kind, value in enumerate((low, high)):
                block = slice((kind * 3 + c) * HALF, (kind * 3 + c + 1) * HALF)
                outgoing[block, :] = jnp.where(first, value[HALF:], value[:HALF])
                kept[block, :] = jnp.where(first, value[:HALF], value[HALF:])


def reduce_kernel(flags, incoming, kept, mu, out, joint):
    @pl.when(flags[0] != 0)
    def _():
        beta = mu[pl.ds(pl.multiple_of(flags[1] * HALF, HALF), HALF), :] + 2.0
        g11, _, g13 = weights(beta)
        ratio = g13 / (beta - 2.0 * g11)
        first = flags[1] == 0
        for c in range(3):
            low, high = (slice((k * 3 + c) * HALF, (k * 3 + c + 1) * HALF) for k in range(2))
            low0, low1 = (
                jnp.where(first, kept[low, :], incoming[low, :]),
                jnp.where(first, incoming[low, :], kept[low, :]),
            )
            high0, high1 = (
                jnp.where(first, kept[high, :], incoming[high, :]),
                jnp.where(first, incoming[high, :], kept[high, :]),
            )
            middle = high0 + low1
            joint[c * HALF : (c + 1) * HALF, :] = middle
            for kind, value in enumerate((low0 + ratio * middle, high1 + ratio * middle)):
                for i in range(2):
                    out[pl.ds(c * 4 + kind * 2 + i, CHIPS, stride=12), :] = value[
                        i * CHIPS : (i + 1) * CHIPS
                    ]


def line_kernel(flags, received, spread, th, tl, lamx, mu, out):
    @pl.when(flags[0] != 0)
    def _():
        def part(c, kind, i):
            return received[pl.ds(c * 4 + kind * 2 + i, CHIPS, stride=12), :]

        place = iota((CHIPS, NZ), 0)
        rows = []
        for c in range(3):
            for i in range(2):
                ahead = jnp.where(
                    place == CHIPS - 1, 0.0, pltpu.roll(part(c, 0, i), CHIPS - 1, 0)
                )
                rows.append(part(c, 1, i) + ahead)
        high, low = split(jnp.concatenate(rows, axis=1))
        modes = mm(spread[...], jnp.concatenate([high, low, high], axis=0))
        factors = []
        for i in range(2):
            row = mu[pl.ds(flags[1] * HALF + i * CHIPS + (flags[2] >> 1), 1), :]
            factors.append((2.0 / (NX + 1)) / (lamx[...] + row))
        modes = modes * jnp.concatenate(factors * 3, axis=1)
        solved = table_times(th[...], tl[...], modes)
        for c in range(3):
            for i in range(2):
                j = c * 2 + i
                value = solved[:, j * NZ : (j + 1) * NZ]
                behind = jnp.where(place == 0, 0.0, pltpu.roll(value, 1, 0))
                out[pl.ds(c * 4 + i, CHIPS, stride=12), :] = behind
                out[pl.ds(c * 4 + 2 + i, CHIPS, stride=12), :] = value


def inverse_kernel(
    flags,
    planes,
    joint,
    joined,
    own,
    other,
    gather,
    codes,
    sz,
    syh,
    syl,
    mu,
    state_home,
    speed_home,
    up_home,
    down_home,
    send,
    out,
    edge_home,
    layer_home,
    held,
    edge,
    layer,
    state,
    speed,
    up,
    down,
    sems,
):
    @pl.when(flags[0] == 0)
    def _():
        pairs = [(speed_home, speed), (up_home, up), (down_home, down)]
        pairs += [(state_home.at[c], state.at[c]) for c in range(3)]
        loads = [pltpu.make_async_copy(a, b, sems.at[i]) for i, (a, b) in enumerate(pairs)]
        for copy in loads:
            copy.start()
        for copy in loads[:3]:
            copy.wait()
        wide = jnp.concatenate([up[768:896, :], speed[...], down[768:896, :]], axis=0)
        copies = []
        for c in range(3):
            block = slice(c * 256, (c + 1) * 256)
            loads[3 + c].wait()
            field = jnp.concatenate([up[block, :], state[c], down[block, :]], axis=0)
            field = near_step(near_step(field, wide), speed[...])
            held[c] = field
            copies.append(pltpu.make_async_copy(held.at[c], out.at[c], sems.at[6 + c]))
            copies[-1].start()
            edge[c] = field.reshape(NJ, NI, NK)[:, NI - 8 :, :]
            layer[c] = state[c, pl.ds(NI - 1, NJ, stride=NI), :]
        for a, b, i in ((edge, edge_home, 9), (layer, layer_home, 10)):
            copies.append(pltpu.make_async_copy(a, b, sems.at[i]))
            copies[-1].start()
        for copy in copies:
            copy.wait()

    @pl.when(flags[0] != 0)
    def _():
        beta = mu[...] + 2.0
        g11, g12, g13 = weights(beta)
        inv = 1.0 / (beta - 2.0 * g11)
        first = flags[1] == 0
        inside = jnp.where(flags[2] == BRICKS - 1, 0.0, 1.0)
        potentials = []
        for c in range(3):

            def full(pieces):
                a, b = pieces(own, joint), pieces(other, joined)
                return jnp.concatenate([jnp.where(first, a, b), jnp.where(first, b, a)], axis=0)

            def solved(kind):
                return full(
                    lambda ref, _: jnp.concatenate(
                        [
                            ref[pl.ds(c * 4 + kind * 2 + i, CHIPS, stride=12), :]
                            for i in range(2)
                        ],
                        axis=0,
                    )
                )

            before, after = solved(0), solved(1)
            middle = full(lambda _, ref: ref[c * HALF : (c + 1) * HALF, :])
            middle = (middle + g13 * (before + after)) * inv
            left = jnp.where(first, before, middle)
            right = jnp.where(first, middle, after)
            f0, f1, f2, f3 = (planes[c, p] for p in range(4))
            u0 = g11 * (f0 + left) + g12 * f1 + g13 * (f2 + right)
            u1 = g12 * (f0 + left + beta * f1 + f2 + right)
            u2 = g13 * (f0 + left) + g12 * f1 + g11 * (f2 + right)
            stack = [u0, u1, u2, right]
            if c:
                stack = [left] + stack + [(beta * right - u2 - f3) * inside]
            field = table_times(syh[...], syl[...], jnp.concatenate(stack, axis=1))
            field = jnp.concatenate(
                [field[:, p * NZ : (p + 1) * NZ] for p in range(len(stack))], axis=0
            )
            potentials.append(times_paired(field, sz[...]))
        rows = iota((RPB, NZ), 0) & (NY - 1)
        lanes = iota((RPB, NZ), 1)

        def dy(field):
            upper = jnp.where(rows == NY - 1, 0.0, pltpu.roll(field, RPB - 1, 0))
            lower = jnp.where(rows == 0, 0.0, pltpu.roll(field, 1, 0))
            return (upper - lower) * 0.5

        def dz(field):
            upper = jnp.where(lanes == NZ - 1, 0.0, pltpu.roll(field, NZ - 1, 1))
            lower = jnp.where(lanes == 0, 0.0, pltpu.roll(field, 1, 1))
            return (upper - lower) * 0.5

        def dx(field):
            return (field[2 * NY : 2 * NY + RPB] - field[:RPB]) * 0.5

        px, py, pz = potentials[0], potentials[1][NY : NY + RPB], potentials[2][NY : NY + RPB]
        velocity = (
            dy(pz) - dz(py),
            dz(px) - dx(potentials[2]),
            dx(potentials[1]) - dy(px),
        )
        copies = []
        for c in range(3):
            held[c] = velocity[c]
            copies.append(pltpu.make_async_copy(held.at[c], out.at[c], sems.at[c]))
            copies[-1].start()
        send[pl.ds(3 * GROUP, TARGETS, stride=BACK), :] = codes[...]
        for c in range(3):
            rows_out = pick(gather[...], velocity[c])
            for lane in range(GROUP):
                send[pl.ds(c * GROUP + lane, TARGETS, stride=BACK), :] = rows_out[
                    lane * TARGETS : (lane + 1) * TARGETS
                ]
        for copy in copies:
            copy.wait()


def cell_kernel(flags, received, *outs):
    @pl.when(flags[0] != 0)
    def _():
        codes = received[pl.ds(3 * GROUP, TARGETS, stride=BACK), :].astype(bf16)
        codes = mm(codes, onehot(iota((NZ, SLOTS), 0) == (iota((NZ, SLOTS), 1) >> 5)))
        mine = iota((TARGETS, SLOTS), 0) == (iota((TARGETS, SLOTS), 1) & (TARGETS - 1))
        code = jnp.sum(jnp.where(mine, codes, 0.0), axis=0, keepdims=True).astype(i32)
        cells = onehot(iota((CZ * NJ, SLOTS), 0) == code - 1)
        for c in range(3):
            rows = jnp.concatenate(
                [
                    received[pl.ds(c * GROUP + lane, TARGETS, stride=BACK), :]
                    for lane in range(GROUP)
                ],
                axis=0,
            )
            sums = pick(cells, rows)
            for k in range(CZ):
                outs[k][c * NJ : (c + 1) * NJ, :] = sums[k * NJ : (k + 1) * NJ]


def close_kernel(flags, field, edge, layer, remesh, b0, b1, b2, b3, out, slab, sem):
    @pl.when(flags[0] == 0)
    def _():
        total = exact((b0[...] + b1[...]) + (b2[...] + b3[...]), remesh[...], NT)
        first = [total[c * NJ : (c + 1) * NJ] for c in range(3)]
        second = [layer[c] for c in range(3)]
        for c in range(3):
            d, e = (c + 1) % 3, (c + 2) % 3
            cross = first[d] * second[e] - first[e] * second[d]
            slab[c] = edge[c]
            slab[c, :, 7, :] = edge[c, :, 7, :] + coupling * cross
        copy = pltpu.make_async_copy(slab, out.at[:, :, pl.ds(NI - 8, 8), :], sem)
        copy.start()
        copy.wait()


def call(kernel, outs, flags, *args, fetch=False, alias=False, far=0, scratch=()):
    args = [jnp.asarray(a) for a in args]
    spaces = [
        pltpu.HBM if fetch or (alias and i == 0) or i >= len(args) - far else pltpu.VMEM
        for i in range(len(args))
    ]
    homes = [len(o) > 2 for o in outs]
    staged = [i for i, o in enumerate(outs) if o[2:] == ("home",)]
    loads = [pltpu.VMEM(a.shape, a.dtype) for a in args] if fetch else []
    stores = [pltpu.VMEM(*outs[i][:2]) for i in staged]
    sems = [pltpu.SemaphoreType.DMA((len(loads) + len(stores),))] if loads or stores else []

    def body(*refs):
        flags, refs = [ref[0] for ref in refs[:4]], refs[4:]
        given, made = list(refs[: len(args)]), list(refs[len(args) : len(args) + len(outs)])
        rest = refs[len(args) + len(outs) :]
        held, kept = rest[: len(loads)], rest[len(loads) : len(loads) + len(stores)]
        own = rest[len(loads) + len(stores) + len(sems) :]
        if sems:
            sem = rest[len(loads) + len(stores)]
        copies = [
            pltpu.make_async_copy(a, b, sem.at[i]) for i, (a, b) in enumerate(zip(given, held))
        ]
        for copy in copies:
            copy.start()
        for copy in copies:
            copy.wait()
        homes_out = [made[i] for i in staged]
        for i, ref in zip(staged, kept):
            made[i] = ref
        kernel(flags, *(held if fetch else given), *made, *own)
        copies = [
            pltpu.make_async_copy(a, b, sem.at[len(loads) + i])
            for i, (a, b) in enumerate(zip(kept, homes_out))
        ]
        for copy in copies:
            copy.start()
        for copy in copies:
            copy.wait()

    return pl.pallas_call(
        body,
        out_shape=[(pltpu.HBM if home else pltpu.VMEM)(*o[:2]) for o, home in zip(outs, homes)],
        in_specs=[pl.BlockSpec(memory_space=pltpu.SMEM)] * 4
        + [pl.BlockSpec(memory_space=space) for space in spaces],
        out_specs=[
            pl.BlockSpec(memory_space=pltpu.HBM if home else pltpu.VMEM) for home in homes
        ],
        scratch_shapes=loads + stores + sems + list(scratch),
        input_output_aliases={4: 0} if alias else {},
        compiler_params=pltpu.CompilerParams(vmem_limit_bytes=24 << 20),
    )(
        *flags,
        *[
            a if alias and i == 0 else pltpu.with_memory_space_constraint(a, space)
            for i, (a, space) in enumerate(zip(args, spaces))
        ],
    )


def place_of(g, y, z, x, c):
    return (((g * CY + y) * CZ + z) * CX + x) * CC + c


def chips():
    return [
        (y, z, x, c) for y in range(CY) for z in range(CZ) for x in range(CX) for c in range(CC)
    ]


def on_device(state, courant, remesh, shell_dest, shell_row, return_dest, return_row, return_block):
    dev = lax.axis_index(DEV)
    flags = [
        v.astype(i32).reshape(1)
        for v in (lax.axis_index("grp"), lax.axis_index("core"), dev, lax.axis_index("z"))
    ]
    field = state.reshape(3, RPB, NZ)
    speed = courant.reshape(RPB, NK)
    sy, sz, line = sines(NY), sines(NZ), line_table()
    syh, syl = halves(sy)
    szp = paired(sz)
    kh, kl = halves(line)
    triple = np.concatenate([kh, kh, kl], axis=1)
    th, tl = np.ascontiguousarray(kh.T), np.ascontiguousarray(kl.T)
    lamx = eigen(NX).astype(np.float32)[:, None]
    mu = (eigen(NY)[:, None] + eigen(NZ)[None, :]).astype(np.float32)

    (blocks,) = call(
        shell_kernel,
        [((3, NJ, NI // 4, NK), f32)],
        flags,
        field.reshape(3, NJ, NI, NK),
        far=1,
        scratch=[pltpu.SemaphoreType.DMA],
    )
    across = [(place_of(0, *q), place_of(1, *q)) for q in chips()]
    blocks = lax.ppermute(blocks.reshape(3, SB, NK), ALL, across)

    sd, sr, rd, rr, rb = (
        v.reshape(1, SB) for v in (shell_dest, shell_row, return_dest, return_row, return_block)
    )
    place, rows, merged = call(
        route_kernel,
        [((SLOTS, SB), bf16), ((BRICKS, NZ), f32), ((2 * NK, 2 * NZ), bf16)],
        flags,
        sd,
        sr,
        remesh,
        sz.astype(np.float32),
        fetch=True,
    )
    turned, gather, codes, last, lead = call(
        ready_kernel,
        [
            ((3, RPB, NZ), f32),
            ((SLOTS, RPB), bf16, "home"),
            ((TARGETS, NZ), f32, "home"),
            ((896, NK), f32, "home"),
            ((896, NK), f32, "home"),
        ],
        flags,
        field,
        speed,
        szp,
        rd,
        rr,
        rb,
        fetch=True,
    )
    blocks, turned = lax.optimization_barrier((blocks, turned))
    (bundle,) = call(
        bucket_kernel, [((BRICKS * CHUNK, NZ), f32)], flags, blocks, rows, place, merged
    )
    bundle, last, lead = lax.optimization_barrier((bundle, last, lead))
    bundle = lax.all_to_all(bundle.reshape(BRICKS, CHUNK, 1, NZ), DEV, 0, 0, tiled=True)
    ahead = [(d, (d + 1) % BRICKS) for d in range(BRICKS)]
    up = lax.ppermute(last, ALL, ahead)
    down = lax.ppermute(lead, ALL, [(b, a) for a, b in ahead])
    bundle, up, down = lax.optimization_barrier((bundle, up, down))
    planes, outgoing, kept = call(
        forward_kernel,
        [((3, 4, NY, NZ), f32), ((3 * NY, NZ), f32), ((3 * NY, NZ), f32)],
        flags,
        bundle.reshape(BRICKS * CHUNK, NZ),
        turned,
        syh,
        syl,
        mu,
    )
    swap = [(0, 1), (1, 0)]
    same = ("y", "z", "x")
    incoming = lax.ppermute(outgoing, "core", swap)
    share, joint = call(
        reduce_kernel,
        [((CHIPS * 12, NZ), f32), ((3 * HALF, NZ), f32)],
        flags,
        incoming,
        kept,
        mu,
    )
    joined = lax.ppermute(joint, "core", swap)
    share = lax.all_to_all(share.reshape(CHIPS, 3, 4, NZ), same, 0, 0, tiled=True)
    (solved,) = call(
        line_kernel,
        [((CHIPS * 12, NZ), f32)],
        flags,
        share.reshape(CHIPS * 12, NZ),
        triple,
        th,
        tl,
        lamx,
        mu,
    )
    own = lax.all_to_all(solved.reshape(CHIPS, 3, 4, NZ), same, 0, 0, tiled=True)
    own = own.reshape(CHIPS * 12, NZ)
    other = lax.ppermute(own, "core", swap)
    halo = pltpu.VMEM((896, NK), f32)
    send, result, edge, layer = call(
        inverse_kernel,
        [
            ((TARGETS * BACK, NZ), f32),
            ((3, RPB, NZ), f32, "raw"),
            ((3, NJ, 8, NK), f32, "raw"),
            ((3, NJ, NK), f32, "raw"),
        ],
        flags,
        planes,
        joint,
        joined,
        own,
        other,
        gather,
        codes,
        szp,
        syh,
        syl,
        mu,
        field,
        speed,
        up,
        down,
        far=4,
        scratch=[
            pltpu.VMEM((3, RPB, NZ), f32),
            pltpu.VMEM((3, NJ, 8, NK), f32),
            pltpu.VMEM((3, NJ, NK), f32),
            pltpu.VMEM((3, RPB, NK), f32),
            pltpu.VMEM((RPB, NK), f32),
            halo,
            halo,
            pltpu.SemaphoreType.DMA((11,)),
        ],
    )
    returned = lax.all_to_all(
        send.reshape(TARGETS, BACK, 1, NZ), ("y", "x", "core"), 0, 0, tiled=True
    )
    sums = call(
        cell_kernel, [((3 * NJ, NZ), f32)] * CZ, flags, returned.reshape(TARGETS * BACK, NZ)
    )
    parts = []
    for k in (0, 1, 3, 2):
        pairs = [
            (place_of(1, y, z, x, c), place_of(0, y, (z + k) % CZ, x, c)) for y, z, x, c in chips()
        ]
        parts.append(lax.ppermute(sums[k], ALL, pairs))
    (result,) = call(
        close_kernel,
        [((3, NJ, NI, NZ), f32, "raw")],
        flags,
        result.reshape(3, NJ, NI, NZ),
        edge,
        layer,
        remesh,
        *parts,
        alias=True,
        scratch=[pltpu.VMEM((3, NJ, 8, NZ), f32), pltpu.SemaphoreType.DMA],
    )
    return result.reshape(1, 3, RPB * NZ)


def solution(mesh):
    fine = Mesh(mesh.devices.reshape(2, CY, CZ, CX, CC), ALL)
    placed = (
        P("grp", None, DEV),
        P(DEV),
        P(),
        P(DEV, None),
        P(DEV),
        P(DEV, None),
        P(DEV),
        P(DEV),
    )
    return jax.shard_map(
        on_device, mesh=fine, in_specs=placed, out_specs=P("grp", None, DEV), check_vma=False
    )
```

```python
import jax
import jax.numpy as jnp
import ml_dtypes
import numpy as np
from jax import lax
from jax.experimental import pallas as pl
from jax.experimental.pallas import tpu as pltpu
from jax.sharding import Mesh
from jax.sharding import PartitionSpec as P

NX, NY, NZ = 512, 256, 128
NI, NK = 64, 128
NJ = 16
CY, CZ, CX, CC = 4, 4, 4, 2
BRICKS = 128
CHIPS = 64
HALF = 128
CAP = 4
SB = 256
RPB = 1024
TARGETS = CY * CX * CC
GROUP = CZ * CAP
SLOTS = BRICKS * CAP
CHUNK = 3 * CAP + 1
BACK = 3 * GROUP + 1
DEV = ("y", "z", "x", "core")
ALL = ("grp",) + DEV

viscosity = 0.2
coupling = 1.0
f32 = jnp.float32
bf16 = jnp.bfloat16
i32 = jnp.int32
highest = lax.Precision.HIGHEST
NT = (((1,), (1,)), ((), ()))


def sines(length):
    counts = np.arange(length) + 1
    phase = counts[:, None] * counts[None, :] % (2 * (length + 1))
    return np.sin(np.pi * phase / (length + 1))


def eigen(length):
    counts = np.arange(length) + 1.0
    return 4.0 * np.sin(0.5 * np.pi * counts / (length + 1)) ** 2


def halves(table):
    table = table.astype(np.float32)
    high = table.astype(ml_dtypes.bfloat16)
    low = (table - high.astype(np.float32)).astype(ml_dtypes.bfloat16)
    return high, low


def paired(table):
    high, low = halves(table)
    return np.block([[high, low], [high, np.zeros_like(low)]]).astype(ml_dtypes.bfloat16)


def line_table():
    plane = 8 * (np.arange(CHIPS) + 1)
    phase = (np.arange(NX) + 1)[:, None] * plane[None, :] % (2 * (NX + 1))
    return np.sin(np.pi * phase / (NX + 1))


def iota(shape, axis):
    return lax.broadcasted_iota(i32, shape, axis)


def split(value):
    high = value.astype(bf16)
    return high, (value - high.astype(f32)).astype(bf16)


def mm(a, b):
    return jnp.dot(a, b, preferred_element_type=f32)


def lanes_paired(value):
    return jnp.concatenate(split(value), axis=1)


def fold(value):
    half = value.shape[1] // 2
    return value[:, :half] + value[:, half:]


def pick(onehot, value):
    return fold(mm(onehot, lanes_paired(value)))


def times_paired(value, table):
    return fold(mm(lanes_paired(value), table))


def table_times(high, low, value):
    vh, vl = split(value)
    return mm(high, vh) + mm(high, vl) + mm(low, vh)


def exact(a, b, dims=(((1,), (0,)), ((), ()))):
    return lax.dot_general(a, b, dims, precision=highest, preferred_element_type=f32)


def onehot(condition):
    return jnp.where(condition, 1.0, 0.0).astype(bf16)


def ranks(matches):
    size = matches.shape[1]
    before = onehot(iota((size, size), 0) < iota((size, size), 1))
    counts = mm(matches.astype(bf16), before)
    return jnp.sum(matches * counts, axis=0, keepdims=True).astype(i32)


def owners(owner):
    core = owner & (CC - 1)
    x = (owner >> 1) & (CX - 1)
    z = (owner >> 3) & (CZ - 1)
    lane = z * CAP + ranks(jnp.where(iota((BRICKS, SB), 0) == owner, 1.0, 0.0))
    return owner >> 5, z, x, core, lane


def route_kernel(flags, sd, sr, remesh, sz, place, codes, merged):
    bricks = iota((BRICKS, SB), 0)
    matches = jnp.where(bricks == sd[...], 1.0, 0.0)
    rank = ranks(matches)
    place[...] = onehot(iota((SLOTS, SB), 0) == rank * BRICKS + sd[...])
    tagged = jnp.where(bricks == rank, (sr[...] + 1).astype(f32), 0.0)
    codes[...] = exact(matches, tagged, NT)
    high, low = split(exact(remesh[...], sz[...]))
    merged[...] = jnp.concatenate(
        [
            jnp.concatenate([high, low], axis=1),
            jnp.concatenate([high, jnp.zeros_like(low)], axis=1),
        ],
        axis=0,
    )


def ready_kernel(
    flags, state, speed, sz, rd, rr, rb, out, gather, spots, codes, last, lead
):
    @pl.when(flags[0] == 0)
    def _():
        for c in range(3):
            last[c * 256 : (c + 1) * 256, :] = state[c, 768:, :]
            lead[c * 256 : (c + 1) * 256, :] = state[c, :256, :]
        last[768:, :] = speed[896:, :]
        lead[768:, :] = speed[:128, :]

    @pl.when(flags[0] != 0)
    def _():
        for c in range(3):
            out[c] = times_paired(state[c], sz[...])
        y, z, x, core, lane = owners(rd[...])
        target = (y * CX + x) * CC + core
        spots[...] = onehot(iota((SLOTS, SB), 0) == lane * TARGETS + target)
        gather[...] = jnp.where(iota((RPB, SB), 0) == rr[...], 1.0, 0.0).T.astype(bf16)
        code = ((z - flags[3]) & (CZ - 1)) * NJ + rb[...] + 1
        tagged = jnp.where(iota((NZ, SB), 0) == lane, code.astype(f32), 0.0)
        sent = onehot(iota((TARGETS, SB), 0) == target)
        codes[...] = lax.dot_general(sent, tagged.astype(bf16), NT, preferred_element_type=f32)


def near_step(field, speed):
    rows = speed.shape[0]
    centre = field[128 : 128 + rows]
    transport = (
        8.0 * (field[192 : 192 + rows] - field[64 : 64 + rows])
        - (field[256 : 256 + rows] - field[:rows])
    ) / 12.0
    place = iota((rows, NK), 0) & (NI - 1)
    above = jnp.where(place == NI - 1, 0.0, pltpu.roll(centre, rows - 1, 0))
    below = jnp.where(place == 0, 0.0, pltpu.roll(centre, 1, 0))
    return centre - speed * transport + viscosity * (above - 2.0 * centre + below)


def shell_kernel(flags, state, out, sem):
    @pl.when(flags[0] == 0)
    def _():
        copy = pltpu.make_async_copy(state.at[:, :, pl.ds(NI - NI // 4, NI // 4), :], out, sem)
        copy.start()
        copy.wait()


def bucket_kernel(flags, blocks, codes, place, merged, out, held, sems):
    @pl.when(flags[0] != 0)
    def _():
        slots = [pick(place[...], times_paired(blocks[c], merged[...])) for c in range(3)]
        part = BRICKS // 4
        copies = []
        for i in range(4):
            first = i * part * CHUNK
            held[pl.ds(first + 3 * CAP, part, stride=CHUNK), :] = codes[i * part : (i + 1) * part]
            for c in range(3):
                for rank in range(CAP):
                    row = rank * BRICKS + i * part
                    held[pl.ds(first + c * CAP + rank, part, stride=CHUNK), :] = slots[c][
                        row : row + part
                    ]
            block = pl.ds(first, part * CHUNK)
            copies.append(pltpu.make_async_copy(held.at[block, :], out.at[block, :], sems.at[i]))
            copies[-1].start()
        for copy in copies:
            copy.wait()


def weights(beta):
    outer = beta * beta - 2.0
    g12 = 1.0 / outer
    g13 = g12 / beta
    g11 = (beta * beta - 1.0) * g13
    return g11, g12, g13


def forward_kernel(flags, received, work, syh, syl, mu, planes, outgoing, kept):
    @pl.when(flags[0] != 0)
    def _():
        beta = mu[...] + 2.0
        g11, g12, g13 = weights(beta)
        first = flags[1] == 0
        codes = received[pl.ds(3 * CAP, BRICKS, stride=CHUNK), :].T
        landing = jnp.concatenate([codes[r : r + 1, :] for r in range(CAP)], axis=1).astype(i32)
        spread = onehot(iota((RPB, SLOTS), 0) == landing - 1)
        for c in range(3):
            rows = jnp.concatenate(
                [received[pl.ds(c * CAP + r, BRICKS, stride=CHUNK), :] for r in range(CAP)], axis=0
            )
            field = (pick(spread, rows) + work[c]) * (4.0 / ((NY + 1) * (NZ + 1)))
            field = jnp.concatenate([field[p * NY : (p + 1) * NY] for p in range(4)], axis=1)
            field = table_times(syh[...], syl[...], field)
            f0, f1, f2, f3 = (field[:, p * NZ : (p + 1) * NZ] for p in range(4))
            for p, plane in enumerate((f0, f1, f2, f3)):
                planes[c, p] = plane
            low = g11 * f0 + g12 * f1 + g13 * f2
            high = f3 + g13 * f0 + g12 * f1 + g11 * f2
            for kind, value in enumerate((low, high)):
                block = slice((kind * 3 + c) * HALF, (kind * 3 + c + 1) * HALF)
                outgoing[block, :] = jnp.where(first, value[HALF:], value[:HALF])
                kept[block, :] = jnp.where(first, value[:HALF], value[HALF:])


def reduce_kernel(flags, incoming, kept, mu, out, joint):
    @pl.when(flags[0] != 0)
    def _():
        beta = mu[pl.ds(pl.multiple_of(flags[1] * HALF, HALF), HALF), :] + 2.0
        g11, _, g13 = weights(beta)
        ratio = g13 / (beta - 2.0 * g11)
        first = flags[1] == 0
        for c in range(3):
            low, high = (slice((k * 3 + c) * HALF, (k * 3 + c + 1) * HALF) for k in range(2))
            low0, low1 = (
                jnp.where(first, kept[low, :], incoming[low, :]),
                jnp.where(first, incoming[low, :], kept[low, :]),
            )
            high0, high1 = (
                jnp.where(first, kept[high, :], incoming[high, :]),
                jnp.where(first, incoming[high, :], kept[high, :]),
            )
            middle = high0 + low1
            joint[c * HALF : (c + 1) * HALF, :] = middle
            for kind, value in enumerate((low0 + ratio * middle, high1 + ratio * middle)):
                for i in range(2):
                    out[pl.ds(c * 4 + kind * 2 + i, CHIPS, stride=12), :] = value[
                        i * CHIPS : (i + 1) * CHIPS
                    ]


def line_kernel(flags, received, spread, th, tl, lamx, mu, out):
    @pl.when(flags[0] != 0)
    def _():
        def part(c, kind, i):
            return received[pl.ds(c * 4 + kind * 2 + i, CHIPS, stride=12), :]

        place = iota((CHIPS, NZ), 0)
        rows = []
        for c in range(3):
            for i in range(2):
                ahead = jnp.where(
                    place == CHIPS - 1, 0.0, pltpu.roll(part(c, 0, i), CHIPS - 1, 0)
                )
                rows.append(part(c, 1, i) + ahead)
        high, low = split(jnp.concatenate(rows, axis=1))
        modes = mm(spread[...], jnp.concatenate([high, low, high], axis=0))
        factors = []
        for i in range(2):
            row = mu[pl.ds(flags[1] * HALF + i * CHIPS + (flags[2] >> 1), 1), :]
            factors.append((2.0 / (NX + 1)) / (lamx[...] + row))
        modes = modes * jnp.concatenate(factors * 3, axis=1)
        solved = table_times(th[...], tl[...], modes)
        for c in range(3):
            for i in range(2):
                j = c * 2 + i
                value = solved[:, j * NZ : (j + 1) * NZ]
                behind = jnp.where(place == 0, 0.0, pltpu.roll(value, 1, 0))
                out[pl.ds(c * 4 + i, CHIPS, stride=12), :] = behind
                out[pl.ds(c * 4 + 2 + i, CHIPS, stride=12), :] = value


def inverse_kernel(
    flags,
    planes,
    joint,
    joined,
    own,
    other,
    gather,
    spots,
    codes,
    sz,
    syh,
    syl,
    mu,
    state,
    speed,
    up,
    down,
    send,
    out,
    edge_home,
    layer_home,
    held,
    edge,
    layer,
    sems,
):
    @pl.when(flags[0] == 0)
    def _():
        wide = jnp.concatenate([up[768:896, :], speed[...], down[768:896, :]], axis=0)
        copies = []
        for c in range(3):
            block = slice(c * 256, (c + 1) * 256)
            field = jnp.concatenate([up[block, :], state[c], down[block, :]], axis=0)
            field = near_step(near_step(field, wide), speed[...])
            held[c] = field
            copies.append(pltpu.make_async_copy(held.at[c], out.at[c], sems.at[6 + c]))
            copies[-1].start()
            edge[c] = field.reshape(NJ, NI, NK)[:, NI - 8 :, :]
            layer[c] = state[c, pl.ds(NI - 1, NJ, stride=NI), :]
        for a, b, i in ((edge, edge_home, 9), (layer, layer_home, 10)):
            copies.append(pltpu.make_async_copy(a, b, sems.at[i]))
            copies[-1].start()
        for copy in copies:
            copy.wait()

    @pl.when(flags[0] != 0)
    def _():
        beta = mu[...] + 2.0
        g11, g12, g13 = weights(beta)
        inv = 1.0 / (beta - 2.0 * g11)
        first = flags[1] == 0
        inside = jnp.where(flags[2] == BRICKS - 1, 0.0, 1.0)
        potentials = []
        for c in range(3):

            def full(pieces):
                a, b = pieces(own, joint), pieces(other, joined)
                return jnp.concatenate([jnp.where(first, a, b), jnp.where(first, b, a)], axis=0)

            def solved(kind):
                return full(
                    lambda ref, _: jnp.concatenate(
                        [
                            ref[pl.ds(c * 4 + kind * 2 + i, CHIPS, stride=12), :]
                            for i in range(2)
                        ],
                        axis=0,
                    )
                )

            before, after = solved(0), solved(1)
            middle = full(lambda _, ref: ref[c * HALF : (c + 1) * HALF, :])
            middle = (middle + g13 * (before + after)) * inv
            left = jnp.where(first, before, middle)
            right = jnp.where(first, middle, after)
            f0, f1, f2, f3 = (planes[c, p] for p in range(4))
            u0 = g11 * (f0 + left) + g12 * f1 + g13 * (f2 + right)
            u1 = g12 * (f0 + left + beta * f1 + f2 + right)
            u2 = g13 * (f0 + left) + g12 * f1 + g11 * (f2 + right)
            stack = [u0, u1, u2, right]
            if c:
                stack = [left] + stack + [(beta * right - u2 - f3) * inside]
            field = table_times(syh[...], syl[...], jnp.concatenate(stack, axis=1))
            field = jnp.concatenate(
                [field[:, p * NZ : (p + 1) * NZ] for p in range(len(stack))], axis=0
            )
            potentials.append(times_paired(field, sz[...]))
        rows = iota((RPB, NZ), 0) & (NY - 1)
        lanes = iota((RPB, NZ), 1)

        def dy(field):
            upper = jnp.where(rows == NY - 1, 0.0, pltpu.roll(field, RPB - 1, 0))
            lower = jnp.where(rows == 0, 0.0, pltpu.roll(field, 1, 0))
            return (upper - lower) * 0.5

        def dz(field):
            upper = jnp.where(lanes == NZ - 1, 0.0, pltpu.roll(field, NZ - 1, 1))
            lower = jnp.where(lanes == 0, 0.0, pltpu.roll(field, 1, 1))
            return (upper - lower) * 0.5

        def dx(field):
            return (field[2 * NY : 2 * NY + RPB] - field[:RPB]) * 0.5

        px, py, pz = potentials[0], potentials[1][NY : NY + RPB], potentials[2][NY : NY + RPB]
        velocity = (
            dy(pz) - dz(py),
            dz(px) - dx(potentials[2]),
            dx(potentials[1]) - dy(px),
        )
        copies = []
        for c in range(3):
            held[c] = velocity[c]
            copies.append(pltpu.make_async_copy(held.at[c], out.at[c], sems.at[c]))
            copies[-1].start()
        send[pl.ds(3 * GROUP, TARGETS, stride=BACK), :] = codes[...]
        for c in range(3):
            rows_out = pick(spots[...], pick(gather[...], velocity[c]))
            for lane in range(GROUP):
                send[pl.ds(c * GROUP + lane, TARGETS, stride=BACK), :] = rows_out[
                    lane * TARGETS : (lane + 1) * TARGETS
                ]
        for copy in copies:
            copy.wait()


def cell_kernel(flags, received, *outs):
    @pl.when(flags[0] != 0)
    def _():
        codes = received[pl.ds(3 * GROUP, TARGETS, stride=BACK), :].astype(bf16)
        codes = mm(codes, onehot(iota((NZ, SLOTS), 0) == (iota((NZ, SLOTS), 1) >> 5)))
        mine = iota((TARGETS, SLOTS), 0) == (iota((TARGETS, SLOTS), 1) & (TARGETS - 1))
        code = jnp.sum(jnp.where(mine, codes, 0.0), axis=0, keepdims=True).astype(i32)
        cells = onehot(iota((CZ * NJ, SLOTS), 0) == code - 1)
        for c in range(3):
            rows = jnp.concatenate(
                [
                    received[pl.ds(c * GROUP + lane, TARGETS, stride=BACK), :]
                    for lane in range(GROUP)
                ],
                axis=0,
            )
            sums = pick(cells, rows)
            for k in range(CZ):
                outs[k][c * NJ : (c + 1) * NJ, :] = sums[k * NJ : (k + 1) * NJ]


def close_kernel(flags, field, edge, layer, remesh, b0, b1, b2, b3, out, slab, sem):
    @pl.when(flags[0] == 0)
    def _():
        total = exact((b0[...] + b1[...]) + (b2[...] + b3[...]), remesh[...], NT)
        first = [total[c * NJ : (c + 1) * NJ] for c in range(3)]
        second = [layer[c] for c in range(3)]
        for c in range(3):
            d, e = (c + 1) % 3, (c + 2) % 3
            cross = first[d] * second[e] - first[e] * second[d]
            slab[c] = edge[c]
            slab[c, :, 7, :] = edge[c, :, 7, :] + coupling * cross
        copy = pltpu.make_async_copy(slab, out.at[:, :, pl.ds(NI - 8, 8), :], sem)
        copy.start()
        copy.wait()


def call(kernel, outs, flags, *args, fetch=False, alias=False, far=0, scratch=()):
    args = [jnp.asarray(a) for a in args]
    spaces = [
        pltpu.HBM if fetch or (alias and i == 0) or i >= len(args) - far else pltpu.VMEM
        for i in range(len(args))
    ]
    homes = [len(o) > 2 for o in outs]
    staged = [i for i, o in enumerate(outs) if o[2:] == ("home",)]
    loads = [pltpu.VMEM(a.shape, a.dtype) for a in args] if fetch else []
    stores = [pltpu.VMEM(*outs[i][:2]) for i in staged]
    sems = [pltpu.SemaphoreType.DMA((len(loads) + len(stores),))] if loads or stores else []

    def body(*refs):
        flags, refs = [ref[0] for ref in refs[:4]], refs[4:]
        given, made = list(refs[: len(args)]), list(refs[len(args) : len(args) + len(outs)])
        rest = refs[len(args) + len(outs) :]
        held, kept = rest[: len(loads)], rest[len(loads) : len(loads) + len(stores)]
        own = rest[len(loads) + len(stores) + len(sems) :]
        if sems:
            sem = rest[len(loads) + len(stores)]
        copies = [
            pltpu.make_async_copy(a, b, sem.at[i]) for i, (a, b) in enumerate(zip(given, held))
        ]
        for copy in copies:
            copy.start()
        for copy in copies:
            copy.wait()
        homes_out = [made[i] for i in staged]
        for i, ref in zip(staged, kept):
            made[i] = ref
        kernel(flags, *(held if fetch else given), *made, *own)
        copies = [
            pltpu.make_async_copy(a, b, sem.at[len(loads) + i])
            for i, (a, b) in enumerate(zip(kept, homes_out))
        ]
        for copy in copies:
            copy.start()
        for copy in copies:
            copy.wait()

    return pl.pallas_call(
        body,
        out_shape=[(pltpu.HBM if home else pltpu.VMEM)(*o[:2]) for o, home in zip(outs, homes)],
        in_specs=[pl.BlockSpec(memory_space=pltpu.SMEM)] * 4
        + [pl.BlockSpec(memory_space=space) for space in spaces],
        out_specs=[
            pl.BlockSpec(memory_space=pltpu.HBM if home else pltpu.VMEM) for home in homes
        ],
        scratch_shapes=loads + stores + sems + list(scratch),
        input_output_aliases={4: 0} if alias else {},
        compiler_params=pltpu.CompilerParams(vmem_limit_bytes=24 << 20),
    )(
        *flags,
        *[
            a if alias and i == 0 else pltpu.with_memory_space_constraint(a, space)
            for i, (a, space) in enumerate(zip(args, spaces))
        ],
    )


def place_of(g, y, z, x, c):
    return (((g * CY + y) * CZ + z) * CX + x) * CC + c


def chips():
    return [
        (y, z, x, c) for y in range(CY) for z in range(CZ) for x in range(CX) for c in range(CC)
    ]


def on_device(state, courant, remesh, shell_dest, shell_row, return_dest, return_row, return_block):
    dev = lax.axis_index(DEV)
    flags = [
        v.astype(i32).reshape(1)
        for v in (lax.axis_index("grp"), lax.axis_index("core"), dev, lax.axis_index("z"))
    ]
    field = state.reshape(3, RPB, NZ)
    speed = courant.reshape(RPB, NK)
    sy, sz, line = sines(NY), sines(NZ), line_table()
    syh, syl = halves(sy)
    szp = paired(sz)
    kh, kl = halves(line)
    triple = np.concatenate([kh, kh, kl], axis=1)
    th, tl = np.ascontiguousarray(kh.T), np.ascontiguousarray(kl.T)
    lamx = eigen(NX).astype(np.float32)[:, None]
    mu = (eigen(NY)[:, None] + eigen(NZ)[None, :]).astype(np.float32)

    (blocks,) = call(
        shell_kernel,
        [((3, NJ, NI // 4, NK), f32)],
        flags,
        field.reshape(3, NJ, NI, NK),
        far=1,
        scratch=[pltpu.SemaphoreType.DMA],
    )
    across = [(place_of(0, *q), place_of(1, *q)) for q in chips()]
    blocks = lax.ppermute(blocks.reshape(3, SB, NK), ALL, across)

    sd, sr, rd, rr, rb = (
        v.reshape(1, SB) for v in (shell_dest, shell_row, return_dest, return_row, return_block)
    )
    place, rows, merged = call(
        route_kernel,
        [((SLOTS, SB), bf16), ((BRICKS, NZ), f32), ((2 * NK, 2 * NZ), bf16)],
        flags,
        sd,
        sr,
        remesh,
        sz.astype(np.float32),
        fetch=True,
    )
    turned, gather, spots, codes, last, lead = call(
        ready_kernel,
        [
            ((3, RPB, NZ), f32),
            ((SB, RPB), bf16, "home"),
        ((SLOTS, SB), bf16, "home"),
            ((TARGETS, NZ), f32, "home"),
            ((896, NK), f32, "home"),
            ((896, NK), f32, "home"),
        ],
        flags,
        field,
        speed,
        szp,
        rd,
        rr,
        rb,
        fetch=True,
    )
    blocks, turned = lax.optimization_barrier((blocks, turned))
    (bundle,) = call(
        bucket_kernel,
        [((BRICKS * CHUNK, NZ), f32, "raw")],
        flags,
        blocks,
        rows,
        place,
        merged,
        scratch=[pltpu.VMEM((BRICKS * CHUNK, NZ), f32), pltpu.SemaphoreType.DMA((4,))],
    )
    bundle, last, lead = lax.optimization_barrier((bundle, last, lead))
    bundle = lax.all_to_all(bundle.reshape(BRICKS, CHUNK, 1, NZ), DEV, 0, 0, tiled=True)
    ahead = [(d, (d + 1) % BRICKS) for d in range(BRICKS)]
    up = lax.ppermute(last, ALL, ahead)
    down = lax.ppermute(lead, ALL, [(b, a) for a, b in ahead])
    bundle, up, down = lax.optimization_barrier((bundle, up, down))
    planes, outgoing, kept = call(
        forward_kernel,
        [((3, 4, NY, NZ), f32), ((3 * NY, NZ), f32), ((3 * NY, NZ), f32)],
        flags,
        bundle.reshape(BRICKS * CHUNK, NZ),
        turned,
        syh,
        syl,
        mu,
    )
    swap = [(0, 1), (1, 0)]
    same = ("y", "z", "x")
    incoming = lax.ppermute(outgoing, "core", swap)
    share, joint = call(
        reduce_kernel,
        [((CHIPS * 12, NZ), f32), ((3 * HALF, NZ), f32)],
        flags,
        incoming,
        kept,
        mu,
    )
    joined = lax.ppermute(joint, "core", swap)
    share = lax.all_to_all(share.reshape(CHIPS, 3, 4, NZ), same, 0, 0, tiled=True)
    (solved,) = call(
        line_kernel,
        [((CHIPS * 12, NZ), f32)],
        flags,
        share.reshape(CHIPS * 12, NZ),
        triple,
        th,
        tl,
        lamx,
        mu,
    )
    own = lax.all_to_all(solved.reshape(CHIPS, 3, 4, NZ), same, 0, 0, tiled=True)
    own = own.reshape(CHIPS * 12, NZ)
    other = lax.ppermute(own, "core", swap)
    send, result, edge, layer = call(
        inverse_kernel,
        [
            ((TARGETS * BACK, NZ), f32),
            ((3, RPB, NZ), f32, "raw"),
            ((3, NJ, 8, NK), f32, "raw"),
            ((3, NJ, NK), f32, "raw"),
        ],
        flags,
        planes,
        joint,
        joined,
        own,
        other,
        gather,
        spots,
        codes,
        szp,
        syh,
        syl,
        mu,
        field,
        speed,
        up,
        down,
        scratch=[
            pltpu.VMEM((3, RPB, NZ), f32),
            pltpu.VMEM((3, NJ, 8, NK), f32),
            pltpu.VMEM((3, NJ, NK), f32),
            pltpu.SemaphoreType.DMA((11,)),
        ],
    )
    returned = lax.all_to_all(
        send.reshape(TARGETS, BACK, 1, NZ), ("y", "x", "core"), 0, 0, tiled=True
    )
    sums = call(
        cell_kernel, [((3 * NJ, NZ), f32)] * CZ, flags, returned.reshape(TARGETS * BACK, NZ)
    )
    parts = []
    for k in (0, 1, 3, 2):
        pairs = [
            (place_of(1, y, z, x, c), place_of(0, y, (z + k) % CZ, x, c)) for y, z, x, c in chips()
        ]
        parts.append(lax.ppermute(sums[k], ALL, pairs))
    (result,) = call(
        close_kernel,
        [((3, NJ, NI, NZ), f32, "raw")],
        flags,
        result.reshape(3, NJ, NI, NZ),
        edge,
        layer,
        remesh,
        *parts,
        alias=True,
        scratch=[pltpu.VMEM((3, NJ, 8, NZ), f32), pltpu.SemaphoreType.DMA],
    )
    return result.reshape(1, 3, RPB * NZ)


def solution(mesh):
    fine = Mesh(mesh.devices.reshape(2, CY, CZ, CX, CC), ALL)
    placed = (
        P("grp", None, DEV),
        P(DEV),
        P(),
        P(DEV, None),
        P(DEV),
        P(DEV, None),
        P(DEV),
        P(DEV),
    )
    return jax.shard_map(
        on_device, mesh=fine, in_specs=placed, out_specs=P("grp", None, DEV), check_vma=False
    )
```

```python
import jax
import jax.numpy as jnp
import ml_dtypes
import numpy as np
from jax import lax
from jax.experimental import pallas as pl
from jax.experimental.pallas import tpu as pltpu
from jax.sharding import Mesh
from jax.sharding import PartitionSpec as P

NX, NY, NZ = 512, 256, 128
NI, NK = 64, 128
NJ = 16
CY, CZ, CX, CC = 4, 4, 4, 2
BRICKS = 128
CHIPS = 64
HALF = 128
CAP = 4
SB = 256
RPB = 1024
TARGETS = CY * CX * CC
GROUP = CZ * CAP
SLOTS = BRICKS * CAP
CHUNK = 3 * CAP + 1
BACK = 3 * GROUP + 1
DEV = ("y", "z", "x", "core")
ALL = ("grp",) + DEV

viscosity = 0.2
coupling = 1.0
f32 = jnp.float32
bf16 = jnp.bfloat16
i32 = jnp.int32
highest = lax.Precision.HIGHEST
NT = (((1,), (1,)), ((), ()))


def sines(length):
    counts = np.arange(length) + 1
    phase = counts[:, None] * counts[None, :] % (2 * (length + 1))
    return np.sin(np.pi * phase / (length + 1))


def eigen(length):
    counts = np.arange(length) + 1.0
    return 4.0 * np.sin(0.5 * np.pi * counts / (length + 1)) ** 2


def halves(table):
    table = table.astype(np.float32)
    high = table.astype(ml_dtypes.bfloat16)
    low = (table - high.astype(np.float32)).astype(ml_dtypes.bfloat16)
    return high, low


def paired(table):
    high, low = halves(table)
    return np.block([[high, low], [high, np.zeros_like(low)]]).astype(ml_dtypes.bfloat16)


def line_table():
    plane = 8 * (np.arange(CHIPS) + 1)
    phase = (np.arange(NX) + 1)[:, None] * plane[None, :] % (2 * (NX + 1))
    return np.sin(np.pi * phase / (NX + 1))


def iota(shape, axis):
    return lax.broadcasted_iota(i32, shape, axis)


def split(value):
    high = value.astype(bf16)
    return high, (value - high.astype(f32)).astype(bf16)


def mm(a, b):
    return jnp.dot(a, b, preferred_element_type=f32)


def lanes_paired(value):
    return jnp.concatenate(split(value), axis=1)


def fold(value):
    half = value.shape[1] // 2
    return value[:, :half] + value[:, half:]


def pick(onehot, value):
    return fold(mm(onehot, lanes_paired(value)))


def times_paired(value, table):
    return fold(mm(lanes_paired(value), table))


def table_times(high, low, value):
    vh, vl = split(value)
    return mm(high, vh) + mm(high, vl) + mm(low, vh)


def exact(a, b, dims=(((1,), (0,)), ((), ()))):
    return lax.dot_general(a, b, dims, precision=highest, preferred_element_type=f32)


def onehot(condition):
    return jnp.where(condition, 1.0, 0.0).astype(bf16)


def ranks(matches):
    size = matches.shape[1]
    before = onehot(iota((size, size), 0) < iota((size, size), 1))
    counts = mm(matches.astype(bf16), before)
    return jnp.sum(matches * counts, axis=0, keepdims=True).astype(i32)


def owners(owner):
    core = owner & (CC - 1)
    x = (owner >> 1) & (CX - 1)
    z = (owner >> 3) & (CZ - 1)
    lane = z * CAP + ranks(jnp.where(iota((BRICKS, SB), 0) == owner, 1.0, 0.0))
    return owner >> 5, z, x, core, lane


def route_kernel(flags, sd, sr, remesh, sz, place, codes, merged):
    bricks = iota((BRICKS, SB), 0)
    matches = jnp.where(bricks == sd[...], 1.0, 0.0)
    rank = ranks(matches)
    place[...] = onehot(iota((SLOTS, SB), 0) == rank * BRICKS + sd[...])
    tagged = jnp.where(bricks == rank, (sr[...] + 1).astype(f32), 0.0)
    codes[...] = exact(matches, tagged, NT)
    high, low = split(exact(remesh[...], sz[...]))
    merged[...] = jnp.concatenate(
        [
            jnp.concatenate([high, low], axis=1),
            jnp.concatenate([high, jnp.zeros_like(low)], axis=1),
        ],
        axis=0,
    )


def ready_kernel(
    flags, state, speed, sz, rd, rr, rb, out, gather, codes, last, lead
):
    @pl.when(flags[0] == 0)
    def _():
        for c in range(3):
            last[c * 256 : (c + 1) * 256, :] = state[c, 768:, :]
            lead[c * 256 : (c + 1) * 256, :] = state[c, :256, :]
        last[768:, :] = speed[896:, :]
        lead[768:, :] = speed[:128, :]

    @pl.when(flags[0] != 0)
    def _():
        for c in range(3):
            out[c] = times_paired(state[c], sz[...])
        y, z, x, core, lane = owners(rd[...])
        target = (y * CX + x) * CC + core
        gather[...] = lax.dot_general(
            onehot(iota((SLOTS, SB), 0) == lane * TARGETS + target),
            onehot(iota((RPB, SB), 0) == rr[...]),
            NT,
            preferred_element_type=f32,
        ).astype(bf16)
        code = ((z - flags[3]) & (CZ - 1)) * NJ + rb[...] + 1
        tagged = jnp.where(iota((NZ, SB), 0) == lane, code.astype(f32), 0.0)
        sent = onehot(iota((TARGETS, SB), 0) == target)
        codes[...] = lax.dot_general(sent, tagged.astype(bf16), NT, preferred_element_type=f32)


def near_step(field, speed):
    rows = speed.shape[0]
    centre = field[128 : 128 + rows]
    transport = (
        8.0 * (field[192 : 192 + rows] - field[64 : 64 + rows])
        - (field[256 : 256 + rows] - field[:rows])
    ) / 12.0
    place = iota((rows, NK), 0) & (NI - 1)
    above = jnp.where(place == NI - 1, 0.0, pltpu.roll(centre, rows - 1, 0))
    below = jnp.where(place == 0, 0.0, pltpu.roll(centre, 1, 0))
    return centre - speed * transport + viscosity * (above - 2.0 * centre + below)


def shell_kernel(flags, state, out, sem):
    @pl.when(flags[0] == 0)
    def _():
        copy = pltpu.make_async_copy(state.at[:, :, pl.ds(NI - NI // 4, NI // 4), :], out, sem)
        copy.start()
        copy.wait()


def bucket_kernel(flags, blocks, codes, place, merged, out, held, sems):
    @pl.when(flags[0] == 0)
    def _():
        slots = [pick(place[...], times_paired(blocks[c], merged[...])) for c in range(3)]
        part = BRICKS // 4
        copies = []
        for i in range(4):
            first = i * part * CHUNK
            held[pl.ds(first + 3 * CAP, part, stride=CHUNK), :] = codes[i * part : (i + 1) * part]
            for c in range(3):
                for rank in range(CAP):
                    row = rank * BRICKS + i * part
                    held[pl.ds(first + c * CAP + rank, part, stride=CHUNK), :] = slots[c][
                        row : row + part
                    ]
            block = pl.ds(first, part * CHUNK)
            target = out.at[pl.ds(BRICKS * CHUNK + first, part * CHUNK), :]
            copies.append(pltpu.make_async_copy(held.at[block, :], target, sems.at[i]))
            copies[-1].start()
        for copy in copies:
            copy.wait()


def weights(beta):
    outer = beta * beta - 2.0
    g12 = 1.0 / outer
    g13 = g12 / beta
    g11 = (beta * beta - 1.0) * g13
    return g11, g12, g13


def forward_kernel(flags, received, work, syh, syl, mu, planes, outgoing, kept):
    @pl.when(flags[0] != 0)
    def _():
        beta = mu[...] + 2.0
        g11, g12, g13 = weights(beta)
        first = flags[1] == 0
        codes = received[pl.ds(3 * CAP, BRICKS, stride=CHUNK), :].T
        landing = jnp.concatenate([codes[r : r + 1, :] for r in range(CAP)], axis=1).astype(i32)
        spread = onehot(iota((RPB, SLOTS), 0) == landing - 1)
        for c in range(3):
            rows = jnp.concatenate(
                [received[pl.ds(c * CAP + r, BRICKS, stride=CHUNK), :] for r in range(CAP)], axis=0
            )
            field = (pick(spread, rows) + work[c]) * (4.0 / ((NY + 1) * (NZ + 1)))
            field = jnp.concatenate([field[p * NY : (p + 1) * NY] for p in range(4)], axis=1)
            field = table_times(syh[...], syl[...], field)
            f0, f1, f2, f3 = (field[:, p * NZ : (p + 1) * NZ] for p in range(4))
            for p, plane in enumerate((f0, f1, f2, f3)):
                planes[c, p] = plane
            low = g11 * f0 + g12 * f1 + g13 * f2
            high = f3 + g13 * f0 + g12 * f1 + g11 * f2
            for kind, value in enumerate((low, high)):
                block = slice((kind * 3 + c) * HALF, (kind * 3 + c + 1) * HALF)
                outgoing[block, :] = jnp.where(first, value[HALF:], value[:HALF])
                kept[block, :] = jnp.where(first, value[:HALF], value[HALF:])


def reduce_kernel(flags, incoming, kept, mu, out, joint):
    @pl.when(flags[0] != 0)
    def _():
        beta = mu[pl.ds(pl.multiple_of(flags[1] * HALF, HALF), HALF), :] + 2.0
        g11, _, g13 = weights(beta)
        ratio = g13 / (beta - 2.0 * g11)
        first = flags[1] == 0
        for c in range(3):
            low, high = (slice((k * 3 + c) * HALF, (k * 3 + c + 1) * HALF) for k in range(2))
            low0, low1 = (
                jnp.where(first, kept[low, :], incoming[low, :]),
                jnp.where(first, incoming[low, :], kept[low, :]),
            )
            high0, high1 = (
                jnp.where(first, kept[high, :], incoming[high, :]),
                jnp.where(first, incoming[high, :], kept[high, :]),
            )
            middle = high0 + low1
            joint[c * HALF : (c + 1) * HALF, :] = middle
            for kind, value in enumerate((low0 + ratio * middle, high1 + ratio * middle)):
                for i in range(2):
                    out[pl.ds(c * 4 + kind * 2 + i, CHIPS, stride=12), :] = value[
                        i * CHIPS : (i + 1) * CHIPS
                    ]


def line_kernel(flags, received, spread, th, tl, lamx, mu, out):
    @pl.when(flags[0] != 0)
    def _():
        def part(c, kind, i):
            return received[pl.ds(c * 4 + kind * 2 + i, CHIPS, stride=12), :]

        place = iota((CHIPS, NZ), 0)
        rows = []
        for c in range(3):
            for i in range(2):
                ahead = jnp.where(
                    place == CHIPS - 1, 0.0, pltpu.roll(part(c, 0, i), CHIPS - 1, 0)
                )
                rows.append(part(c, 1, i) + ahead)
        high, low = split(jnp.concatenate(rows, axis=1))
        modes = mm(spread[...], jnp.concatenate([high, low, high], axis=0))
        factors = []
        for i in range(2):
            row = mu[pl.ds(flags[1] * HALF + i * CHIPS + (flags[2] >> 1), 1), :]
            factors.append((2.0 / (NX + 1)) / (lamx[...] + row))
        modes = modes * jnp.concatenate(factors * 3, axis=1)
        solved = table_times(th[...], tl[...], modes)
        for c in range(3):
            for i in range(2):
                j = c * 2 + i
                value = solved[:, j * NZ : (j + 1) * NZ]
                behind = jnp.where(place == 0, 0.0, pltpu.roll(value, 1, 0))
                out[pl.ds(c * 4 + i, CHIPS, stride=12), :] = behind
                out[pl.ds(c * 4 + 2 + i, CHIPS, stride=12), :] = value


def inverse_kernel(
    flags,
    planes,
    joint,
    joined,
    own,
    other,
    gather,
    codes,
    sz,
    syh,
    syl,
    mu,
    state,
    speed,
    up,
    down,
    send,
    out,
    edge_home,
    layer_home,
    held,
    edge,
    layer,
    sems,
):
    @pl.when(flags[0] == 0)
    def _():
        wide = jnp.concatenate([up[768:896, :], speed[...], down[768:896, :]], axis=0)
        copies = []
        for c in range(3):
            block = slice(c * 256, (c + 1) * 256)
            field = jnp.concatenate([up[block, :], state[c], down[block, :]], axis=0)
            field = near_step(near_step(field, wide), speed[...])
            held[c] = field
            copies.append(pltpu.make_async_copy(held.at[c], out.at[c], sems.at[6 + c]))
            copies[-1].start()
            edge[c] = field.reshape(NJ, NI, NK)[:, NI - 8 :, :]
            layer[c] = state[c, pl.ds(NI - 1, NJ, stride=NI), :]
        for a, b, i in ((edge, edge_home, 9), (layer, layer_home, 10)):
            copies.append(pltpu.make_async_copy(a, b, sems.at[i]))
            copies[-1].start()
        for copy in copies:
            copy.wait()

    @pl.when(flags[0] != 0)
    def _():
        beta = mu[...] + 2.0
        g11, g12, g13 = weights(beta)
        inv = 1.0 / (beta - 2.0 * g11)
        first = flags[1] == 0
        inside = jnp.where(flags[2] == BRICKS - 1, 0.0, 1.0)
        potentials = []
        for c in range(3):

            def full(pieces):
                a, b = pieces(own, joint), pieces(other, joined)
                return jnp.concatenate([jnp.where(first, a, b), jnp.where(first, b, a)], axis=0)

            def solved(kind):
                return full(
                    lambda ref, _: jnp.concatenate(
                        [
                            ref[pl.ds(c * 4 + kind * 2 + i, CHIPS, stride=12), :]
                            for i in range(2)
                        ],
                        axis=0,
                    )
                )

            before, after = solved(0), solved(1)
            middle = full(lambda _, ref: ref[c * HALF : (c + 1) * HALF, :])
            middle = (middle + g13 * (before + after)) * inv
            left = jnp.where(first, before, middle)
            right = jnp.where(first, middle, after)
            f0, f1, f2, f3 = (planes[c, p] for p in range(4))
            u0 = g11 * (f0 + left) + g12 * f1 + g13 * (f2 + right)
            u1 = g12 * (f0 + left + beta * f1 + f2 + right)
            u2 = g13 * (f0 + left) + g12 * f1 + g11 * (f2 + right)
            stack = [u0, u1, u2, right]
            if c:
                stack = [left] + stack + [(beta * right - u2 - f3) * inside]
            field = table_times(syh[...], syl[...], jnp.concatenate(stack, axis=1))
            field = jnp.concatenate(
                [field[:, p * NZ : (p + 1) * NZ] for p in range(len(stack))], axis=0
            )
            potentials.append(times_paired(field, sz[...]))
        rows = iota((RPB, NZ), 0) & (NY - 1)
        lanes = iota((RPB, NZ), 1)

        def dy(field):
            upper = jnp.where(rows == NY - 1, 0.0, pltpu.roll(field, RPB - 1, 0))
            lower = jnp.where(rows == 0, 0.0, pltpu.roll(field, 1, 0))
            return (upper - lower) * 0.5

        def dz(field):
            upper = jnp.where(lanes == NZ - 1, 0.0, pltpu.roll(field, NZ - 1, 1))
            lower = jnp.where(lanes == 0, 0.0, pltpu.roll(field, 1, 1))
            return (upper - lower) * 0.5

        def dx(field):
            return (field[2 * NY : 2 * NY + RPB] - field[:RPB]) * 0.5

        px, py, pz = potentials[0], potentials[1][NY : NY + RPB], potentials[2][NY : NY + RPB]
        velocity = (
            dy(pz) - dz(py),
            dz(px) - dx(potentials[2]),
            dx(potentials[1]) - dy(px),
        )
        copies = []
        for c in range(3):
            held[c] = velocity[c]
            copies.append(pltpu.make_async_copy(held.at[c], out.at[c], sems.at[c]))
            copies[-1].start()
        send[pl.ds(3 * GROUP, TARGETS, stride=BACK), :] = codes[...]
        for c in range(3):
            rows_out = pick(gather[...], velocity[c])
            for lane in range(GROUP):
                send[pl.ds(c * GROUP + lane, TARGETS, stride=BACK), :] = rows_out[
                    lane * TARGETS : (lane + 1) * TARGETS
                ]
        for copy in copies:
            copy.wait()


def cell_kernel(flags, received, *outs):
    @pl.when(flags[0] != 0)
    def _():
        codes = received[pl.ds(3 * GROUP, TARGETS, stride=BACK), :].astype(bf16)
        codes = mm(codes, onehot(iota((NZ, SLOTS), 0) == (iota((NZ, SLOTS), 1) >> 5)))
        mine = iota((TARGETS, SLOTS), 0) == (iota((TARGETS, SLOTS), 1) & (TARGETS - 1))
        code = jnp.sum(jnp.where(mine, codes, 0.0), axis=0, keepdims=True).astype(i32)
        cells = onehot(iota((CZ * NJ, SLOTS), 0) == code - 1)
        for c in range(3):
            rows = jnp.concatenate(
                [
                    received[pl.ds(c * GROUP + lane, TARGETS, stride=BACK), :]
                    for lane in range(GROUP)
                ],
                axis=0,
            )
            sums = pick(cells, rows)
            for k in range(CZ):
                outs[k][c * NJ : (c + 1) * NJ, :] = sums[k * NJ : (k + 1) * NJ]


def close_kernel(flags, field, edge, layer, remesh, b0, b1, b2, b3, out, slab, sem):
    @pl.when(flags[0] == 0)
    def _():
        total = exact((b0[...] + b1[...]) + (b2[...] + b3[...]), remesh[...], NT)
        first = [total[c * NJ : (c + 1) * NJ] for c in range(3)]
        second = [layer[c] for c in range(3)]
        for c in range(3):
            d, e = (c + 1) % 3, (c + 2) % 3
            cross = first[d] * second[e] - first[e] * second[d]
            slab[c] = edge[c]
            slab[c, :, 7, :] = edge[c, :, 7, :] + coupling * cross
        copy = pltpu.make_async_copy(slab, out.at[:, :, pl.ds(NI - 8, 8), :], sem)
        copy.start()
        copy.wait()


def call(kernel, outs, flags, *args, fetch=False, alias=False, far=0, scratch=()):
    args = [jnp.asarray(a) for a in args]
    spaces = [
        pltpu.HBM if fetch or (alias and i == 0) or i >= len(args) - far else pltpu.VMEM
        for i in range(len(args))
    ]
    homes = [len(o) > 2 for o in outs]
    staged = [i for i, o in enumerate(outs) if o[2:] == ("home",)]
    loads = [pltpu.VMEM(a.shape, a.dtype) for a in args] if fetch else []
    stores = [pltpu.VMEM(*outs[i][:2]) for i in staged]
    sems = [pltpu.SemaphoreType.DMA((len(loads) + len(stores),))] if loads or stores else []

    def body(*refs):
        flags, refs = [ref[0] for ref in refs[:4]], refs[4:]
        given, made = list(refs[: len(args)]), list(refs[len(args) : len(args) + len(outs)])
        rest = refs[len(args) + len(outs) :]
        held, kept = rest[: len(loads)], rest[len(loads) : len(loads) + len(stores)]
        own = rest[len(loads) + len(stores) + len(sems) :]
        if sems:
            sem = rest[len(loads) + len(stores)]
        copies = [
            pltpu.make_async_copy(a, b, sem.at[i]) for i, (a, b) in enumerate(zip(given, held))
        ]
        for copy in copies:
            copy.start()
        for copy in copies:
            copy.wait()
        homes_out = [made[i] for i in staged]
        for i, ref in zip(staged, kept):
            made[i] = ref
        kernel(flags, *(held if fetch else given), *made, *own)
        copies = [
            pltpu.make_async_copy(a, b, sem.at[len(loads) + i])
            for i, (a, b) in enumerate(zip(kept, homes_out))
        ]
        for copy in copies:
            copy.start()
        for copy in copies:
            copy.wait()

    return pl.pallas_call(
        body,
        out_shape=[(pltpu.HBM if home else pltpu.VMEM)(*o[:2]) for o, home in zip(outs, homes)],
        in_specs=[pl.BlockSpec(memory_space=pltpu.SMEM)] * 4
        + [pl.BlockSpec(memory_space=space) for space in spaces],
        out_specs=[
            pl.BlockSpec(memory_space=pltpu.HBM if home else pltpu.VMEM) for home in homes
        ],
        scratch_shapes=loads + stores + sems + list(scratch),
        input_output_aliases={4: 0} if alias else {},
        compiler_params=pltpu.CompilerParams(vmem_limit_bytes=24 << 20),
    )(
        *flags,
        *[
            a if alias and i == 0 else pltpu.with_memory_space_constraint(a, space)
            for i, (a, space) in enumerate(zip(args, spaces))
        ],
    )


def place_of(g, y, z, x, c):
    return (((g * CY + y) * CZ + z) * CX + x) * CC + c


def chips():
    return [
        (y, z, x, c) for y in range(CY) for z in range(CZ) for x in range(CX) for c in range(CC)
    ]


def on_device(state, courant, remesh, shell_dest, shell_row, return_dest, return_row, return_block):
    dev = lax.axis_index(DEV)
    flags = [
        v.astype(i32).reshape(1)
        for v in (lax.axis_index("grp"), lax.axis_index("core"), dev, lax.axis_index("z"))
    ]
    field = state.reshape(3, RPB, NZ)
    speed = courant.reshape(RPB, NK)
    sy, sz, line = sines(NY), sines(NZ), line_table()
    syh, syl = halves(sy)
    szp = paired(sz)
    kh, kl = halves(line)
    triple = np.concatenate([kh, kh, kl], axis=1)
    th, tl = np.ascontiguousarray(kh.T), np.ascontiguousarray(kl.T)
    lamx = eigen(NX).astype(np.float32)[:, None]
    mu = (eigen(NY)[:, None] + eigen(NZ)[None, :]).astype(np.float32)

    (blocks,) = call(
        shell_kernel,
        [((3, NJ, NI // 4, NK), f32)],
        flags,
        field.reshape(3, NJ, NI, NK),
        far=1,
        scratch=[pltpu.SemaphoreType.DMA],
    )
    sd, sr, rd, rr, rb = (
        v.reshape(1, SB) for v in (shell_dest, shell_row, return_dest, return_row, return_block)
    )
    place, rows, merged = call(
        route_kernel,
        [((SLOTS, SB), bf16), ((BRICKS, NZ), f32), ((2 * NK, 2 * NZ), bf16)],
        flags,
        sd,
        sr,
        remesh,
        sz.astype(np.float32),
        fetch=True,
    )
    (bundle,) = call(
        bucket_kernel,
        [((2 * BRICKS * CHUNK, NZ), f32, "raw")],
        flags,
        blocks.reshape(3, SB, NK),
        rows,
        place,
        merged,
        scratch=[pltpu.VMEM((BRICKS * CHUNK, NZ), f32), pltpu.SemaphoreType.DMA((4,))],
    )
    bundle = lax.all_to_all(bundle.reshape(2 * BRICKS, CHUNK, 1, NZ), ALL, 0, 0, tiled=True)
    turned, gather, codes, last, lead = call(
        ready_kernel,
        [
            ((3, RPB, NZ), f32),
            ((SLOTS, RPB), bf16, "home"),
            ((TARGETS, NZ), f32, "home"),
            ((896, NK), f32, "home"),
            ((896, NK), f32, "home"),
        ],
        flags,
        field,
        speed,
        szp,
        rd,
        rr,
        rb,
        fetch=True,
    )
    ahead = [(d, (d + 1) % BRICKS) for d in range(BRICKS)]
    up = lax.ppermute(last, ALL, ahead)
    down = lax.ppermute(lead, ALL, [(b, a) for a, b in ahead])
    bundle, up, down = lax.optimization_barrier((bundle, up, down))
    planes, outgoing, kept = call(
        forward_kernel,
        [((3, 4, NY, NZ), f32), ((3 * NY, NZ), f32), ((3 * NY, NZ), f32)],
        flags,
        bundle.reshape(2 * BRICKS * CHUNK, NZ),
        turned,
        syh,
        syl,
        mu,
    )
    swap = [(0, 1), (1, 0)]
    same = ("y", "z", "x")
    incoming = lax.ppermute(outgoing, "core", swap)
    share, joint = call(
        reduce_kernel,
        [((CHIPS * 12, NZ), f32), ((3 * HALF, NZ), f32)],
        flags,
        incoming,
        kept,
        mu,
    )
    joined = lax.ppermute(joint, "core", swap)
    share = lax.all_to_all(share.reshape(CHIPS, 3, 4, NZ), same, 0, 0, tiled=True)
    (solved,) = call(
        line_kernel,
        [((CHIPS * 12, NZ), f32)],
        flags,
        share.reshape(CHIPS * 12, NZ),
        triple,
        th,
        tl,
        lamx,
        mu,
    )
    own = lax.all_to_all(solved.reshape(CHIPS, 3, 4, NZ), same, 0, 0, tiled=True)
    own = own.reshape(CHIPS * 12, NZ)
    other = lax.ppermute(own, "core", swap)
    send, result, edge, layer = call(
        inverse_kernel,
        [
            ((TARGETS * BACK, NZ), f32),
            ((3, RPB, NZ), f32, "raw"),
            ((3, NJ, 8, NK), f32, "raw"),
            ((3, NJ, NK), f32, "raw"),
        ],
        flags,
        planes,
        joint,
        joined,
        own,
        other,
        gather,
        codes,
        szp,
        syh,
        syl,
        mu,
        field,
        speed,
        up,
        down,
        scratch=[
            pltpu.VMEM((3, RPB, NZ), f32),
            pltpu.VMEM((3, NJ, 8, NK), f32),
            pltpu.VMEM((3, NJ, NK), f32),
            pltpu.SemaphoreType.DMA((11,)),
        ],
    )
    returned = lax.all_to_all(
        send.reshape(TARGETS, BACK, 1, NZ), ("y", "x", "core"), 0, 0, tiled=True
    )
    sums = call(
        cell_kernel, [((3 * NJ, NZ), f32)] * CZ, flags, returned.reshape(TARGETS * BACK, NZ)
    )
    parts = []
    for k in (0, 1, 3, 2):
        pairs = [
            (place_of(1, y, z, x, c), place_of(0, y, (z + k) % CZ, x, c)) for y, z, x, c in chips()
        ]
        parts.append(lax.ppermute(sums[k], ALL, pairs))
    (result,) = call(
        close_kernel,
        [((3, NJ, NI, NZ), f32, "raw")],
        flags,
        result.reshape(3, NJ, NI, NZ),
        edge,
        layer,
        remesh,
        *parts,
        alias=True,
        scratch=[pltpu.VMEM((3, NJ, 8, NZ), f32), pltpu.SemaphoreType.DMA],
    )
    return result.reshape(1, 3, RPB * NZ)


def solution(mesh):
    fine = Mesh(mesh.devices.reshape(2, CY, CZ, CX, CC), ALL)
    placed = (
        P("grp", None, DEV),
        P(DEV),
        P(),
        P(DEV, None),
        P(DEV),
        P(DEV, None),
        P(DEV),
        P(DEV),
    )
    return jax.shard_map(
        on_device, mesh=fine, in_specs=placed, out_specs=P("grp", None, DEV), check_vma=False
    )
```

```python
import jax
import jax.numpy as jnp
import ml_dtypes
import numpy as np
from jax import lax
from jax.experimental import pallas as pl
from jax.experimental.pallas import tpu as pltpu
from jax.sharding import Mesh
from jax.sharding import PartitionSpec as P

NX, NY, NZ = 512, 256, 128
NI, NK = 64, 128
NJ = 16
CY, CZ, CX, CC = 4, 4, 4, 2
BRICKS = 128
CHIPS = 64
HALF = 128
CAP = 4
SB = 256
RPB = 1024
TARGETS = CY * CX * CC
GROUP = CZ * CAP
SLOTS = BRICKS * CAP
CHUNK = 3 * CAP + 1
BACK = 3 * GROUP + 1
DEV = ("y", "z", "x", "core")
ALL = ("grp",) + DEV

viscosity = 0.2
coupling = 1.0
f32 = jnp.float32
bf16 = jnp.bfloat16
i32 = jnp.int32
highest = lax.Precision.HIGHEST
NT = (((1,), (1,)), ((), ()))


def sines(length):
    counts = np.arange(length) + 1
    phase = counts[:, None] * counts[None, :] % (2 * (length + 1))
    return np.sin(np.pi * phase / (length + 1))


def eigen(length):
    counts = np.arange(length) + 1.0
    return 4.0 * np.sin(0.5 * np.pi * counts / (length + 1)) ** 2


def halves(table):
    table = table.astype(np.float32)
    high = table.astype(ml_dtypes.bfloat16)
    low = (table - high.astype(np.float32)).astype(ml_dtypes.bfloat16)
    return high, low


def paired(table):
    high, low = halves(table)
    return np.block([[high, low], [high, np.zeros_like(low)]]).astype(ml_dtypes.bfloat16)


def line_table():
    plane = 8 * (np.arange(CHIPS) + 1)
    phase = (np.arange(NX) + 1)[:, None] * plane[None, :] % (2 * (NX + 1))
    return np.sin(np.pi * phase / (NX + 1))


def iota(shape, axis):
    return lax.broadcasted_iota(i32, shape, axis)


def split(value):
    high = value.astype(bf16)
    return high, (value - high.astype(f32)).astype(bf16)


def mm(a, b):
    return jnp.dot(a, b, preferred_element_type=f32)


def lanes_paired(value):
    return jnp.concatenate(split(value), axis=1)


def fold(value):
    half = value.shape[1] // 2
    return value[:, :half] + value[:, half:]


def pick(onehot, value):
    return fold(mm(onehot, lanes_paired(value)))


def times_paired(value, table):
    return fold(mm(lanes_paired(value), table))


def table_times(high, low, value):
    vh, vl = split(value)
    return mm(high, vh) + mm(high, vl) + mm(low, vh)


def exact(a, b, dims=(((1,), (0,)), ((), ()))):
    return lax.dot_general(a, b, dims, precision=highest, preferred_element_type=f32)


def onehot(condition):
    return jnp.where(condition, 1.0, 0.0).astype(bf16)


def ranks(matches):
    size = matches.shape[1]
    before = onehot(iota((size, size), 0) < iota((size, size), 1))
    counts = mm(matches.astype(bf16), before)
    return jnp.sum(matches * counts, axis=0, keepdims=True).astype(i32)


def owners(owner):
    core = owner & (CC - 1)
    x = (owner >> 1) & (CX - 1)
    z = (owner >> 3) & (CZ - 1)
    lane = z * CAP + ranks(jnp.where(iota((BRICKS, SB), 0) == owner, 1.0, 0.0))
    return owner >> 5, z, x, core, lane


def route_kernel(flags, sd, sr, remesh, sz, place, codes, merged):
    bricks = iota((BRICKS, SB), 0)
    matches = jnp.where(bricks == sd[...], 1.0, 0.0)
    rank = ranks(matches)
    place[...] = onehot(iota((SLOTS, SB), 0) == rank * BRICKS + sd[...])
    tagged = jnp.where(bricks == rank, (sr[...] + 1).astype(f32), 0.0)
    codes[...] = exact(matches, tagged, NT)
    high, low = split(exact(remesh[...], sz[...]))
    merged[...] = jnp.concatenate(
        [
            jnp.concatenate([high, low], axis=1),
            jnp.concatenate([high, jnp.zeros_like(low)], axis=1),
        ],
        axis=0,
    )


def ready_kernel(
    flags, state, speed, sz, rd, rr, rb, out, gather, codes, last, lead
):
    @pl.when(flags[0] == 0)
    def _():
        for c in range(3):
            last[c * 256 : (c + 1) * 256, :] = state[c, 768:, :]
            lead[c * 256 : (c + 1) * 256, :] = state[c, :256, :]
        last[768:, :] = speed[896:, :]
        lead[768:, :] = speed[:128, :]

    @pl.when(flags[0] != 0)
    def _():
        for c in range(3):
            out[c] = times_paired(state[c], sz[...])
        y, z, x, core, lane = owners(rd[...])
        target = (y * CX + x) * CC + core
        gather[...] = lax.dot_general(
            onehot(iota((SLOTS, SB), 0) == lane * TARGETS + target),
            onehot(iota((RPB, SB), 0) == rr[...]),
            NT,
            preferred_element_type=f32,
        ).astype(bf16)
        code = ((z - flags[3]) & (CZ - 1)) * NJ + rb[...] + 1
        tagged = jnp.where(iota((NZ, SB), 0) == lane, code.astype(f32), 0.0)
        sent = onehot(iota((TARGETS, SB), 0) == target)
        codes[...] = lax.dot_general(sent, tagged.astype(bf16), NT, preferred_element_type=f32)


def near_step(field, speed):
    rows = speed.shape[0]
    centre = field[128 : 128 + rows]
    transport = (
        8.0 * (field[192 : 192 + rows] - field[64 : 64 + rows])
        - (field[256 : 256 + rows] - field[:rows])
    ) / 12.0
    place = iota((rows, NK), 0) & (NI - 1)
    above = jnp.where(place == NI - 1, 0.0, pltpu.roll(centre, rows - 1, 0))
    below = jnp.where(place == 0, 0.0, pltpu.roll(centre, 1, 0))
    return centre - speed * transport + viscosity * (above - 2.0 * centre + below)


def shell_kernel(flags, state, out, sem):
    @pl.when(flags[0] == 0)
    def _():
        copy = pltpu.make_async_copy(state.at[:, :, pl.ds(NI - NI // 4, NI // 4), :], out, sem)
        copy.start()
        copy.wait()


def bucket_kernel(flags, blocks, codes, place, merged, out, held, sems):
    @pl.when(flags[0] == 0)
    def _():
        slots = [pick(place[...], times_paired(blocks[c], merged[...])) for c in range(3)]
        part = BRICKS // 4
        copies = []
        for i in range(4):
            first = i * part * CHUNK
            held[pl.ds(first + 3 * CAP, part, stride=CHUNK), :] = codes[i * part : (i + 1) * part]
            for c in range(3):
                for rank in range(CAP):
                    row = rank * BRICKS + i * part
                    held[pl.ds(first + c * CAP + rank, part, stride=CHUNK), :] = slots[c][
                        row : row + part
                    ]
            block = pl.ds(first, part * CHUNK)
            target = out.at[pl.ds(BRICKS * CHUNK + first, part * CHUNK), :]
            copies.append(pltpu.make_async_copy(held.at[block, :], target, sems.at[i]))
            copies[-1].start()
        for copy in copies:
            copy.wait()


def weights(beta):
    outer = beta * beta - 2.0
    g12 = 1.0 / outer
    g13 = g12 / beta
    g11 = (beta * beta - 1.0) * g13
    return g11, g12, g13


def forward_kernel(
    flags, received, work, mu, high_home, low_home, planes, outgoing, kept, syh, syl, sems
):
    @pl.when(flags[0] != 0)
    def _():
        copies = [
            pltpu.make_async_copy(high_home, syh, sems.at[0]),
            pltpu.make_async_copy(low_home, syl, sems.at[1]),
        ]
        for copy in copies:
            copy.start()
        beta = mu[...] + 2.0
        g11, g12, g13 = weights(beta)
        first = flags[1] == 0
        codes = received[pl.ds(3 * CAP, BRICKS, stride=CHUNK), :].T
        landing = jnp.concatenate([codes[r : r + 1, :] for r in range(CAP)], axis=1).astype(i32)
        spread = onehot(iota((RPB, SLOTS), 0) == landing - 1)
        for c in range(3):
            rows = jnp.concatenate(
                [received[pl.ds(c * CAP + r, BRICKS, stride=CHUNK), :] for r in range(CAP)], axis=0
            )
            field = (pick(spread, rows) + work[c]) * (4.0 / ((NY + 1) * (NZ + 1)))
            field = jnp.concatenate([field[p * NY : (p + 1) * NY] for p in range(4)], axis=1)
            if c == 0:
                for copy in copies:
                    copy.wait()
            field = table_times(syh[...], syl[...], field)
            f0, f1, f2, f3 = (field[:, p * NZ : (p + 1) * NZ] for p in range(4))
            for p, plane in enumerate((f0, f1, f2, f3)):
                planes[c, p] = plane
            low = g11 * f0 + g12 * f1 + g13 * f2
            high = f3 + g13 * f0 + g12 * f1 + g11 * f2
            for kind, value in enumerate((low, high)):
                block = slice((kind * 3 + c) * HALF, (kind * 3 + c + 1) * HALF)
                outgoing[block, :] = jnp.where(first, value[HALF:], value[:HALF])
                kept[block, :] = jnp.where(first, value[:HALF], value[HALF:])


def reduce_kernel(flags, incoming, kept, mu, out, joint):
    @pl.when(flags[0] != 0)
    def _():
        beta = mu[pl.ds(pl.multiple_of(flags[1] * HALF, HALF), HALF), :] + 2.0
        g11, _, g13 = weights(beta)
        ratio = g13 / (beta - 2.0 * g11)
        first = flags[1] == 0
        for c in range(3):
            low, high = (slice((k * 3 + c) * HALF, (k * 3 + c + 1) * HALF) for k in range(2))
            low0, low1 = (
                jnp.where(first, kept[low, :], incoming[low, :]),
                jnp.where(first, incoming[low, :], kept[low, :]),
            )
            high0, high1 = (
                jnp.where(first, kept[high, :], incoming[high, :]),
                jnp.where(first, incoming[high, :], kept[high, :]),
            )
            middle = high0 + low1
            joint[c * HALF : (c + 1) * HALF, :] = middle
            for kind, value in enumerate((low0 + ratio * middle, high1 + ratio * middle)):
                for i in range(2):
                    out[pl.ds(c * 4 + kind * 2 + i, CHIPS, stride=12), :] = value[
                        i * CHIPS : (i + 1) * CHIPS
                    ]


def line_kernel(flags, received, spread, th, tl, lamx, mu, out):
    @pl.when(flags[0] != 0)
    def _():
        def part(c, kind, i):
            return received[pl.ds(c * 4 + kind * 2 + i, CHIPS, stride=12), :]

        place = iota((CHIPS, NZ), 0)
        rows = []
        for c in range(3):
            for i in range(2):
                ahead = jnp.where(
                    place == CHIPS - 1, 0.0, pltpu.roll(part(c, 0, i), CHIPS - 1, 0)
                )
                rows.append(part(c, 1, i) + ahead)
        high, low = split(jnp.concatenate(rows, axis=1))
        modes = mm(spread[...], jnp.concatenate([high, low, high], axis=0))
        factors = []
        for i in range(2):
            row = mu[pl.ds(flags[1] * HALF + i * CHIPS + (flags[2] >> 1), 1), :]
            factors.append((2.0 / (NX + 1)) / (lamx[...] + row))
        modes = modes * jnp.concatenate(factors * 3, axis=1)
        solved = table_times(th[...], tl[...], modes)
        for c in range(3):
            for i in range(2):
                j = c * 2 + i
                value = solved[:, j * NZ : (j + 1) * NZ]
                behind = jnp.where(place == 0, 0.0, pltpu.roll(value, 1, 0))
                out[pl.ds(c * 4 + i, CHIPS, stride=12), :] = behind
                out[pl.ds(c * 4 + 2 + i, CHIPS, stride=12), :] = value


def inverse_kernel(
    flags,
    planes,
    joint,
    joined,
    own,
    other,
    gather,
    codes,
    sz,
    syh,
    syl,
    mu,
    state,
    speed,
    up,
    down,
    send,
    out,
    edge_home,
    layer_home,
    held,
    edge,
    layer,
    sems,
):
    @pl.when(flags[0] == 0)
    def _():
        wide = jnp.concatenate([up[768:896, :], speed[...], down[768:896, :]], axis=0)
        copies = []
        for c in range(3):
            block = slice(c * 256, (c + 1) * 256)
            field = jnp.concatenate([up[block, :], state[c], down[block, :]], axis=0)
            field = near_step(near_step(field, wide), speed[...])
            held[c] = field
            copies.append(pltpu.make_async_copy(held.at[c], out.at[c], sems.at[6 + c]))
            copies[-1].start()
            edge[c] = field.reshape(NJ, NI, NK)[:, NI - 8 :, :]
            layer[c] = state[c, pl.ds(NI - 1, NJ, stride=NI), :]
        for a, b, i in ((edge, edge_home, 9), (layer, layer_home, 10)):
            copies.append(pltpu.make_async_copy(a, b, sems.at[i]))
            copies[-1].start()
        for copy in copies:
            copy.wait()

    @pl.when(flags[0] != 0)
    def _():
        beta = mu[...] + 2.0
        g11, g12, g13 = weights(beta)
        inv = 1.0 / (beta - 2.0 * g11)
        first = flags[1] == 0
        inside = jnp.where(flags[2] == BRICKS - 1, 0.0, 1.0)
        potentials = []
        for c in range(3):

            def full(pieces):
                a, b = pieces(own, joint), pieces(other, joined)
                return jnp.concatenate([jnp.where(first, a, b), jnp.where(first, b, a)], axis=0)

            def solved(kind):
                return full(
                    lambda ref, _: jnp.concatenate(
                        [
                            ref[pl.ds(c * 4 + kind * 2 + i, CHIPS, stride=12), :]
                            for i in range(2)
                        ],
                        axis=0,
                    )
                )

            before, after = solved(0), solved(1)
            middle = full(lambda _, ref: ref[c * HALF : (c + 1) * HALF, :])
            middle = (middle + g13 * (before + after)) * inv
            left = jnp.where(first, before, middle)
            right = jnp.where(first, middle, after)
            f0, f1, f2, f3 = (planes[c, p] for p in range(4))
            u0 = g11 * (f0 + left) + g12 * f1 + g13 * (f2 + right)
            u1 = g12 * (f0 + left + beta * f1 + f2 + right)
            u2 = g13 * (f0 + left) + g12 * f1 + g11 * (f2 + right)
            stack = [u0, u1, u2, right]
            if c:
                stack = [left] + stack + [(beta * right - u2 - f3) * inside]
            field = table_times(syh[...], syl[...], jnp.concatenate(stack, axis=1))
            field = jnp.concatenate(
                [field[:, p * NZ : (p + 1) * NZ] for p in range(len(stack))], axis=0
            )
            potentials.append(times_paired(field, sz[...]))
        rows = iota((RPB, NZ), 0) & (NY - 1)
        lanes = iota((RPB, NZ), 1)

        def dy(field):
            upper = jnp.where(rows == NY - 1, 0.0, pltpu.roll(field, RPB - 1, 0))
            lower = jnp.where(rows == 0, 0.0, pltpu.roll(field, 1, 0))
            return (upper - lower) * 0.5

        def dz(field):
            upper = jnp.where(lanes == NZ - 1, 0.0, pltpu.roll(field, NZ - 1, 1))
            lower = jnp.where(lanes == 0, 0.0, pltpu.roll(field, 1, 1))
            return (upper - lower) * 0.5

        def dx(field):
            return (field[2 * NY : 2 * NY + RPB] - field[:RPB]) * 0.5

        px, py, pz = potentials[0], potentials[1][NY : NY + RPB], potentials[2][NY : NY + RPB]
        velocity = (
            dy(pz) - dz(py),
            dz(px) - dx(potentials[2]),
            dx(potentials[1]) - dy(px),
        )
        copies = []
        for c in range(3):
            held[c] = velocity[c]
            copies.append(pltpu.make_async_copy(held.at[c], out.at[c], sems.at[c]))
            copies[-1].start()
        send[pl.ds(3 * GROUP, TARGETS, stride=BACK), :] = codes[...]
        for c in range(3):
            rows_out = pick(gather[...], velocity[c])
            for lane in range(GROUP):
                send[pl.ds(c * GROUP + lane, TARGETS, stride=BACK), :] = rows_out[
                    lane * TARGETS : (lane + 1) * TARGETS
                ]
        for copy in copies:
            copy.wait()


def cell_kernel(flags, received, *outs):
    @pl.when(flags[0] != 0)
    def _():
        codes = received[pl.ds(3 * GROUP, TARGETS, stride=BACK), :].astype(bf16)
        codes = mm(codes, onehot(iota((NZ, SLOTS), 0) == (iota((NZ, SLOTS), 1) >> 5)))
        mine = iota((TARGETS, SLOTS), 0) == (iota((TARGETS, SLOTS), 1) & (TARGETS - 1))
        code = jnp.sum(jnp.where(mine, codes, 0.0), axis=0, keepdims=True).astype(i32)
        cells = onehot(iota((CZ * NJ, SLOTS), 0) == code - 1)
        for c in range(3):
            rows = jnp.concatenate(
                [
                    received[pl.ds(c * GROUP + lane, TARGETS, stride=BACK), :]
                    for lane in range(GROUP)
                ],
                axis=0,
            )
            sums = pick(cells, rows)
            for k in range(CZ):
                outs[k][c * NJ : (c + 1) * NJ, :] = sums[k * NJ : (k + 1) * NJ]


def close_kernel(flags, field, edge, layer, remesh, b0, b1, b2, b3, out, slab, sem):
    @pl.when(flags[0] == 0)
    def _():
        total = exact((b0[...] + b1[...]) + (b2[...] + b3[...]), remesh[...], NT)
        first = [total[c * NJ : (c + 1) * NJ] for c in range(3)]
        second = [layer[c] for c in range(3)]
        for c in range(3):
            d, e = (c + 1) % 3, (c + 2) % 3
            cross = first[d] * second[e] - first[e] * second[d]
            slab[c] = edge[c]
            slab[c, :, 7, :] = edge[c, :, 7, :] + coupling * cross
        copy = pltpu.make_async_copy(slab, out.at[:, :, pl.ds(NI - 8, 8), :], sem)
        copy.start()
        copy.wait()


def call(kernel, outs, flags, *args, fetch=False, alias=False, far=0, scratch=()):
    args = [jnp.asarray(a) for a in args]
    spaces = [
        pltpu.HBM if fetch or (alias and i == 0) or i >= len(args) - far else pltpu.VMEM
        for i in range(len(args))
    ]
    homes = [len(o) > 2 for o in outs]
    staged = [i for i, o in enumerate(outs) if o[2:] == ("home",)]
    loads = [pltpu.VMEM(a.shape, a.dtype) for a in args] if fetch else []
    stores = [pltpu.VMEM(*outs[i][:2]) for i in staged]
    sems = [pltpu.SemaphoreType.DMA((len(loads) + len(stores),))] if loads or stores else []

    def body(*refs):
        flags, refs = [ref[0] for ref in refs[:4]], refs[4:]
        given, made = list(refs[: len(args)]), list(refs[len(args) : len(args) + len(outs)])
        rest = refs[len(args) + len(outs) :]
        held, kept = rest[: len(loads)], rest[len(loads) : len(loads) + len(stores)]
        own = rest[len(loads) + len(stores) + len(sems) :]
        if sems:
            sem = rest[len(loads) + len(stores)]
        copies = [
            pltpu.make_async_copy(a, b, sem.at[i]) for i, (a, b) in enumerate(zip(given, held))
        ]
        for copy in copies:
            copy.start()
        for copy in copies:
            copy.wait()
        homes_out = [made[i] for i in staged]
        for i, ref in zip(staged, kept):
            made[i] = ref
        kernel(flags, *(held if fetch else given), *made, *own)
        copies = [
            pltpu.make_async_copy(a, b, sem.at[len(loads) + i])
            for i, (a, b) in enumerate(zip(kept, homes_out))
        ]
        for copy in copies:
            copy.start()
        for copy in copies:
            copy.wait()

    return pl.pallas_call(
        body,
        out_shape=[(pltpu.HBM if home else pltpu.VMEM)(*o[:2]) for o, home in zip(outs, homes)],
        in_specs=[pl.BlockSpec(memory_space=pltpu.SMEM)] * 4
        + [pl.BlockSpec(memory_space=space) for space in spaces],
        out_specs=[
            pl.BlockSpec(memory_space=pltpu.HBM if home else pltpu.VMEM) for home in homes
        ],
        scratch_shapes=loads + stores + sems + list(scratch),
        input_output_aliases={4: 0} if alias else {},
        compiler_params=pltpu.CompilerParams(vmem_limit_bytes=24 << 20),
    )(
        *flags,
        *[
            a if alias and i == 0 else pltpu.with_memory_space_constraint(a, space)
            for i, (a, space) in enumerate(zip(args, spaces))
        ],
    )


def place_of(g, y, z, x, c):
    return (((g * CY + y) * CZ + z) * CX + x) * CC + c


def chips():
    return [
        (y, z, x, c) for y in range(CY) for z in range(CZ) for x in range(CX) for c in range(CC)
    ]


def on_device(state, courant, remesh, shell_dest, shell_row, return_dest, return_row, return_block):
    dev = lax.axis_index(DEV)
    flags = [
        v.astype(i32).reshape(1)
        for v in (lax.axis_index("grp"), lax.axis_index("core"), dev, lax.axis_index("z"))
    ]
    field = state.reshape(3, RPB, NZ)
    speed = courant.reshape(RPB, NK)
    sy, sz, line = sines(NY), sines(NZ), line_table()
    syh, syl = halves(sy)
    szp = paired(sz)
    kh, kl = halves(line)
    triple = np.concatenate([kh, kh, kl], axis=1)
    th, tl = np.ascontiguousarray(kh.T), np.ascontiguousarray(kl.T)
    lamx = eigen(NX).astype(np.float32)[:, None]
    mu = (eigen(NY)[:, None] + eigen(NZ)[None, :]).astype(np.float32)

    (blocks,) = call(
        shell_kernel,
        [((3, NJ, NI // 4, NK), f32)],
        flags,
        field.reshape(3, NJ, NI, NK),
        far=1,
        scratch=[pltpu.SemaphoreType.DMA],
    )
    sd, sr, rd, rr, rb = (
        v.reshape(1, SB) for v in (shell_dest, shell_row, return_dest, return_row, return_block)
    )
    place, rows, merged = call(
        route_kernel,
        [((SLOTS, SB), bf16), ((BRICKS, NZ), f32), ((2 * NK, 2 * NZ), bf16)],
        flags,
        sd,
        sr,
        remesh,
        sz.astype(np.float32),
        fetch=True,
    )
    (bundle,) = call(
        bucket_kernel,
        [((2 * BRICKS * CHUNK, NZ), f32, "raw")],
        flags,
        blocks.reshape(3, SB, NK),
        rows,
        place,
        merged,
        scratch=[pltpu.VMEM((BRICKS * CHUNK, NZ), f32), pltpu.SemaphoreType.DMA((4,))],
    )
    bundle = lax.all_to_all(bundle.reshape(2 * BRICKS, CHUNK, 1, NZ), ALL, 0, 0, tiled=True)
    turned, gather, codes, last, lead = call(
        ready_kernel,
        [
            ((3, RPB, NZ), f32),
            ((SLOTS, RPB), bf16, "home"),
            ((TARGETS, NZ), f32, "home"),
            ((896, NK), f32, "home"),
            ((896, NK), f32, "home"),
        ],
        flags,
        field,
        speed,
        szp,
        rd,
        rr,
        rb,
        fetch=True,
    )
    ahead = [(d, (d + 1) % BRICKS) for d in range(BRICKS)]
    up = lax.ppermute(last, ALL, ahead)
    down = lax.ppermute(lead, ALL, [(b, a) for a, b in ahead])
    planes, outgoing, kept = call(
        forward_kernel,
        [((3, 4, NY, NZ), f32), ((3 * NY, NZ), f32), ((3 * NY, NZ), f32)],
        flags,
        bundle.reshape(2 * BRICKS * CHUNK, NZ),
        turned,
        mu,
        syh,
        syl,
        far=2,
        scratch=[
            pltpu.VMEM((NY, NY), bf16),
            pltpu.VMEM((NY, NY), bf16),
            pltpu.SemaphoreType.DMA((2,)),
        ],
    )
    swap = [(0, 1), (1, 0)]
    same = ("y", "z", "x")
    incoming = lax.ppermute(outgoing, "core", swap)
    share, joint = call(
        reduce_kernel,
        [((CHIPS * 12, NZ), f32), ((3 * HALF, NZ), f32)],
        flags,
        incoming,
        kept,
        mu,
    )
    joined = lax.ppermute(joint, "core", swap)
    share = lax.all_to_all(share.reshape(CHIPS, 3, 4, NZ), same, 0, 0, tiled=True)
    (solved,) = call(
        line_kernel,
        [((CHIPS * 12, NZ), f32)],
        flags,
        share.reshape(CHIPS * 12, NZ),
        triple,
        th,
        tl,
        lamx,
        mu,
    )
    own = lax.all_to_all(solved.reshape(CHIPS, 3, 4, NZ), same, 0, 0, tiled=True)
    own = own.reshape(CHIPS * 12, NZ)
    other = lax.ppermute(own, "core", swap)
    send, result, edge, layer = call(
        inverse_kernel,
        [
            ((TARGETS * BACK, NZ), f32),
            ((3, RPB, NZ), f32, "raw"),
            ((3, NJ, 8, NK), f32, "raw"),
            ((3, NJ, NK), f32, "raw"),
        ],
        flags,
        planes,
        joint,
        joined,
        own,
        other,
        gather,
        codes,
        szp,
        syh,
        syl,
        mu,
        field,
        speed,
        up,
        down,
        scratch=[
            pltpu.VMEM((3, RPB, NZ), f32),
            pltpu.VMEM((3, NJ, 8, NK), f32),
            pltpu.VMEM((3, NJ, NK), f32),
            pltpu.SemaphoreType.DMA((11,)),
        ],
    )
    returned = lax.all_to_all(
        send.reshape(TARGETS, BACK, 1, NZ), ("y", "x", "core"), 0, 0, tiled=True
    )
    sums = call(
        cell_kernel, [((3 * NJ, NZ), f32)] * CZ, flags, returned.reshape(TARGETS * BACK, NZ)
    )
    parts = []
    for k in (0, 1, 3, 2):
        pairs = [
            (place_of(1, y, z, x, c), place_of(0, y, (z + k) % CZ, x, c)) for y, z, x, c in chips()
        ]
        parts.append(lax.ppermute(sums[k], ALL, pairs))
    (result,) = call(
        close_kernel,
        [((3, NJ, NI, NZ), f32, "raw")],
        flags,
        result.reshape(3, NJ, NI, NZ),
        edge,
        layer,
        remesh,
        *parts,
        alias=True,
        scratch=[pltpu.VMEM((3, NJ, 8, NZ), f32), pltpu.SemaphoreType.DMA],
    )
    return result.reshape(1, 3, RPB * NZ)


def solution(mesh):
    fine = Mesh(mesh.devices.reshape(2, CY, CZ, CX, CC), ALL)
    placed = (
        P("grp", None, DEV),
        P(DEV),
        P(),
        P(DEV, None),
        P(DEV),
        P(DEV, None),
        P(DEV),
        P(DEV),
    )
    return jax.shard_map(
        on_device, mesh=fine, in_specs=placed, out_specs=P("grp", None, DEV), check_vma=False
    )
```
